32 devices in a mesh: tm: 4 (over y, x), res: 8 (over z, core).
Axes of the slice: x: 2, y: 2, z: 4, core: 2. Of those that a mesh axis runs over, the one named last changes fastest.
Arguments:
- node_feats: bfloat16 [4, 1024, 512], P('tm', 'res'), may hold values from -6 to 6
- edge_feats: bfloat16 [4, 1024, 60, 192], P('tm', 'res'), may hold values from -6 to 6
- node_cotan: bfloat16 [4, 1024, 512], P('tm', 'res'), may hold values from -6 to 6
- edge_cotan: bfloat16 [4, 1024, 60, 192], P('tm', 'res'), may hold values from -6 to 6
- neighbour: int32 [1024, 60], P('res'), may hold values from 0 to 383, as said below
- edge_mask: int32 [1024, 60], P('res'), may hold values from 0 to 1, as said below
- fetch_rows: int32 [8, 8, 32], P('res'), may hold values from 0 to 1023, as said below
- chain_ids: int32 [1024], P('res'), may hold values from 0 to 23, as said below
- complex_flag: int32 [1024], P('res'), may hold values from 0 to 1, as said below
- message_in: bfloat16 [1216, 512], replicated, may hold values from -0.15625 to 0.15625
- message_mid: bfloat16 [512, 512], replicated, may hold values from -0.25 to 0.25
- message_out: bfloat16 [512, 512], replicated, may hold values from -0.75 to 0.75
- gain_node: bfloat16 [512], replicated, may hold values from 0.5 to 1.5
- offset_node: bfloat16 [512], replicated, may hold values from -3 to 3
- expand_weight: bfloat16 [512, 2048], replicated, may hold values from -0.25 to 0.25
- contract_weight: bfloat16 [2048, 512], replicated, may hold values from -0.125 to 0.125
- gain_ffn: bfloat16 [512], replicated, may hold values from 0.5 to 1.5
- offset_ffn: bfloat16 [512], replicated, may hold values from -3 to 3
- update_in: bfloat16 [1216, 192], replicated, may hold values from -0.15625 to 0.15625
- update_mid: bfloat16 [192, 192], replicated, may hold values from -0.4375 to 0.4375
- update_out: bfloat16 [192, 192], replicated, may hold values from -0.4375 to 0.4375
- gain_edge: bfloat16 [192], replicated, may hold values from 0.5 to 1.5
- offset_edge: bfloat16 [192], replicated, may hold values from -3 to 3
Outputs:
- node_out: bfloat16 [4, 1024, 512], P('tm', 'res')
- edge_out: bfloat16 [4, 1024, 60, 192], P('tm', 'res')
- node_grad: float32 [4, 1024, 512], P('tm', 'res')
- edge_grad: float32 [4, 1024, 60, 192], P('tm', 'res')
- grad_message_in: float32 [1216, 512], replicated
- grad_message_mid: float32 [512, 512], replicated
- grad_message_out: float32 [512, 512], replicated
- grad_gain_node: float32 [512], replicated
- grad_offset_node: float32 [512], replicated
- grad_expand: float32 [512, 2048], replicated
- grad_contract: float32 [2048, 512], replicated
- grad_gain_ffn: float32 [512], replicated
- grad_offset_ffn: float32 [512], replicated
- grad_update_in: float32 [1216, 192], replicated
- grad_update_mid: float32 [192, 192], replicated
- grad_update_out: float32 [192, 192], replicated
- grad_gain_edge: float32 [192], replicated
- grad_offset_edge: float32 [192], replicated
The draws below stay inside these ranges and needn't reach their ends.
Inputs may be any that keep to these rules, and one draw needn't show every extreme that they name: `neighbour`: below 128 an entry names a residue of the own block; an entry s of 128 or more names the residue fetch_rows[block, (s - 128) // 32, (s - 128) % 32]. fetch_rows[d, p] holds 32 distinct residues of block p, that is of p * 128 to (p + 1) * 128 - 1. `chain_ids`: never falls along residues; no chain crosses from one block of 128 residues to the next. `complex_flag`: equal for all residues of a chain; the first chain of every block is in the complex. `edge_mask`: some residues are padding with no live edge.
All inputs are finite; a program needn't handle non-finite values.
Results may differ from the reference program's by a relative error of at most 0.02.
Values may be sent and summed in bfloat16 or wider, within the bound.
A program may use at most 256 MiB of HBM per device.

```python
import jax
import jax.numpy as jnp
from jax import lax

D = 512
E = 192
FF = 2048
K = 60
R_DEV = 128
CAP = 32
CONCAT = 1216
RESIDUES = 1024
N_TM = 4


def graph_draw(key):
    blocks = RESIDUES // R_DEV
    keys = jax.random.split(jax.random.fold_in(key, 7), 8)
    positions = jnp.arange(RESIDUES, dtype=jnp.int32)
    within = positions % R_DEV
    block_of = positions // R_DEV
    first_cut = jax.random.randint(keys[0], (blocks,), 1, R_DEV // 2)
    second_cut = jax.random.randint(keys[1], (blocks,), R_DEV // 2, R_DEV)
    chains = 3 * block_of + (within >= first_cut[block_of]).astype(jnp.int32) + (within >= second_cut[block_of]).astype(jnp.int32)
    chain_complex = (jax.random.randint(keys[2], (3 * blocks,), 0, 4) > 0).astype(jnp.int32)
    chain_complex = chain_complex.at[::3].set(1)
    complex_flag = chain_complex[chains]
    pair_keys = jax.random.split(keys[3], blocks * blocks)

    def choose_rows(sub_key):
        return jax.random.permutation(sub_key, R_DEV)[:CAP].astype(jnp.int32)
    orders = jax.vmap(choose_rows)(pair_keys).reshape(blocks, blocks, CAP)
    fetch = orders + (jnp.arange(blocks, dtype=jnp.int32) * R_DEV)[None, :, None]
    local_pick = jax.random.randint(keys[4], (RESIDUES, K), 0, R_DEV)
    remote_pick = R_DEV + jax.random.randint(keys[5], (RESIDUES, K), 0, blocks * CAP)
    which_side = jax.random.randint(keys[6], (RESIDUES, K), 0, 2)
    neighbour = jnp.where(which_side > 0, remote_pick, local_pick).astype(jnp.int32)
    padding = jax.random.randint(keys[7], (RESIDUES,), 0, 16) == 0
    live_edge = jax.random.randint(jax.random.fold_in(keys[7], 1), (RESIDUES, K), 0, 8) > 0
    edge_mask = jnp.logical_and(live_edge, jnp.logical_not(padding)[:, None]).astype(jnp.int32)
    return (neighbour, edge_mask, fetch.astype(jnp.int32), chains.astype(jnp.int32), complex_flag.astype(jnp.int32))


def draw_neighbour(key, part):
    return graph_draw(key)[0]


def draw_edge_mask(key, part):
    return graph_draw(key)[1]


def draw_fetch_rows(key, part):
    return graph_draw(key)[2]


def draw_chain_ids(key, part):
    return graph_draw(key)[3]


def draw_complex_flag(key, part):
    return graph_draw(key)[4]


def block_scale(rng, extent, cuts, least, largest):
    def one(axis_at, blocks):
        heights = jax.random.uniform(jax.random.fold_in(jax.random.fold_in(rng, 6), axis_at), (blocks,), jnp.float32, least / len(cuts), largest / len(cuts))
        return jnp.repeat(jnp.exp(heights), extent[axis_at] // blocks).reshape((-1,) + (1,) * (len(extent) - axis_at - 1))

    loudness = one(*cuts[0])
    for cut in cuts[1:]:
        loudness = loudness * one(*cut)
    return loudness


def normal_values(key, dims, width, bound, cuts=(), kind=jnp.bfloat16):
    loudness = block_scale(key, dims, cuts, -0.22, 0.18) if cuts else 1.0
    values = jax.random.normal(key, dims, jnp.float32) * width * loudness
    return jnp.minimum(jnp.maximum(values, -bound), bound).astype(kind)


def setup_inputs(seed: int = 0) -> dict:
    seeds = jax.random.split(jax.random.key(seed), 24)
    return {
        "node_feats": normal_values(seeds[0], (N_TM, RESIDUES, D), 1.0, 6.0, ((0, 4), (1, 8))),
        "edge_feats": normal_values(seeds[1], (N_TM, RESIDUES, K, E), 1.0, 6.0, ((0, 4), (1, 8))),
        "node_cotan": normal_values(seeds[2], (N_TM, RESIDUES, D), 1.0, 6.0, ((0, 4), (1, 8))),
        "edge_cotan": normal_values(seeds[3], (N_TM, RESIDUES, K, E), 1.0, 6.0, ((0, 4), (1, 8))),
        "neighbour": draw_neighbour(jax.random.fold_in(seeds[23], 71), 0),
        "edge_mask": draw_edge_mask(jax.random.fold_in(seeds[23], 71), 0),
        "fetch_rows": draw_fetch_rows(jax.random.fold_in(seeds[23], 71), 0),
        "chain_ids": draw_chain_ids(jax.random.fold_in(seeds[23], 71), 0),
        "complex_flag": draw_complex_flag(jax.random.fold_in(seeds[23], 71), 0),
        "message_in": normal_values(seeds[9], (CONCAT, D), CONCAT ** -0.5, 0.15625),
        "message_mid": normal_values(seeds[10], (D, D), D ** -0.5, 0.25),
        "message_out": normal_values(seeds[11], (D, D), (D // 8) ** -0.5, 0.75),
        "gain_node": jnp.clip(1.0 + 0.1 * jax.random.normal(seeds[12], (D,), jnp.float32), 0.5, 1.5).astype(jnp.bfloat16),
        "offset_node": normal_values(seeds[13], (D,), 0.5, 3.0),
        "expand_weight": normal_values(seeds[14], (D, FF), D ** -0.5, 0.25),
        "contract_weight": normal_values(seeds[15], (FF, D), FF ** -0.5, 0.125),
        "gain_ffn": jnp.clip(1.0 + 0.1 * jax.random.normal(seeds[16], (D,), jnp.float32), 0.5, 1.5).astype(jnp.bfloat16),
        "offset_ffn": normal_values(seeds[17], (D,), 0.5, 3.0),
        "update_in": normal_values(seeds[18], (CONCAT, E), CONCAT ** -0.5, 0.15625),
        "update_mid": normal_values(seeds[19], (E, E), E ** -0.5, 0.4375),
        "update_out": normal_values(seeds[20], (E, E), E ** -0.5, 0.4375),
        "gain_edge": jnp.clip(1.0 + 0.1 * jax.random.normal(seeds[21], (E,), jnp.float32), 0.5, 1.5).astype(jnp.bfloat16),
        "offset_edge": normal_values(seeds[22], (E,), 0.5, 3.0),
    }


@jax.custom_vjp
def low(v):
    return lax.optimization_barrier(v.astype(jnp.bfloat16)).astype(jnp.float32)

@jax.custom_vjp
def low_back(v):
    return v

def low_keep(v):
    return (low(v), None)

def low_pass(kept, grad):
    return (grad,)

def back_keep(v):
    return (v, None)

def back_low(kept, grad):
    return (low(grad),)
low.defvjp(low_keep, low_pass)
low_back.defvjp(back_keep, back_low)
EPSILON = 1e-05

def activate(values):
    return jax.nn.gelu(values, approximate=True)

def layer_norm(values, gain_vec, offset):
    centred = values - lax.optimization_barrier(jnp.mean(values, axis=-1, keepdims=True))
    spread = lax.optimization_barrier(jnp.mean(centred * centred, axis=-1, keepdims=True))
    return centred * lax.rsqrt(spread + EPSILON) * gain_vec + offset

def product(left_op, right_op):
    return jnp.dot(left_op, right_op, precision=lax.Precision.HIGHEST)

def edge_product(edges, weight):
    return jnp.einsum('bke,ef->bkf', edges, weight, precision=lax.Precision.HIGHEST)

def group_forward(params, node_in, edge_in, global_ids, keep):
    message_in, message_mid, message_out, gain_node, offset_node, expand_weight, contract_weight, gain_ffn, offset_ffn, update_in, update_mid, update_out, gain_edge, offset_edge = params
    feat_width = node_in.shape[1]
    block_count = node_in.shape[0] // R_DEV

    def by_block(array):
        return array.reshape((block_count, R_DEV) + array.shape[1:])
    counted = jnp.maximum(lax.optimization_barrier(jnp.sum(keep, axis=1)), 1.0)
    self_proj = low_back(product(node_in, message_in[:feat_width]))
    neigh_proj = low_back(product(node_in, message_in[feat_width:2 * feat_width]))

    def message_block(pieces):
        self_rows, edge_rows, id_rows, keep_rows = pieces
        pre_one = low_back(self_rows[:, None, :] + neigh_proj[id_rows] + edge_product(edge_rows, message_in[2 * feat_width:]))
        pre_two = low_back(edge_product(low(activate(pre_one)), message_mid))
        message = low_back(edge_product(low(activate(pre_two)), message_out))
        return lax.optimization_barrier(jnp.sum(message * keep_rows[:, :, None], axis=1))
    summed = lax.map(jax.checkpoint(message_block), (by_block(self_proj), by_block(edge_in), by_block(global_ids), by_block(keep)))
    aggregate = summed.reshape(node_in.shape) / counted[:, None]
    first = layer_norm(node_in + aggregate, gain_node, offset_node)
    inner = low_back(product(low(first), expand_weight))
    ffn_out = low_back(product(low(activate(inner)), contract_weight))
    updated = layer_norm(first + ffn_out, gain_ffn, offset_ffn)
    updated_low = low(updated)
    self_edge = low_back(product(updated_low, update_in[:feat_width]))
    neigh_edge = low_back(product(updated_low, update_in[feat_width:2 * feat_width]))

    def edge_block(pieces):
        self_rows, edge_rows, id_rows = pieces
        pre_three = low_back(self_rows[:, None, :] + neigh_edge[id_rows] + edge_product(edge_rows, update_in[2 * feat_width:]))
        pre_four = low_back(edge_product(low(activate(pre_three)), update_mid))
        branch = low_back(edge_product(low(activate(pre_four)), update_out))
        return layer_norm(edge_rows + branch, gain_edge, offset_edge)
    edge_new = lax.map(jax.checkpoint(edge_block), (by_block(self_edge), by_block(edge_in), by_block(global_ids)))
    return (updated, edge_new.reshape(edge_in.shape))

def reference(node_feats, edge_feats, node_cotan, edge_cotan, neighbour, edge_mask, fetch_rows, chain_ids, complex_flag, message_in, message_mid, message_out, gain_node, offset_node, expand_weight, contract_weight, gain_ffn, offset_ffn, update_in, update_mid, update_out, gain_edge, offset_edge):
    owner = (jnp.arange(RESIDUES, dtype=jnp.int32) // R_DEV)[:, None]
    slot_index = jnp.maximum(neighbour - R_DEV, 0)
    remote = fetch_rows[owner, slot_index // CAP, slot_index % CAP]
    global_ids = jnp.where(neighbour < R_DEV, owner * R_DEV + neighbour, remote).astype(jnp.int32)
    tag_all = chain_ids * 2 + complex_flag
    other_tag = tag_all[global_ids]
    joined = jnp.logical_or(chain_ids[:, None] == other_tag // 2, complex_flag[:, None] * (other_tag % 2) > 0)
    keep = edge_mask.astype(jnp.float32) * joined.astype(jnp.float32)
    params = tuple((weight.astype(jnp.float32) for weight in (message_in, message_mid, message_out, gain_node, offset_node, expand_weight, contract_weight, gain_ffn, offset_ffn, update_in, update_mid, update_out, gain_edge, offset_edge)))

    def one_group(totals, pieces):
        node_in = pieces[0].astype(jnp.float32)
        edge_in = pieces[1].astype(jnp.float32)
        node_back = pieces[2].astype(jnp.float32)
        edge_back = pieces[3].astype(jnp.float32)

        def forward(weights, nodes, edges):
            return group_forward(weights, nodes, edges, global_ids, keep)
        outputs, pullback = jax.vjp(forward, params, node_in, edge_in)
        grads = pullback((node_back, edge_back))
        totals = jax.tree.map(jnp.add, totals, grads[0])
        return (totals, (outputs[0].astype(jnp.bfloat16), outputs[1].astype(jnp.bfloat16), grads[1], grads[2]))
    zeros = jax.tree.map(jnp.zeros_like, params)
    totals, stacked = lax.scan(one_group, zeros, (node_feats, edge_feats, node_cotan, edge_cotan))
    return (stacked[0], stacked[1], stacked[2], stacked[3], totals[0], totals[1], totals[2], totals[3], totals[4], totals[5], totals[6], totals[7], totals[8], totals[9], totals[10], totals[11], totals[12], totals[13])
```

```python
import functools
import jax
import jax.numpy as jnp
from jax import lax
from jax.experimental import pallas as pl
from jax.experimental.pallas import tpu as pltpu
from jax.sharding import PartitionSpec as P

EPSILON = 1e-05
CURVE = 0.7978845608028654
CUBIC = 0.044715
F32 = jnp.float32
BF16 = jnp.bfloat16
VMEM_LIMIT = 60 * 1024 * 1024
MESH = pl.DeviceIdType.MESH


def nn(a, b):
    return lax.dot_general(a, b, (((1,), (0,)), ((), ())), preferred_element_type=F32)


def nt(a, b):
    return lax.dot_general(a, b, (((1,), (1,)), ((), ())), preferred_element_type=F32)


def tn(a, b):
    return lax.dot_general(a, b, (((0,), (0,)), ((), ())), preferred_element_type=F32)


def gelu_parts(v):
    square = v * v
    t = jnp.tanh(v * (CURVE + (CURVE * CUBIC) * square))
    half = 0.5 + 0.5 * t
    slope = half + (half - half * half) * (v * (2.0 * CURVE + (6.0 * CURVE * CUBIC) * square))
    return v * half, slope


def tile_lanes(block, count):
    return jnp.concatenate([block] * count, axis=1) if count > 1 else block


def edge_operand(table_len, slabs, base, e_ref, nbr_ref):
    columns = []
    for j in range(slabs):
        row = nbr_ref[pl.ds(base + j, 1), :]
        ids = lax.broadcasted_iota(jnp.int32, (table_len, row.shape[1]), 0)
        hot = jnp.where(ids == row, 1.0, 0.0).astype(BF16)
        columns.append(jnp.concatenate([hot, e_ref[j]], axis=0))
    return jnp.concatenate(columns, axis=1) if slabs > 1 else columns[0]


def message_forward_body(table_len, feat, slabs, e_ref, nbr_ref, mask_ref, own_ref, lhs_ref, self_ref, mid_ref,
                         h1_ref, gp1_ref, gp2_ref, s_ref, keep_ref, cnt_ref):
    step = pl.program_id(0)
    base = step * slabs
    rows = nbr_ref.shape[1]

    @pl.when(step == 0)
    def _():
        s_ref[...] = jnp.zeros_like(s_ref)
        cnt_ref[...] = jnp.zeros_like(cnt_ref)

    own = own_ref[...]
    own_chain = own // 2
    own_flag = own % 2
    total = s_ref[...]
    count = cnt_ref[...]
    for j in range(slabs):
        row = nbr_ref[pl.ds(base + j, 1), :]
        ids = lax.broadcasted_iota(jnp.int32, (table_len, rows), 0)
        hot = jnp.where(ids == row, 1.0, 0.0).astype(BF16)
        x = jnp.concatenate([hot, e_ref[j]], axis=0)
        pre = nn(lhs_ref[...], x)
        other = pre[feat : feat + 1, :].astype(jnp.int32)
        joined = jnp.logical_or(own_chain == other // 2, own_flag * (other % 2) > 0)
        keep = jnp.where(joined, 1.0, 0.0) * mask_ref[pl.ds(base + j, 1), :].astype(F32)
        keep_ref[j] = keep
        count = count + keep
        hidden, slope = gelu_parts(pre[:feat] + self_ref[...])
        hidden = hidden.astype(BF16)
        h1_ref[j] = hidden
        gp1_ref[j] = slope.astype(BF16)
        hidden, slope = gelu_parts(nn(mid_ref[...], hidden))
        gp2_ref[j] = slope.astype(BF16)
        total = total + hidden * keep
    s_ref[...] = total
    cnt_ref[...] = count


def message_forward(e, nbr, mask, own_tag, lhs, self_t, mid_t, slabs):
    fan, edge_w, rows = e.shape
    feat = self_t.shape[0]
    table_len = lhs.shape[1] - edge_w
    whole = lambda a: pl.BlockSpec(a.shape, lambda i: (0,) * a.ndim)
    slab = lambda f: pl.BlockSpec((slabs, f, rows), lambda i: (i, 0, 0))
    big = jax.ShapeDtypeStruct((fan, feat, rows), BF16)
    return pl.pallas_call(
        functools.partial(message_forward_body, table_len, feat, slabs),
        grid=(fan // slabs,),
        in_specs=[slab(edge_w), whole(nbr), whole(mask), whole(own_tag), whole(lhs), whole(self_t), whole(mid_t)],
        out_specs=[slab(feat), slab(feat), slab(feat), pl.BlockSpec((feat, rows), lambda i: (0, 0)), slab(1),
                   pl.BlockSpec((1, rows), lambda i: (0, 0))],
        out_shape=[big, big, big, jax.ShapeDtypeStruct((feat, rows), F32), jax.ShapeDtypeStruct((fan, 1, rows), F32),
                   jax.ShapeDtypeStruct((1, rows), F32)],
        compiler_params=pltpu.CompilerParams(vmem_limit_bytes=VMEM_LIMIT),
        name="message_forward",
    )(e, nbr, mask, own_tag, lhs, self_t, mid_t)


def edge_body(table_len, slabs, e_ref, cot_ref, nbr_ref, lhs_ref, self_ref, mid_t_ref, out_t_ref, mid_ref, out_ref, edge_ref,
              gain_ref, offset_ref,
              new_ref, part_ref, gout_ref, gmid_ref, gin_ref, dself_ref, ggain_ref, goff_ref):
    step = pl.program_id(0)
    base = step * slabs
    rows = nbr_ref.shape[1]

    @pl.when(step == 0)
    def _():
        for ref in (gout_ref, gmid_ref, gin_ref, dself_ref, ggain_ref, goff_ref):
            ref[...] = jnp.zeros_like(ref)

    x = edge_operand(table_len, slabs, base, e_ref, nbr_ref)
    self_t = tile_lanes(self_ref[...], slabs)
    hidden_three, slope_three = gelu_parts(nn(lhs_ref[...], x) + self_t)
    hidden_three = hidden_three.astype(BF16)
    hidden_four, slope_four = gelu_parts(nn(mid_t_ref[...], hidden_three))
    hidden_four = hidden_four.astype(BF16)
    branch = nn(out_t_ref[...], hidden_four)
    gain = gain_ref[...]
    offset = offset_ref[...]
    scale = 1.0 / e_ref.shape[1]
    resid = []
    ggain = ggain_ref[...]
    goff = goff_ref[...]
    for j in range(slabs):
        z = e_ref[j].astype(F32) + branch[:, j * rows : (j + 1) * rows]
        z = z - jnp.sum(z, axis=0, keepdims=True) * scale
        r = lax.rsqrt(jnp.sum(z * z, axis=0, keepdims=True) * scale + EPSILON)
        h = z * r
        new_ref[j] = (h * gain + offset).astype(BF16)
        dy = cot_ref[j].astype(F32)
        ggain = ggain + dy * h
        goff = goff + dy
        dh = dy * gain
        one = jnp.sum(dh, axis=0, keepdims=True) * scale
        two = jnp.sum(dh * h, axis=0, keepdims=True) * scale
        resid.append(r * (dh - one - h * two))
    ggain_ref[...] = ggain
    goff_ref[...] = goff
    resid = jnp.concatenate(resid, axis=1) if slabs > 1 else resid[0]
    delta = resid.astype(BF16)
    gout_ref[...] += nt(hidden_four, delta)
    delta_four = (nn(out_ref[...], delta) * slope_four).astype(BF16)
    gmid_ref[...] += nt(hidden_three, delta_four)
    delta_three = nn(mid_ref[...], delta_four) * slope_three
    low = delta_three.astype(BF16)
    gin_ref[...] += nt(x, low)
    part = resid + nn(edge_ref[...], low)
    dself = dself_ref[...]
    for j in range(slabs):
        cut = slice(j * rows, (j + 1) * rows)
        part_ref[j] = part[:, cut]
        dself = dself + low[:, cut].astype(F32)
    dself_ref[...] = dself


def edge_pass(e, cot, nbr, lhs, self_t, mid_t, out_t, mid, out, edge, gain, offset, slabs):
    fan, edge_w, rows = e.shape
    table_len = lhs.shape[1] - edge_w
    whole = lambda a: pl.BlockSpec(a.shape, lambda i: (0,) * a.ndim)
    slab = pl.BlockSpec((slabs, edge_w, rows), lambda i: (i, 0, 0))
    keep = lambda *s: (pl.BlockSpec(s, lambda i: (0,) * len(s)), jax.ShapeDtypeStruct(s, F32))
    sums = [keep(edge_w, edge_w), keep(edge_w, edge_w), keep(table_len + edge_w, edge_w), keep(edge_w, rows), keep(edge_w, rows),
            keep(edge_w, rows)]
    consts = (nbr, lhs, self_t, mid_t, out_t, mid, out, edge, gain, offset)
    return pl.pallas_call(
        functools.partial(edge_body, table_len, slabs),
        grid=(fan // slabs,),
        in_specs=[slab, slab] + [whole(a) for a in consts],
        out_specs=[slab, slab] + [s for s, _ in sums],
        out_shape=[jax.ShapeDtypeStruct(e.shape, BF16), jax.ShapeDtypeStruct(e.shape, F32)] + [s for _, s in sums],
        compiler_params=pltpu.CompilerParams(vmem_limit_bytes=VMEM_LIMIT),
        name="edge_pass",
    )(e, cot, *consts)


def message_backward_body(table_len, slabs, e_ref, h1_ref, gp1_ref, gp2_ref, part_ref, keep_ref, nbr_ref, d2_ref, mid_ref, edge_ref,
                          egrad_ref, gmid_ref, gin_ref, dself_ref):
    step = pl.program_id(0)
    base = step * slabs
    rows = nbr_ref.shape[1]

    @pl.when(step == 0)
    def _():
        for ref in (gmid_ref, gin_ref, dself_ref):
            ref[...] = jnp.zeros_like(ref)

    x = edge_operand(table_len, slabs, base, e_ref, nbr_ref)
    back = d2_ref[...]
    wide = lambda ref: jnp.concatenate([ref[j] for j in range(slabs)], axis=1)
    two = jnp.concatenate([(back * keep_ref[j] * gp2_ref[j].astype(F32)).astype(BF16) for j in range(slabs)], axis=1)
    gmid_ref[...] += nt(wide(h1_ref), two)
    one = (nn(mid_ref[...], two) * wide(gp1_ref).astype(F32)).astype(BF16)
    gin_ref[...] += nt(x, one)
    part = nn(edge_ref[...], one)
    dself = dself_ref[...]
    for j in range(slabs):
        cut = slice(j * rows, (j + 1) * rows)
        egrad_ref[j] = part_ref[j] + part[:, cut]
        dself = dself + one[:, cut].astype(F32)
    dself_ref[...] = dself


def message_backward(e, h1, gp1, gp2, part, keep, nbr, d2, mid, edge, table_len, slabs):
    fan, edge_w, rows = e.shape
    feat = d2.shape[0]
    whole = lambda a: pl.BlockSpec(a.shape, lambda i: (0,) * a.ndim)
    slab = lambda f: pl.BlockSpec((slabs, f, rows), lambda i: (i, 0, 0))
    fixed = lambda *s: (pl.BlockSpec(s, lambda i: (0,) * len(s)), jax.ShapeDtypeStruct(s, F32))
    sums = [fixed(feat, feat), fixed(table_len + edge_w, feat), fixed(feat, rows)]
    consts = (nbr, d2, mid, edge)
    return pl.pallas_call(
        functools.partial(message_backward_body, table_len, slabs),
        grid=(fan // slabs,),
        in_specs=[slab(edge_w), slab(feat), slab(feat), slab(feat), slab(edge_w), slab(1)] + [whole(a) for a in consts],
        out_specs=[slab(edge_w)] + [s for s, _ in sums],
        out_shape=[jax.ShapeDtypeStruct(e.shape, F32)] + [s for _, s in sums],
        compiler_params=pltpu.CompilerParams(vmem_limit_bytes=VMEM_LIMIT),
        name="message_backward",
    )(e, h1, gp1, gp2, part, keep, *consts)


def ring_place(n):
    me = lax.axis_index("res")
    return me, [lax.rem(me + s, n) for s in range(n)]


def greet(peers):
    barrier = pltpu.get_barrier_semaphore()
    for peer in peers[1:]:
        pl.semaphore_signal(barrier, inc=1, device_id={"res": peer}, device_id_type=MESH)
    pl.semaphore_wait(barrier, len(peers) - 1)


def copy_to(peer, source, target, send, recv):
    return pltpu.make_async_remote_copy(
        src_ref=source, dst_ref=target, send_sem=send, recv_sem=recv, device_id={"res": peer}, device_id_type=MESH
    )


def swap(n, me, peers, source, target, send, recv):
    sent = [copy_to(peers[s], source.at[s], target.at[me], send.at[s], recv.at[me]) for s in range(1, n)]
    back = [copy_to(peers[s], source.at[s], target.at[peers[s]], send.at[s], recv.at[peers[s]]) for s in range(1, n)]
    return sent, back


def row_norm(values):
    values = values - jnp.mean(values, axis=1, keepdims=True)
    r = lax.rsqrt(jnp.mean(values * values, axis=1, keepdims=True) + EPSILON)
    return values * r, r


def row_norm_back(dh, h, r):
    return r * (dh - jnp.mean(dh, axis=1, keepdims=True) - h * jnp.mean(dh * h, axis=1, keepdims=True))


def table_rows_body(n, fetch_ref, x_ref, chain_ref, flag_ref, win_ref, mid_ref, umid_ref, uout_ref, uin_ref,
                    lhs_ref, self_ref, midt_ref, umidt_ref, uoutt_ref, uedge_ref, sel_ref, tag_ref,
                    idx_out, idx_in, row_out, far, send_a, recv_a, send_b, recv_b):
    me, peers = ring_place(n)
    rows, feat = x_ref.shape
    cap = fetch_ref.shape[1]
    edge_w = win_ref.shape[0] - 2 * feat
    idx_out[...] = jnp.full(idx_out.shape, -1, jnp.int32)
    for s in range(n):
        idx_out[s, 0:1, 0:cap] = fetch_ref[pl.ds(peers[s], 1), :]
    greet(peers)
    sent, back = swap(n, me, peers, idx_out, idx_in, send_a, recv_a)
    for copy in sent:
        copy.start()
    tag = chain_ref[...] * 2 + flag_ref[...]
    tag_ref[...] = tag
    x = x_ref[...]
    wide_tag = jnp.transpose(jnp.broadcast_to(tag.astype(F32), (rows, rows)))
    rich = jnp.concatenate([x, wide_tag.astype(BF16)], axis=1)
    self_ref[...] = jnp.transpose(nn(x, win_ref[:feat, :]))

    def choose(row):
        ids = lax.broadcasted_iota(jnp.int32, (rows, row.shape[1]), 0) + me * rows
        hot = jnp.transpose(jnp.where(ids == row, 1.0, 0.0))[:cap].astype(BF16)
        return hot, nn(hot, rich).astype(BF16)

    hot, block = choose(idx_out[0, 0:1, :])
    sel_ref[me] = hot
    far[me] = block
    copies, backs = swap(n, me, peers, row_out, far, send_b, recv_b)
    for s in range(1, n):
        back[s - 1].wait_recv()
        hot, block = choose(idx_in[peers[s], 0:1, :])
        sel_ref[peers[s]] = hot
        row_out[s] = block
        copies[s - 1].start()
    midt_ref[...] = jnp.transpose(mid_ref[...])
    umidt_ref[...] = jnp.transpose(umid_ref[...])
    uoutt_ref[...] = jnp.transpose(uout_ref[...])
    uedge_ref[...] = jnp.transpose(uin_ref[:, 2 * feat :])
    neigh = win_ref[feat : 2 * feat, :]
    extra = lhs_ref.shape[0] - feat
    table_len = rows + n * cap
    lhs_ref[feat:, table_len:] = jnp.zeros((extra, edge_w), BF16)
    lhs_ref[:feat, table_len:] = jnp.transpose(win_ref[2 * feat :, :])
    lhs_ref[:feat, :rows] = jnp.transpose(nn(x, neigh)).astype(BF16)
    lhs_ref[feat:, :rows] = jnp.broadcast_to(tag.astype(F32), (extra, rows)).astype(BF16)
    for copy in backs:
        copy.wait_recv()
    got = far[...].reshape(n * cap, far.shape[2])
    lhs_ref[:feat, rows:table_len] = jnp.transpose(nn(got[:, :feat], neigh)).astype(BF16)
    lhs_ref[feat:, rows:table_len] = jnp.transpose(got[:, feat:].astype(F32))[:extra].astype(BF16)
    for copy in sent + copies:
        copy.wait_send()


def vmem_call(body, args, outs, scratch, collective, name):
    whole = pl.BlockSpec(memory_space=pltpu.VMEM)
    return pl.pallas_call(
        body,
        out_shape=[jax.ShapeDtypeStruct(s, d) for s, d in outs],
        in_specs=[whole] * len(args),
        out_specs=[whole] * len(outs),
        scratch_shapes=scratch,
        compiler_params=pltpu.CompilerParams(vmem_limit_bytes=VMEM_LIMIT, collective_id=collective, has_side_effects=True),
        name=name,
    )(*args)


def table_rows(n, fetch, x, chain, flag, win, mid, umid, uout, uin):
    rows, feat = x.shape
    cap = fetch.shape[1]
    edge_w = win.shape[0] - 2 * feat
    table_len = rows + n * cap
    outs = [((feat + 16, table_len + edge_w), BF16), ((feat, rows), F32), (mid.shape, BF16), (umid.shape, BF16), (uout.shape, BF16),
            ((edge_w, edge_w), BF16), ((n, cap, rows), BF16), ((1, rows), jnp.int32)]
    sems = [pltpu.SemaphoreType.DMA((n,))] * 4
    scratch = [pltpu.VMEM((n, 8, 128), jnp.int32)] * 2 + [pltpu.VMEM((n, cap, feat + rows), BF16)] * 2 + sems
    return vmem_call(functools.partial(table_rows_body, n), (fetch, x, chain, flag, win, mid, umid, uout, uin), outs, scratch, 0,
                     "table_rows")


def node_forward_body(n, s_ref, cnt_ref, x_ref, mout_ref, gain_ref, off_ref, exp_ref, con_ref, gain2_ref, off2_ref, sel_ref, uin_ref,
                      node_ref, lhs_ref, self_ref, h1_ref, r1_ref, h2_ref, r2_ref, acted_ref, slope_ref,
                      row_out, far, send_a, recv_a):
    me, peers = ring_place(n)
    rows, feat = x_ref.shape
    cap = sel_ref.shape[1]
    edge_w = uin_ref.shape[0]
    mean = jnp.transpose(s_ref[...] / jnp.maximum(cnt_ref[...], 1.0))
    upper = mean.astype(BF16)
    lower = (mean - upper.astype(F32)).astype(BF16)
    aggregate = nn(upper, mout_ref[...]) + nn(lower, mout_ref[...])
    h, r = row_norm(x_ref[...].astype(F32) + aggregate)
    h1_ref[...] = h
    r1_ref[...] = r
    first = h * gain_ref[...].astype(F32) + off_ref[...].astype(F32)
    hidden, slope = gelu_parts(nn(first.astype(BF16), exp_ref[...]))
    acted = hidden.astype(BF16)
    acted_ref[...] = acted
    slope_ref[...] = slope
    h, r = row_norm(first + nn(acted, con_ref[...]))
    h2_ref[...] = h
    r2_ref[...] = r
    low = (h * gain2_ref[...].astype(F32) + off2_ref[...].astype(F32)).astype(BF16)
    node_ref[...] = low
    neigh = nt(low, uin_ref[:, feat : 2 * feat])
    packed = neigh.astype(BF16)
    greet(peers)
    copies, backs = swap(n, me, peers, row_out, far, send_a, recv_a)
    for s in range(1, n):
        row_out[s] = nn(sel_ref[peers[s]], packed).astype(BF16)
        copies[s - 1].start()
    far[me] = nn(sel_ref[me], packed).astype(BF16)
    self_ref[...] = nt(uin_ref[:, :feat], low)
    table_len = rows + n * cap
    lhs_ref[:, :rows] = jnp.transpose(neigh).astype(BF16)
    lhs_ref[:, table_len:] = uin_ref[:, 2 * feat :]
    for copy in backs:
        copy.wait_recv()
    lhs_ref[:, rows:table_len] = jnp.transpose(far[...].reshape(n * cap, edge_w))
    for copy in copies:
        copy.wait_send()


def node_forward(n, s, cnt, x, mout, gain, off, expand, contract, gain2, off2, sel, uin):
    rows, feat = x.shape
    cap = sel.shape[1]
    edge_w = uin.shape[0]
    table_len = rows + n * cap
    hidden = expand.shape[1]
    outs = [(x.shape, BF16), ((edge_w, table_len + edge_w), BF16), ((edge_w, rows), F32), (x.shape, F32), ((rows, 1), F32),
            (x.shape, F32), ((rows, 1), F32), ((rows, hidden), BF16), ((rows, hidden), F32)]
    scratch = [pltpu.VMEM((n, cap, edge_w), BF16)] * 2 + [pltpu.SemaphoreType.DMA((n,))] * 2
    return vmem_call(functools.partial(node_forward_body, n),
                     (s, cnt, x, mout, gain, off, expand, contract, gain2, off2, sel, uin), outs, scratch, 1, "node_forward")


def gather_back(n, me, peers, gin_ref, sel_ref, row_out, far, send, recv, rows):
    cap = sel_ref.shape[1]
    width = gin_ref.shape[1]
    greet(peers)
    copies, backs = swap(n, me, peers, row_out, far, send, recv)
    for s in range(1, n):
        start = pl.multiple_of(rows + peers[s] * cap, cap)
        row_out[s] = gin_ref[pl.ds(start, cap), :].astype(BF16)
        copies[s - 1].start()
    far[me] = gin_ref[pl.ds(pl.multiple_of(rows + me * cap, cap), cap), :].astype(BF16)
    for copy in backs:
        copy.wait_recv()
    picked = tn(sel_ref[...].reshape(n * cap, rows), far[...].reshape(n * cap, width))
    total = gin_ref[:rows, :] + picked
    for copy in copies:
        copy.wait_send()
    return total.astype(BF16)


def node_backward_body(n, gin_ref, dself_ref, sel_ref, node_ref, cot_ref, uin_ref, h1_ref, r1_ref, h2_ref, r2_ref, acted_ref, slope_ref,
                       gain_ref, off_ref, gain2_ref, exp_ref, con_ref, s_ref, cnt_ref, mout_ref, ggain_ref, goff_ref,
                       dfirst_ref, d2_ref, guin_ref, gmout_ref, gexp_ref, gcon_ref, gv_ref, ge_ref,
                       row_out, far, send_a, recv_a):
    me, peers = ring_place(n)
    rows, feat = node_ref.shape
    edge_w = uin_ref.shape[0]
    own = gather_back(n, me, peers, gin_ref, sel_ref, row_out, far, send_a, recv_a, rows)
    table_len = gin_ref.shape[0] - edge_w
    dself_t = dself_ref[...].astype(BF16)
    dself = jnp.transpose(dself_ref[...]).astype(BF16)
    node = node_ref[...]
    guin_ref[:, :feat] = nn(dself_t, node)
    guin_ref[:, feat : 2 * feat] = tn(own, node)
    guin_ref[:, 2 * feat :] = jnp.transpose(gin_ref[table_len:, :])
    dy = cot_ref[...].astype(F32) + nn(dself, uin_ref[:, :feat]) + nn(own, uin_ref[:, feat : 2 * feat])
    h2 = h2_ref[...]
    gv_ref[2:3, :] = jnp.sum(dy * h2, axis=0, keepdims=True)
    gv_ref[3:4, :] = jnp.sum(dy, axis=0, keepdims=True)
    second = row_norm_back(dy * gain2_ref[...].astype(F32), h2, r2_ref[...])
    dffn = second.astype(BF16)
    gcon_ref[...] = tn(acted_ref[...], dffn)
    dinner = (nt(dffn, con_ref[...]) * slope_ref[...]).astype(BF16)
    h1 = h1_ref[...]
    gain = gain_ref[...].astype(F32)
    first_low = (h1 * gain + off_ref[...].astype(F32)).astype(BF16)
    gexp_ref[...] = tn(first_low, dinner)
    dy = second + nt(dinner, exp_ref[...])
    gv_ref[0:1, :] = jnp.sum(dy * h1, axis=0, keepdims=True)
    gv_ref[1:2, :] = jnp.sum(dy, axis=0, keepdims=True)
    dfirst = row_norm_back(dy * gain, h1, r1_ref[...])
    dfirst_ref[...] = dfirst
    back = (jnp.transpose(dfirst) / jnp.maximum(cnt_ref[...], 1.0)).astype(BF16)
    d2_ref[...] = nn(mout_ref[...], back)
    gmout_ref[...] = nt(s_ref[...].astype(BF16), back)
    ge_ref[0:1, :] = jnp.sum(jnp.transpose(ggain_ref[...]), axis=0, keepdims=True)
    ge_ref[1:2, :] = jnp.sum(jnp.transpose(goff_ref[...]), axis=0, keepdims=True)


def node_backward(n, gin, dself, sel, node, cot, uin, h1, r1, h2, r2, acted, slope, gain, off, gain2, expand, contract, s, cnt, mout,
                  ggain, goff):
    rows, feat = node.shape
    cap = sel.shape[1]
    edge_w = uin.shape[0]
    outs = [(node.shape, F32), ((feat, rows), F32), (uin.shape, F32), (mout.shape, F32), (expand.shape, F32), (contract.shape, F32),
            ((4, feat), F32), ((2, edge_w), F32)]
    scratch = [pltpu.VMEM((n, cap, edge_w), BF16)] * 2 + [pltpu.SemaphoreType.DMA((n,))] * 2
    return vmem_call(functools.partial(node_backward_body, n),
                     (gin, dself, sel, node, cot, uin, h1, r1, h2, r2, acted, slope, gain, off, gain2, expand, contract, s, cnt, mout,
                      ggain, goff), outs, scratch, 2, "node_backward")


def node_finish_body(n, gin_ref, dself_ref, sel_ref, x_ref, dfirst_ref, win_ref, grad_ref, gwin_ref, row_out, far, send_a, recv_a):
    me, peers = ring_place(n)
    rows, feat = x_ref.shape
    own = gather_back(n, me, peers, gin_ref, sel_ref, row_out, far, send_a, recv_a, rows)
    table_len = gin_ref.shape[0] - (win_ref.shape[0] - 2 * feat)
    dself = jnp.transpose(dself_ref[...]).astype(BF16)
    x = x_ref[...]
    grad_ref[...] = dfirst_ref[...] + nt(dself, win_ref[:feat, :]) + nt(own, win_ref[feat : 2 * feat, :])
    gwin_ref[:feat, :] = tn(x, dself)
    gwin_ref[feat : 2 * feat, :] = tn(x, own)
    gwin_ref[2 * feat :, :] = gin_ref[table_len:, :]


def node_finish(n, gin, dself, sel, x, dfirst, win):
    cap = sel.shape[1]
    outs = [(x.shape, F32), (win.shape, F32)]
    scratch = [pltpu.VMEM((n, cap, x.shape[1]), BF16)] * 2 + [pltpu.SemaphoreType.DMA((n,))] * 2
    return vmem_call(functools.partial(node_finish_body, n), (gin, dself, sel, x, dfirst, win), outs, scratch, 3, "node_finish")


def local(n, node_feats, edge_feats, node_cotan, edge_cotan, neighbour, edge_mask, fetch_rows, chain_ids, complex_flag, message_in,
          message_mid, message_out, gain_node, offset_node, expand_weight, contract_weight, gain_ffn, offset_ffn, update_in, update_mid,
          update_out, gain_edge, offset_edge):
    x = node_feats[0]
    rows, feat = x.shape
    fan = neighbour.shape[1]
    edge_w = edge_feats.shape[3]
    e = jnp.transpose(edge_feats[0], (1, 2, 0))
    cot = jnp.transpose(edge_cotan[0], (1, 2, 0))
    nbr = jnp.transpose(neighbour)
    mask = jnp.transpose(edge_mask)
    uin = jnp.transpose(update_in)
    line = lambda v: v.reshape(1, -1)
    lhs, self_t, mid_t, umid_t, uout_t, uedge, sel, tag = table_rows(
        n, fetch_rows[0], x, line(chain_ids), line(complex_flag), message_in, message_mid, update_mid, update_out, uin
    )
    table_len = lhs.shape[1] - edge_w
    slabs = next(c for c in (10, 6, 4, 2, 1) if fan % c == 0)
    h1, gp1, gp2, s, keep, cnt = message_forward(e, nbr, mask, tag, lhs, self_t, mid_t, slabs)
    node, lhs3, self3, n1, r1, n2, r2, acted, slope = node_forward(
        n, s, cnt, x, message_out, line(gain_node), line(offset_node), expand_weight, contract_weight, line(gain_ffn), line(offset_ffn),
        sel, uin
    )
    column = lambda v: v.astype(F32).reshape(-1, 1)
    edge_new, part, guout, gumid, gin3, dself3, ggain, goff = edge_pass(
        e, cot, nbr, lhs3, self3, umid_t, uout_t, update_mid, update_out, uedge, column(gain_edge), column(offset_edge), slabs
    )
    dfirst, d2, guin, gmout, gexp, gcon, gv, ge = node_backward(
        n, gin3, dself3, sel, node, node_cotan[0], uin, n1, r1, n2, r2, acted, slope, line(gain_node), line(offset_node), line(gain_ffn),
        expand_weight, contract_weight, s, cnt, message_out, ggain, goff
    )
    egrad, gmid, gin1, dself1 = message_backward(
        e, h1, gp1, gp2, part, keep, nbr, d2, message_mid, message_in[2 * feat :], table_len, slabs
    )
    ngrad, gwin = node_finish(n, gin1, dself1, sel, x, dfirst, message_in)
    gwin, gmid, gmout, gv, gexp, gcon, guin, gumid, guout, ge = lax.psum(
        (gwin, gmid, gmout, gv, gexp, gcon, guin, gumid, guout, ge), ("tm", "res")
    )
    native = lambda a: jnp.transpose(a, (2, 0, 1))[None]
    return (node[None], native(edge_new), ngrad[None], native(egrad), gwin, gmid, gmout, gv[0], gv[1], gexp, gcon, gv[2], gv[3],
            jnp.transpose(guin), gumid, guout, ge[0], ge[1])


def solution(mesh):
    grouped, placed, copied = P("tm", "res", None), P("res", None), P()
    wide = P("tm", "res", None, None)
    arguments = (grouped, wide, grouped, wide, placed, placed, P("res", None, None), P("res"), P("res")) + (copied,) * 14
    return jax.shard_map(
        functools.partial(local, mesh.shape["res"]),
        mesh=mesh,
        in_specs=arguments,
        out_specs=(grouped, wide, grouped, wide) + (copied,) * 14,
        check_vma=False,
    )
```

```python
import functools
import jax
import jax.numpy as jnp
from jax import lax
from jax.experimental import pallas as pl
from jax.experimental.pallas import tpu as pltpu
from jax.sharding import PartitionSpec as P

EPSILON = 1e-05
CURVE = 0.7978845608028654
CUBIC = 0.044715
F32 = jnp.float32
BF16 = jnp.bfloat16
VMEM_LIMIT = 60 * 1024 * 1024
MESH = pl.DeviceIdType.MESH


def nn(a, b):
    return lax.dot_general(a, b, (((1,), (0,)), ((), ())), preferred_element_type=F32)


def nt(a, b):
    return lax.dot_general(a, b, (((1,), (1,)), ((), ())), preferred_element_type=F32)


def tn(a, b):
    return lax.dot_general(a, b, (((0,), (0,)), ((), ())), preferred_element_type=F32)


def gelu_parts(v):
    square = v * v
    t = jnp.tanh(v * (CURVE + (CURVE * CUBIC) * square))
    half = 0.5 + 0.5 * t
    slope = half + (half - half * half) * (v * (2.0 * CURVE + (6.0 * CURVE * CUBIC) * square))
    return v * half, slope


def tile_lanes(block, count):
    return jnp.concatenate([block] * count, axis=1) if count > 1 else block


def edge_operand(table_len, slabs, base, e_ref, nbr_ref):
    columns = []
    for j in range(slabs):
        row = nbr_ref[pl.ds(base + j, 1), :]
        ids = lax.broadcasted_iota(jnp.int32, (table_len, row.shape[1]), 0)
        hot = jnp.where(ids == row, 1.0, 0.0).astype(BF16)
        columns.append(jnp.concatenate([hot, e_ref[j]], axis=0))
    return jnp.concatenate(columns, axis=1) if slabs > 1 else columns[0]


def message_forward_body(table_len, feat, slabs, e_ref, nbr_ref, mask_ref, own_ref, lhs_ref, self_ref, mid_ref,
                         h1_ref, gp1_ref, gp2_ref, s_ref, keep_ref, cnt_ref):
    step = pl.program_id(0)
    base = step * slabs
    rows = nbr_ref.shape[1]

    @pl.when(step == 0)
    def _():
        s_ref[...] = jnp.zeros_like(s_ref)
        cnt_ref[...] = jnp.zeros_like(cnt_ref)

    own = own_ref[...]
    own_chain = own // 2
    own_flag = own % 2
    pre = nn(lhs_ref[...], edge_operand(table_len, slabs, base, e_ref, nbr_ref))
    hidden, slope = gelu_parts(pre[:feat] + tile_lanes(self_ref[...], slabs))
    hidden = hidden.astype(BF16)
    slope = slope.astype(BF16)
    total = s_ref[...]
    count = cnt_ref[...]
    keeps = []
    for j in range(slabs):
        cut = slice(j * rows, (j + 1) * rows)
        h1_ref[j] = hidden[:, cut]
        gp1_ref[j] = slope[:, cut]
        other = pre[feat : feat + 1, cut].astype(jnp.int32)
        joined = jnp.logical_or(own_chain == other // 2, own_flag * (other % 2) > 0)
        keep = jnp.where(joined, 1.0, 0.0) * mask_ref[pl.ds(base + j, 1), :].astype(F32)
        keep_ref[j] = keep
        keeps.append(keep)
        count = count + keep
    hidden, slope = gelu_parts(nn(mid_ref[...], hidden))
    slope = slope.astype(BF16)
    for j in range(slabs):
        cut = slice(j * rows, (j + 1) * rows)
        gp2_ref[j] = slope[:, cut]
        total = total + hidden[:, cut] * keeps[j]
    s_ref[...] = total
    cnt_ref[...] = count


def message_forward(e, nbr, mask, own_tag, lhs, self_t, mid_t, slabs):
    fan, edge_w, rows = e.shape
    feat = self_t.shape[0]
    table_len = lhs.shape[1] - edge_w
    whole = lambda a: pl.BlockSpec(a.shape, lambda i: (0,) * a.ndim)
    slab = lambda f: pl.BlockSpec((slabs, f, rows), lambda i: (i, 0, 0))
    big = jax.ShapeDtypeStruct((fan, feat, rows), BF16)
    return pl.pallas_call(
        functools.partial(message_forward_body, table_len, feat, slabs),
        grid=(fan // slabs,),
        in_specs=[slab(edge_w), whole(nbr), whole(mask), whole(own_tag), whole(lhs), whole(self_t), whole(mid_t)],
        out_specs=[slab(feat), slab(feat), slab(feat), pl.BlockSpec((feat, rows), lambda i: (0, 0)), slab(1),
                   pl.BlockSpec((1, rows), lambda i: (0, 0))],
        out_shape=[big, big, big, jax.ShapeDtypeStruct((feat, rows), F32), jax.ShapeDtypeStruct((fan, 1, rows), F32),
                   jax.ShapeDtypeStruct((1, rows), F32)],
        compiler_params=pltpu.CompilerParams(vmem_limit_bytes=VMEM_LIMIT),
        name="message_forward",
    )(e, nbr, mask, own_tag, lhs, self_t, mid_t)


def edge_body(table_len, slabs, e_ref, cot_ref, nbr_ref, lhs_ref, self_ref, mid_t_ref, out_t_ref, mid_ref, out_ref, edge_ref,
              gain_ref, offset_ref,
              new_ref, part_ref, gout_ref, gmid_ref, gin_ref, dself_ref, ggain_ref, goff_ref):
    step = pl.program_id(0)
    base = step * slabs
    rows = nbr_ref.shape[1]

    @pl.when(step == 0)
    def _():
        for ref in (gout_ref, gmid_ref, gin_ref, dself_ref, ggain_ref, goff_ref):
            ref[...] = jnp.zeros_like(ref)

    x = edge_operand(table_len, slabs, base, e_ref, nbr_ref)
    self_t = tile_lanes(self_ref[...], slabs)
    hidden_three, slope_three = gelu_parts(nn(lhs_ref[...], x) + self_t)
    hidden_three = hidden_three.astype(BF16)
    hidden_four, slope_four = gelu_parts(nn(mid_t_ref[...], hidden_three))
    hidden_four = hidden_four.astype(BF16)
    branch = nn(out_t_ref[...], hidden_four)
    gain = gain_ref[...]
    offset = offset_ref[...]
    scale = 1.0 / e_ref.shape[1]
    resid = []
    ggain = ggain_ref[...]
    goff = goff_ref[...]
    for j in range(slabs):
        z = e_ref[j].astype(F32) + branch[:, j * rows : (j + 1) * rows]
        z = z - jnp.sum(z, axis=0, keepdims=True) * scale
        r = lax.rsqrt(jnp.sum(z * z, axis=0, keepdims=True) * scale + EPSILON)
        h = z * r
        new_ref[j] = (h * gain + offset).astype(BF16)
        dy = cot_ref[j].astype(F32)
        ggain = ggain + dy * h
        goff = goff + dy
        dh = dy * gain
        one = jnp.sum(dh, axis=0, keepdims=True) * scale
        two = jnp.sum(dh * h, axis=0, keepdims=True) * scale
        resid.append(r * (dh - one - h * two))
    ggain_ref[...] = ggain
    goff_ref[...] = goff
    resid = jnp.concatenate(resid, axis=1) if slabs > 1 else resid[0]
    delta = resid.astype(BF16)
    gout_ref[...] += nt(hidden_four, delta)
    delta_four = (nn(out_ref[...], delta) * slope_four).astype(BF16)
    gmid_ref[...] += nt(hidden_three, delta_four)
    delta_three = nn(mid_ref[...], delta_four) * slope_three
    low = delta_three.astype(BF16)
    gin_ref[...] += nt(x, low)
    part = resid + nn(edge_ref[...], low)
    dself = dself_ref[...]
    for j in range(slabs):
        cut = slice(j * rows, (j + 1) * rows)
        part_ref[j] = part[:, cut]
        dself = dself + low[:, cut].astype(F32)
    dself_ref[...] = dself


def edge_pass(e, cot, nbr, lhs, self_t, mid_t, out_t, mid, out, edge, gain, offset, slabs):
    fan, edge_w, rows = e.shape
    table_len = lhs.shape[1] - edge_w
    whole = lambda a: pl.BlockSpec(a.shape, lambda i: (0,) * a.ndim)
    slab = pl.BlockSpec((slabs, edge_w, rows), lambda i: (i, 0, 0))
    keep = lambda *s: (pl.BlockSpec(s, lambda i: (0,) * len(s)), jax.ShapeDtypeStruct(s, F32))
    sums = [keep(edge_w, edge_w), keep(edge_w, edge_w), keep(table_len + edge_w, edge_w), keep(edge_w, rows), keep(edge_w, rows),
            keep(edge_w, rows)]
    consts = (nbr, lhs, self_t, mid_t, out_t, mid, out, edge, gain, offset)
    return pl.pallas_call(
        functools.partial(edge_body, table_len, slabs),
        grid=(fan // slabs,),
        in_specs=[slab, slab] + [whole(a) for a in consts],
        out_specs=[slab, slab] + [s for s, _ in sums],
        out_shape=[jax.ShapeDtypeStruct(e.shape, BF16), jax.ShapeDtypeStruct(e.shape, F32)] + [s for _, s in sums],
        compiler_params=pltpu.CompilerParams(vmem_limit_bytes=VMEM_LIMIT),
        name="edge_pass",
    )(e, cot, *consts)


LANES = 512


def spot():
    group, place = lax.axis_index("tm"), lax.axis_index("res")
    return group, place, lax.rem(place, 2), place // 2, lax.rem(group, 2), group // 2


def grain(places):
    return 16 * max(1, places // 4)


def piece(places, depth, index):
    across = min(places, 4)
    rows, wide = piece_shape(places, depth)
    top = pl.multiple_of((index // across) * rows, rows)
    left = pl.multiple_of(lax.rem(index, across) * wide, wide)
    return pl.ds(top, rows), pl.ds(left, wide)


def piece_shape(places, depth):
    across = min(places, 4)
    return depth // (places // across), LANES // across


def remote(source, target, send, recv, group, place):
    return pltpu.make_async_remote_copy(
        src_ref=source, dst_ref=target, send_sem=send, recv_sem=recv, device_id={"tm": group, "res": place}, device_id_type=MESH
    )


class Chunk:
    def __init__(self, places, source, result, acc, from_core, from_first, from_second, from_line, stage, out, sends, recvs, local):
        self.places, self.source, self.result, self.acc = places, source, result, acc
        self.from_core, self.from_first, self.from_second = from_core, from_first, from_second
        self.from_line, self.stage, self.out = from_line, stage, out
        self.sends, self.recvs, self.local = sends, recvs, local
        self.depth = acc.shape[1]
        self.at = 0

    def advance(self):
        parts = (self.spread, self.halve, self.quarter, self.scatter, self.settle, self.gather, self.widen, self.share, self.store,
                 self.close)
        if self.at < len(parts):
            parts[self.at]()
            self.at += 1
        return self.at < len(parts)

    def link(self, slot, source, target, group, place):
        return functools.partial(remote, source, target, self.sends.at[slot], self.recvs.at[slot], group, place)

    def core_copy(self):
        group, place, core, lane, x, y = spot()
        theirs = pl.multiple_of((1 - core) * 8, 8)
        return self.link(0, self.source.at[pl.ds(theirs, 8)], self.from_core, group, place + 1 - 2 * core)

    def load_copy(self):
        core = spot()[2]
        return pltpu.make_async_copy(self.source.at[pl.ds(pl.multiple_of(core * 8, 8), 8)], self.acc, self.local.at[0])

    def half_copies(self):
        group, place, core, lane, x, y = spot()
        return [
            self.link(1, self.acc.at[pl.ds((1 - x) * 2, 2)], self.from_first.at[pl.ds(0, 2)], group + 1 - 2 * x, place),
            self.link(2, self.acc.at[pl.ds(4 + (1 - y) * 2, 2)], self.from_first.at[pl.ds(2, 2)], group + 2 - 4 * y, place),
        ]

    def quarter_copies(self):
        group, place, core, lane, x, y = spot()
        return [
            self.link(3, self.acc.at[x * 2 + 1 - y], self.from_second.at[0], group + 2 - 4 * y, place),
            self.link(4, self.acc.at[4 + y * 2 + 1 - x], self.from_second.at[1], group + 1 - 2 * x, place),
        ]

    def line_copies(self):
        group, place, core, lane, x, y = spot()
        copies = []
        for s in range(1, self.places):
            ahead, behind = lax.rem(lane + s, self.places), lax.rem(lane + self.places - s, self.places)
            rows, wide = piece(self.places, self.depth, ahead)
            view = self.stage.at[:, rows, wide]
            copies.append((self.link(4 + s, view, self.from_line.at[lane], group, ahead * 2 + core),
                           self.link(4 + s, view, self.from_line.at[behind], group, behind * 2 + core)))
        return copies

    def own(self):
        group, place, core, lane, x, y = spot()
        return core * 8 + x * 2 + y, core * 8 + 4 + y * 2 + x

    def spread_copies(self):
        group, place, core, lane, x, y = spot()
        copies = []
        slot = 4 + self.places
        for own in self.own():
            for s in range(1, self.places):
                ahead, behind = lax.rem(lane + s, self.places), lax.rem(lane + self.places - s, self.places)
                rows, wide = piece(self.places, self.depth, lane)
                back_rows, back_wide = piece(self.places, self.depth, behind)
                view, back = self.out.at[own, rows, wide], self.out.at[own, back_rows, back_wide]
                copies.append((self.link(slot, view, view, group, ahead * 2 + core), self.link(slot, back, back, group, behind * 2 + core)))
                slot += 1
        return copies

    def both(self, slot, view, back, group, place):
        return self.link(slot, view, view, group, place), self.link(slot, back, back, group, place)

    def gather_copies(self):
        group, place, core, lane, x, y = spot()
        slot = 2 + 3 * self.places
        first, second = self.own()
        return [
            self.both(slot, self.out.at[first], self.out.at[core * 8 + x * 2 + 1 - y], group + 2 - 4 * y, place),
            self.both(slot + 1, self.out.at[second], self.out.at[core * 8 + 4 + y * 2 + 1 - x], group + 1 - 2 * x, place),
        ]

    def widen_copies(self):
        group, place, core, lane, x, y = spot()
        slot = 4 + 3 * self.places
        two = lambda start: self.out.at[pl.ds(start, 2)]
        return [
            self.both(slot, two(core * 8 + x * 2), two(core * 8 + 2 - x * 2), group + 1 - 2 * x, place),
            self.both(slot + 1, two(core * 8 + 4 + y * 2), two(core * 8 + 6 - y * 2), group + 2 - 4 * y, place),
        ]

    def share_copy(self):
        group, place, core, lane, x, y = spot()
        eight = lambda which: self.out.at[pl.ds(pl.multiple_of(which * 8, 8), 8)]
        return self.both(6 + 3 * self.places, eight(core), eight(1 - core), group, place + 1 - 2 * core)

    def store_copy(self, which, slot):
        eight = pl.ds(pl.multiple_of(which * 8, 8), 8)
        return pltpu.make_async_copy(self.out.at[eight], self.result.at[eight], self.local.at[slot])

    def spread(self):
        self.core_copy()().start()
        self.load_copy().start()

    def halve(self):
        group, place, core, lane, x, y = spot()
        self.load_copy().wait()
        self.core_copy()().wait()
        acc, extra = self.acc, self.from_core
        give = [(1 - x) * 2, 4 + (1 - y) * 2]
        keep = [x * 2, 4 + y * 2]
        for start in give:
            for i in range(2):
                acc[start + i] = acc[start + i] + extra[start + i]
        for copy in self.half_copies():
            copy().start()
        for start in keep:
            for i in range(2):
                acc[start + i] = acc[start + i] + extra[start + i]

    def quarter(self):
        group, place, core, lane, x, y = spot()
        for copy in self.half_copies():
            copy().wait()
        acc, extra = self.acc, self.from_first
        acc[x * 2 + 1 - y] = acc[x * 2 + 1 - y] + extra[1 - y]
        acc[4 + y * 2 + 1 - x] = acc[4 + y * 2 + 1 - x] + extra[3 - x]
        for copy in self.quarter_copies():
            copy().start()
        self.stage[0] = acc[x * 2 + y] + extra[y]
        self.stage[1] = acc[4 + y * 2 + x] + extra[2 + x]

    def scatter(self):
        for copy in self.quarter_copies():
            copy().wait()
        for s in range(2):
            self.stage[s] = self.stage[s] + self.from_second[s]
        for send, arrive in self.line_copies():
            send().start()

    def settle(self):
        group, place, core, lane, x, y = spot()
        rows, wide = piece(self.places, self.depth, lane)
        total = self.stage[:, rows, wide].astype(F32)
        pairs = self.line_copies()
        for s in range(1, self.places):
            pairs[s - 1][1]().wait_recv()
            total = total + self.from_line[lax.rem(lane + self.places - s, self.places)].astype(F32)
        first, second = self.own()
        total = total.astype(BF16)
        self.out[first, rows, wide] = total[0]
        self.out[second, rows, wide] = total[1]
        for send, arrive in self.spread_copies():
            send().start()
        for send, arrive in pairs:
            send().wait_send()

    def finish(self, pairs):
        for send, arrive in pairs:
            arrive().wait_recv()
        for send, arrive in pairs:
            send().wait_send()

    def gather(self):
        self.finish(self.spread_copies())
        for send, arrive in self.gather_copies():
            send().start()

    def widen(self):
        self.finish(self.gather_copies())
        for send, arrive in self.widen_copies():
            send().start()

    def share(self):
        core = spot()[2]
        self.finish(self.widen_copies())
        self.share_copy()[0]().start()
        self.store_copy(core, 1).start()

    def store(self):
        core = spot()[2]
        self.share_copy()[1]().wait_recv()
        self.store_copy(1 - core, 2).start()

    def close(self):
        core = spot()[2]
        self.share_copy()[0]().wait_send()
        self.store_copy(core, 1).wait()
        self.store_copy(1 - core, 2).wait()


CHUNK_REFS = 10


def chunk_scratch(places, depth):
    rows, wide = piece_shape(places, depth)
    shapes = [(8, depth, LANES), (8, depth, LANES), (4, depth, LANES), (2, depth, LANES), (places, 2, rows, wide), (2, depth, LANES),
              (16, depth, LANES)]
    links = 7 + 3 * places
    return [pltpu.VMEM(s, BF16) for s in shapes] + [pltpu.SemaphoreType.DMA((links,))] * 2 + [pltpu.SemaphoreType.DMA((3,))]


def greet_all(n):
    group, place, core, lane, x, y = spot()
    barrier = pltpu.get_barrier_semaphore()
    partners = [(group + 1 - 2 * x, place), (group + 2 - 4 * y, place)]
    partners += [(group, lax.rem(place + s, n)) for s in range(1, n)]
    for near, far in partners:
        pl.semaphore_signal(barrier, inc=1, device_id={"tm": near, "res": far}, device_id_type=MESH)
    pl.semaphore_wait(barrier, len(partners))


def run_rounds(active, waiting=()):
    waiting = list(waiting)
    active = list(active)
    while active or waiting:
        if waiting:
            active.append(waiting.pop(0))
        active = [chunk for chunk in active if chunk.advance()]


def chunk_plan(places, early_rows, late_first, late_second):
    unit = grain(places)
    depth = lambda rows: -(-rows // (16 * unit)) * unit
    total = depth(early_rows)
    third = total // 3 // unit * unit
    return [third, third, total - 2 * third], [depth(late_first), depth(late_second)]


def pack(bufs, row, value):
    start = 0
    value = value.astype(BF16)
    for buf in bufs:
        size = buf.shape[0] * buf.shape[1]
        depth = buf.shape[1]
        low, high = max(row, start), min(row + value.shape[0], start + size)
        while low < high:
            slot, inner = divmod(low - start, depth)
            step = min(high - low, depth - inner)
            buf[slot, inner : inner + step, : value.shape[1]] = value[low - row : low - row + step]
            low += step
        start += size


def unpack(bufs, row, count, width):
    pieces = []
    start = 0
    for buf in bufs:
        depth = buf.shape[1]
        size = buf.shape[0] * depth
        low, high = max(row, start), min(row + count, start + size)
        while low < high:
            slot, inner = divmod(low - start, depth)
            step = min(high - low, depth - inner)
            pieces.append((buf[slot, inner : inner + step, : width], low - row))
            low += step
        start += size
    return pieces


def ring_place(n):
    me = lax.axis_index("res")
    return me, [lax.rem(me + s, n) for s in range(n)]


def greet(peers):
    barrier = pltpu.get_barrier_semaphore()
    for peer in peers[1:]:
        pl.semaphore_signal(barrier, inc=1, device_id={"res": peer}, device_id_type=MESH)
    pl.semaphore_wait(barrier, len(peers) - 1)


def copy_to(peer, source, target, send, recv):
    return pltpu.make_async_remote_copy(
        src_ref=source, dst_ref=target, send_sem=send, recv_sem=recv, device_id={"res": peer}, device_id_type=MESH
    )


def swap(n, me, peers, source, target, send, recv):
    sent = [copy_to(peers[s], source.at[s], target.at[me], send.at[s], recv.at[me]) for s in range(1, n)]
    back = [copy_to(peers[s], source.at[s], target.at[peers[s]], send.at[s], recv.at[peers[s]]) for s in range(1, n)]
    return sent, back


def row_norm(values):
    values = values - jnp.mean(values, axis=1, keepdims=True)
    r = lax.rsqrt(jnp.mean(values * values, axis=1, keepdims=True) + EPSILON)
    return values * r, r


def row_norm_back(dh, h, r):
    return r * (dh - jnp.mean(dh, axis=1, keepdims=True) - h * jnp.mean(dh * h, axis=1, keepdims=True))


def table_rows_body(n, fetch_ref, x_ref, chain_ref, flag_ref, win_ref, mid_ref, umid_ref, uout_ref, uin_ref,
                    lhs_ref, self_ref, midt_ref, umidt_ref, uoutt_ref, uedge_ref, sel_ref, tag_ref,
                    idx_out, idx_in, row_out, far, send_a, recv_a, send_b, recv_b):
    me, peers = ring_place(n)
    rows, feat = x_ref.shape
    cap = fetch_ref.shape[1]
    edge_w = win_ref.shape[0] - 2 * feat
    idx_out[...] = jnp.full(idx_out.shape, -1, jnp.int32)
    for s in range(n):
        idx_out[s, 0:1, 0:cap] = fetch_ref[pl.ds(peers[s], 1), :]
    greet(peers)
    sent, back = swap(n, me, peers, idx_out, idx_in, send_a, recv_a)
    for copy in sent:
        copy.start()
    tag = chain_ref[...] * 2 + flag_ref[...]
    tag_ref[...] = tag
    x = x_ref[...]
    wide_tag = jnp.transpose(jnp.broadcast_to(tag.astype(F32), (rows, rows)))
    rich = jnp.concatenate([x, wide_tag.astype(BF16)], axis=1)
    self_ref[...] = jnp.transpose(nn(x, win_ref[:feat, :]))

    def choose(row):
        ids = lax.broadcasted_iota(jnp.int32, (rows, row.shape[1]), 0) + me * rows
        hot = jnp.transpose(jnp.where(ids == row, 1.0, 0.0))[:cap].astype(BF16)
        return hot, nn(hot, rich).astype(BF16)

    hot, block = choose(idx_out[0, 0:1, :])
    sel_ref[me] = hot
    far[me] = block
    copies, backs = swap(n, me, peers, row_out, far, send_b, recv_b)
    for s in range(1, n):
        back[s - 1].wait_recv()
        hot, block = choose(idx_in[peers[s], 0:1, :])
        sel_ref[peers[s]] = hot
        row_out[s] = block
        copies[s - 1].start()
    midt_ref[...] = jnp.transpose(mid_ref[...])
    umidt_ref[...] = jnp.transpose(umid_ref[...])
    uoutt_ref[...] = jnp.transpose(uout_ref[...])
    uedge_ref[...] = jnp.transpose(uin_ref[:, 2 * feat :])
    neigh = win_ref[feat : 2 * feat, :]
    extra = lhs_ref.shape[0] - feat
    table_len = rows + n * cap
    lhs_ref[feat:, table_len:] = jnp.zeros((extra, edge_w), BF16)
    lhs_ref[:feat, table_len:] = jnp.transpose(win_ref[2 * feat :, :])
    lhs_ref[:feat, :rows] = jnp.transpose(nn(x, neigh)).astype(BF16)
    lhs_ref[feat:, :rows] = jnp.broadcast_to(tag.astype(F32), (extra, rows)).astype(BF16)
    for copy in backs:
        copy.wait_recv()
    got = far[...].reshape(n * cap, far.shape[2])
    lhs_ref[:feat, rows:table_len] = jnp.transpose(nn(got[:, :feat], neigh)).astype(BF16)
    lhs_ref[feat:, rows:table_len] = jnp.transpose(got[:, feat:].astype(F32))[:extra].astype(BF16)
    for copy in sent + copies:
        copy.wait_send()


def vmem_call(body, args, outs, scratch, collective, name):
    whole = pl.BlockSpec(memory_space=pltpu.VMEM)
    return pl.pallas_call(
        body,
        out_shape=[jax.ShapeDtypeStruct(s, d) for s, d in outs],
        in_specs=[whole] * len(args),
        out_specs=[whole] * len(outs),
        scratch_shapes=scratch,
        compiler_params=pltpu.CompilerParams(vmem_limit_bytes=VMEM_LIMIT, collective_id=collective, has_side_effects=True),
        name=name,
    )(*args)


def table_rows(n, fetch, x, chain, flag, win, mid, umid, uout, uin):
    rows, feat = x.shape
    cap = fetch.shape[1]
    edge_w = win.shape[0] - 2 * feat
    table_len = rows + n * cap
    outs = [((feat + 16, table_len + edge_w), BF16), ((feat, rows), F32), (mid.shape, BF16), (umid.shape, BF16), (uout.shape, BF16),
            ((edge_w, edge_w), BF16), ((n, cap, rows), BF16), ((1, rows), jnp.int32)]
    sems = [pltpu.SemaphoreType.DMA((n,))] * 4
    scratch = [pltpu.VMEM((n, 8, 128), jnp.int32)] * 2 + [pltpu.VMEM((n, cap, feat + rows), BF16)] * 2 + sems
    return vmem_call(functools.partial(table_rows_body, n), (fetch, x, chain, flag, win, mid, umid, uout, uin), outs, scratch, 0,
                     "table_rows")


def node_forward_body(n, s_ref, cnt_ref, x_ref, mout_ref, gain_ref, off_ref, exp_ref, con_ref, gain2_ref, off2_ref, sel_ref, uin_ref,
                      node_ref, lhs_ref, self_ref, h1_ref, r1_ref, h2_ref, r2_ref, acted_ref, slope_ref,
                      row_out, far, send_a, recv_a):
    me, peers = ring_place(n)
    rows, feat = x_ref.shape
    cap = sel_ref.shape[1]
    edge_w = uin_ref.shape[0]
    mean = jnp.transpose(s_ref[...] / jnp.maximum(cnt_ref[...], 1.0))
    upper = mean.astype(BF16)
    lower = (mean - upper.astype(F32)).astype(BF16)
    aggregate = nn(upper, mout_ref[...]) + nn(lower, mout_ref[...])
    h, r = row_norm(x_ref[...].astype(F32) + aggregate)
    h1_ref[...] = h
    r1_ref[...] = r
    first = h * gain_ref[...].astype(F32) + off_ref[...].astype(F32)
    hidden, slope = gelu_parts(nn(first.astype(BF16), exp_ref[...]))
    acted = hidden.astype(BF16)
    acted_ref[...] = acted
    slope_ref[...] = slope
    h, r = row_norm(first + nn(acted, con_ref[...]))
    h2_ref[...] = h
    r2_ref[...] = r
    low = (h * gain2_ref[...].astype(F32) + off2_ref[...].astype(F32)).astype(BF16)
    node_ref[...] = low
    neigh = nt(low, uin_ref[:, feat : 2 * feat])
    packed = neigh.astype(BF16)
    greet(peers)
    copies, backs = swap(n, me, peers, row_out, far, send_a, recv_a)
    for s in range(1, n):
        row_out[s] = nn(sel_ref[peers[s]], packed).astype(BF16)
        copies[s - 1].start()
    far[me] = nn(sel_ref[me], packed).astype(BF16)
    self_ref[...] = nt(uin_ref[:, :feat], low)
    table_len = rows + n * cap
    lhs_ref[:, :rows] = jnp.transpose(neigh).astype(BF16)
    lhs_ref[:, table_len:] = uin_ref[:, 2 * feat :]
    for copy in backs:
        copy.wait_recv()
    lhs_ref[:, rows:table_len] = jnp.transpose(far[...].reshape(n * cap, edge_w))
    for copy in copies:
        copy.wait_send()


def node_forward(n, s, cnt, x, mout, gain, off, expand, contract, gain2, off2, sel, uin):
    rows, feat = x.shape
    cap = sel.shape[1]
    edge_w = uin.shape[0]
    table_len = rows + n * cap
    hidden = expand.shape[1]
    outs = [(x.shape, BF16), ((edge_w, table_len + edge_w), BF16), ((edge_w, rows), F32), (x.shape, F32), ((rows, 1), F32),
            (x.shape, F32), ((rows, 1), F32), ((rows, hidden), BF16), ((rows, hidden), F32)]
    scratch = [pltpu.VMEM((n, cap, edge_w), BF16)] * 2 + [pltpu.SemaphoreType.DMA((n,))] * 2
    return vmem_call(functools.partial(node_forward_body, n),
                     (s, cnt, x, mout, gain, off, expand, contract, gain2, off2, sel, uin), outs, scratch, 1, "node_forward")


def swap_back_start(n, me, peers, gin, sel_ref, row_out, far, send, recv, rows):
    cap = sel_ref.shape[1]
    copies, backs = swap(n, me, peers, row_out, far, send, recv)
    for s in range(1, n):
        start = pl.multiple_of(rows + peers[s] * cap, cap)
        row_out[s] = gin[pl.ds(start, cap), :].astype(BF16)
        copies[s - 1].start()
    far[me] = gin[pl.ds(pl.multiple_of(rows + me * cap, cap), cap), :].astype(BF16)
    return copies, backs


def swap_back_finish(n, copies, gin, sel_ref, far, rows):
    cap = sel_ref.shape[1]
    width = gin.shape[1]
    for copy in copies[1]:
        copy.wait_recv()
    total = gin[:rows, :] + tn(sel_ref[...].reshape(n * cap, rows), far[...].reshape(n * cap, width))
    for copy in copies[0]:
        copy.wait_send()
    return total.astype(BF16)


def node_backward_body(n, gin_ref, dself_ref, sel_ref, node_ref, cot_ref, uin_ref, h1_ref, r1_ref, h2_ref, r2_ref, acted_ref, slope_ref,
                       gain_ref, off_ref, gain2_ref, exp_ref, con_ref, s_ref, cnt_ref, mout_ref, ggain_ref, goff_ref,
                       gumid_ref, guout_ref, dfirst_ref, d2_ref, *rest):
    chunks, (row_out, far, send_a, recv_a) = rest[:-4], rest[-4:]
    me, peers = ring_place(n)
    rows, feat = node_ref.shape
    edge_w = uin_ref.shape[0]
    greet(peers)
    copies = swap_back_start(n, me, peers, gin_ref, sel_ref, row_out, far, send_a, recv_a, rows)
    own = swap_back_finish(n, copies, gin_ref, sel_ref, far, rows)
    table_len = gin_ref.shape[0] - edge_w
    dself_t = dself_ref[...].astype(BF16)
    dself = jnp.transpose(dself_ref[...]).astype(BF16)
    node = node_ref[...]
    at = early_rows(feat, acted_ref.shape[1], edge_w)
    pack(chunks, at["update_self"], nn(dself_t, node))
    pack(chunks, at["update_neigh"], tn(own, node))
    gap = jnp.zeros((edge_w, 256 - edge_w), F32)
    pack(chunks, at["update_edge"], jnp.concatenate([jnp.transpose(gin_ref[table_len:, :]), gap, gumid_ref[...], gap], axis=1))
    pack(chunks, at["update_out"], jnp.concatenate([guout_ref[...], jnp.zeros((edge_w, feat - edge_w), F32)], axis=1))
    dy = cot_ref[...].astype(F32) + nn(dself, uin_ref[:, :feat]) + nn(own, uin_ref[:, feat : 2 * feat])
    h2 = h2_ref[...]
    ffn_sums = [jnp.sum(dy * h2, axis=0, keepdims=True), jnp.sum(dy, axis=0, keepdims=True)]
    second = row_norm_back(dy * gain2_ref[...].astype(F32), h2, r2_ref[...])
    dffn = second.astype(BF16)
    for b in range(acted_ref.shape[1] // feat):
        pack(chunks, at["contract"] + b * feat, tn(acted_ref[:, b * feat : (b + 1) * feat], dffn))
    dinner = (nt(dffn, con_ref[...]) * slope_ref[...]).astype(BF16)
    h1 = h1_ref[...]
    gain = gain_ref[...].astype(F32)
    first_low = (h1 * gain + off_ref[...].astype(F32)).astype(BF16)
    for b in range(acted_ref.shape[1] // feat):
        pack(chunks, at["expand"] + b * feat, tn(first_low, dinner[:, b * feat : (b + 1) * feat]))
    dy = second + nt(dinner, exp_ref[...])
    sums = [jnp.sum(dy * h1, axis=0, keepdims=True), jnp.sum(dy, axis=0, keepdims=True)] + ffn_sums
    dfirst = row_norm_back(dy * gain, h1, r1_ref[...])
    dfirst_ref[...] = dfirst
    back = (jnp.transpose(dfirst) / jnp.maximum(cnt_ref[...], 1.0)).astype(BF16)
    d2_ref[...] = nn(mout_ref[...], back)
    pack(chunks, at["message_out"], nt(s_ref[...].astype(BF16), back))
    side = jnp.zeros((1, feat - edge_w), F32)
    for ref in (ggain_ref, goff_ref):
        sums.append(jnp.concatenate([jnp.sum(jnp.transpose(ref[...]), axis=0, keepdims=True), side], axis=1))
    pack(chunks, at["vectors"], jnp.concatenate(sums + [jnp.zeros((10, feat), F32)], axis=0))
    used = at["end"]
    spare = sum(c.shape[0] * c.shape[1] for c in chunks) - used
    if spare:
        pack(chunks, used, jnp.zeros((spare, feat), F32))


def early_rows(feat, hidden, edge_w):
    at, row = {}, 0
    for name, count in (("contract", hidden), ("expand", hidden), ("message_out", feat), ("update_self", edge_w),
                        ("update_neigh", edge_w), ("update_edge", edge_w), ("update_out", edge_w), ("vectors", 16)):
        at[name] = row
        row += count
    at["end"] = row
    return at


def node_backward(n, gin, dself, sel, node, cot, uin, h1, r1, h2, r2, acted, slope, gain, off, gain2, expand, contract, s, cnt, mout,
                  ggain, goff, gumid, guout, depths):
    rows, feat = node.shape
    cap = sel.shape[1]
    edge_w = uin.shape[0]
    outs = [(node.shape, F32), ((feat, rows), F32)] + [((16, d, LANES), BF16) for d in depths]
    scratch = [pltpu.VMEM((n, cap, edge_w), BF16)] * 2 + [pltpu.SemaphoreType.DMA((n,))] * 2
    return vmem_call(functools.partial(node_backward_body, n),
                     (gin, dself, sel, node, cot, uin, h1, r1, h2, r2, acted, slope, gain, off, gain2, expand, contract, s, cnt, mout,
                      ggain, goff, gumid, guout), outs, scratch, 2, "node_backward")


EARLY_STEPS = {0: (0, 1, 2), 1: (0, 1), 3: (0, 2), 4: (1,), 5: (0,)}


def message_backward_body(n, table_len, slabs, early, late, *refs):
    (e_ref, h1_ref, gp1_ref, gp2_ref, part_ref, keep_ref, nbr_ref, d2_ref, mid_ref, win_ref, x_ref, dfirst_ref, sel_ref) = refs[:13]
    refs = refs[13:]
    sources, refs = refs[:early], refs[early:]
    egrad_ref, grad_ref, results, refs = refs[0], refs[1], refs[2 : 2 + early + late], refs[2 + early + late :]
    (gmid, gin, dself_sum, row_out, far, send_a, recv_a), refs = refs[:7], refs[7:]
    late_sources, refs = refs[:late], refs[late:]
    places = n // 2
    chunks = [Chunk(places, (list(sources) + list(late_sources))[i], results[i], *refs[CHUNK_REFS * i : CHUNK_REFS * (i + 1)])
              for i in range(early + late)]
    step = pl.program_id(0)
    base = step * slabs
    steps = pl.num_programs(0)
    rows = nbr_ref.shape[1]
    feat = d2_ref.shape[0]

    @pl.when(step == 0)
    def _():
        greet_all(n)
        for ref in (gmid, gin, dself_sum):
            ref[...] = jnp.zeros_like(ref)

    for at, which in EARLY_STEPS.items():

        @pl.when(step == at)
        def _(which=which):
            for i in which:
                chunks[i].advance()

    x = edge_operand(table_len, slabs, base, e_ref, nbr_ref)
    back = d2_ref[...]
    wide = lambda ref: jnp.concatenate([ref[j] for j in range(slabs)], axis=1)
    two = jnp.concatenate([(back * keep_ref[j] * gp2_ref[j].astype(F32)).astype(BF16) for j in range(slabs)], axis=1)
    gmid[...] += nt(wide(h1_ref), two)
    one = (nn(mid_ref[...], two) * wide(gp1_ref).astype(F32)).astype(BF16)
    gin[...] += nt(x, one)
    part = nn(win_ref[2 * feat :, :], one)
    total = dself_sum[...]
    for j in range(slabs):
        cut = slice(j * rows, (j + 1) * rows)
        egrad_ref[j] = part_ref[j] + part[:, cut]
        total = total + one[:, cut].astype(F32)
    dself_sum[...] = total

    @pl.when(step == steps - 1)
    def _():
        me, peers = ring_place(n)
        copies = swap_back_start(n, me, peers, gin, sel_ref, row_out, far, send_a, recv_a, rows)
        first, second = late_sources
        pack([first], 0, gmid[...])
        pack([first], feat, gin[table_len:, :])
        end = feat + gin.shape[0] - table_len
        spare = first.shape[0] * first.shape[1] - end
        if spare:
            pack([first], end, jnp.zeros((spare, feat), F32))
        chunks[early].advance()
        dself = jnp.transpose(dself_sum[...]).astype(BF16)
        nodes = x_ref[...]
        pack([second], 0, tn(nodes, dself))
        own = swap_back_finish(n, copies, gin, sel_ref, far, rows)
        pack([second], feat, tn(nodes, own))
        spare = second.shape[0] * second.shape[1] - 2 * feat
        if spare:
            pack([second], 2 * feat, jnp.zeros((spare, feat), F32))
        chunks[early + 1].advance()
        grad_ref[...] = dfirst_ref[...] + nt(dself, win_ref[:feat, :]) + nt(own, win_ref[feat : 2 * feat, :])
        run_rounds(chunks)


def message_backward(n, e, h1, gp1, gp2, part, keep, nbr, d2, mid, win, x, dfirst, sel, sources, late_depths, table_len, slabs):
    fan, edge_w, rows = e.shape
    feat = d2.shape[0]
    cap = sel.shape[1]
    places = n // 2
    whole = lambda a: pl.BlockSpec(a.shape, lambda i: (0,) * a.ndim)
    slab = lambda f: pl.BlockSpec((slabs, f, rows), lambda i: (i, 0, 0))
    anywhere = pl.BlockSpec(memory_space=pl.ANY)
    consts = (nbr, d2, mid, win, x, dfirst, sel)
    depths = [s.shape[1] for s in sources] + list(late_depths)
    scratch = [pltpu.VMEM((feat, feat), F32), pltpu.VMEM((table_len + edge_w, feat), F32), pltpu.VMEM((feat, rows), F32)]
    scratch += [pltpu.VMEM((n, cap, feat), BF16)] * 2 + [pltpu.SemaphoreType.DMA((n,))] * 2
    scratch += [pltpu.VMEM((16, d, LANES), BF16) for d in late_depths]
    for d in depths:
        scratch += chunk_scratch(places, d)
    return pl.pallas_call(
        functools.partial(message_backward_body, n, table_len, slabs, len(sources), len(late_depths)),
        grid=(fan // slabs,),
        in_specs=[slab(edge_w), slab(feat), slab(feat), slab(feat), slab(edge_w), slab(1)] + [whole(a) for a in consts]
        + [anywhere] * len(sources),
        out_specs=[slab(edge_w), whole(x)] + [anywhere] * len(depths),
        out_shape=[jax.ShapeDtypeStruct(e.shape, F32), jax.ShapeDtypeStruct(x.shape, F32)]
        + [jax.ShapeDtypeStruct((16, d, LANES), BF16) for d in depths],
        scratch_shapes=scratch,
        compiler_params=pltpu.CompilerParams(vmem_limit_bytes=VMEM_LIMIT, collective_id=3, has_side_effects=True),
        name="message_backward",
    )(e, h1, gp1, gp2, part, keep, *consts, *sources)


def unpack_body(early, late, feat, hidden, edge_w, *refs):
    count = early + late
    sources, refs = refs[:count], refs[count:]
    (gwin, gmid, gmout, gexp, gcon, guin, gumid, guout, gv, ge), refs = refs[:10], refs[10:]
    held, refs = refs[:count], refs[count:]
    (swin, smid, smout, sexp, scon, suin), load, send = refs[:6], refs[6], refs[7]
    loads = [pltpu.make_async_copy(sources[i], held[i], load.at[i]) for i in range(count)]
    for copy in loads:
        copy.start()
    at = early_rows(feat, hidden, edge_w)
    sent = []

    def push(source, target):
        copy = pltpu.make_async_copy(source, target, send.at[len(sent)])
        copy.start()
        sent.append(copy)

    ready = [0]

    def section(bufs, row, size, width, target, top=0, left=0, lane=0):
        for value, offset in unpack(bufs, row, size, LANES):
            target[top + offset : top + offset + value.shape[0], left : left + width] = value[:, lane : lane + width].astype(F32)

    def need(rows, first):
        start = 0
        for i in range(first, count):
            if start < rows and i >= ready[0]:
                loads[i].wait()
                ready[0] = i + 1
            start += held[i].shape[0] * held[i].shape[1]

    front, back = held[:early], held[early:]
    for b in range(hidden // feat):
        need(at["contract"] + (b + 1) * feat, 0)
        section(front, at["contract"] + b * feat, feat, feat, scon, top=b * feat)
        push(scon.at[pl.ds(b * feat, feat)], gcon.at[pl.ds(b * feat, feat)])
    for b in range(hidden // feat):
        need(at["expand"] + (b + 1) * feat, 0)
        section(front, at["expand"] + b * feat, feat, feat, sexp, left=b * feat)
        push(sexp.at[:, pl.ds(b * feat, feat)], gexp.at[:, pl.ds(b * feat, feat)])
    for copy in loads[ready[0]:]:
        copy.wait()
    section(front, at["message_out"], feat, feat, smout)
    push(smout, gmout)
    section(front, at["update_self"], edge_w, feat, suin)
    section(front, at["update_neigh"], edge_w, feat, suin, left=feat)
    section(front, at["update_edge"], edge_w, edge_w, suin, left=2 * feat)
    push(suin, guin)
    section(front, at["update_edge"], edge_w, edge_w, gumid, lane=256)
    section(front, at["update_out"], edge_w, edge_w, guout)
    vectors = unpack(front, at["vectors"], 16, LANES)[0][0].astype(F32)
    gv[...] = vectors[:4]
    ge[...] = vectors[4:6, :edge_w]
    section(back[:1], 0, feat, feat, smid)
    push(smid, gmid)
    section(back[:1], feat, edge_w, feat, swin, top=2 * feat)
    section(back[1:], 0, 2 * feat, feat, swin)
    push(swin, gwin)
    for copy in sent:
        copy.wait()


def unpack_all(chunks, early, feat, hidden, edge_w):
    whole, anywhere = pl.BlockSpec(memory_space=pltpu.VMEM), pl.BlockSpec(memory_space=pl.ANY)
    big = [(2 * feat + edge_w, feat), (feat, feat), (feat, feat), (feat, hidden), (hidden, feat), (edge_w, 2 * feat + edge_w)]
    small = [(edge_w, edge_w), (edge_w, edge_w), (4, feat), (2, edge_w)]
    return pl.pallas_call(
        functools.partial(unpack_body, early, len(chunks) - early, feat, hidden, edge_w),
        in_specs=[anywhere] * len(chunks),
        out_specs=[anywhere] * 6 + [whole] * 4,
        out_shape=[jax.ShapeDtypeStruct(s, F32) for s in big + small],
        scratch_shapes=[pltpu.VMEM(c.shape, BF16) for c in chunks] + [pltpu.VMEM(s, F32) for s in big]
        + [pltpu.SemaphoreType.DMA((len(chunks),)), pltpu.SemaphoreType.DMA((16,))],
        compiler_params=pltpu.CompilerParams(vmem_limit_bytes=VMEM_LIMIT),
        name="unpack_all",
    )(*chunks)


def local(n, node_feats, edge_feats, node_cotan, edge_cotan, neighbour, edge_mask, fetch_rows, chain_ids, complex_flag, message_in,
          message_mid, message_out, gain_node, offset_node, expand_weight, contract_weight, gain_ffn, offset_ffn, update_in, update_mid,
          update_out, gain_edge, offset_edge):
    x = node_feats[0]
    rows, feat = x.shape
    fan = neighbour.shape[1]
    edge_w = edge_feats.shape[3]
    e = jnp.transpose(edge_feats[0], (1, 2, 0))
    cot = jnp.transpose(edge_cotan[0], (1, 2, 0))
    nbr = jnp.transpose(neighbour)
    mask = jnp.transpose(edge_mask)
    uin = jnp.transpose(update_in)
    line = lambda v: v.reshape(1, -1)
    lhs, self_t, mid_t, umid_t, uout_t, uedge, sel, tag = table_rows(
        n, fetch_rows[0], x, line(chain_ids), line(complex_flag), message_in, message_mid, update_mid, update_out, uin
    )
    table_len = lhs.shape[1] - edge_w
    slabs = next(c for c in (10, 6, 4, 2, 1) if fan % c == 0)
    h1, gp1, gp2, s, keep, cnt = message_forward(e, nbr, mask, tag, lhs, self_t, mid_t, slabs)
    node, lhs3, self3, n1, r1, n2, r2, acted, slope = node_forward(
        n, s, cnt, x, message_out, line(gain_node), line(offset_node), expand_weight, contract_weight, line(gain_ffn), line(offset_ffn),
        sel, uin
    )
    column = lambda v: v.astype(F32).reshape(-1, 1)
    edge_new, part, guout, gumid, gin3, dself3, ggain, goff = edge_pass(
        e, cot, nbr, lhs3, self3, umid_t, uout_t, update_mid, update_out, uedge, column(gain_edge), column(offset_edge), slabs
    )
    hidden = expand_weight.shape[1]
    early_depths, late_depths = chunk_plan(n // 2, early_rows(feat, hidden, edge_w)["end"], feat + edge_w, 2 * feat)
    dfirst, d2, *sources = node_backward(
        n, gin3, dself3, sel, node, node_cotan[0], uin, n1, r1, n2, r2, acted, slope, line(gain_node), line(offset_node), line(gain_ffn),
        expand_weight, contract_weight, s, cnt, message_out, ggain, goff, gumid, guout, early_depths
    )
    egrad, ngrad, *sums = message_backward(
        n, e, h1, gp1, gp2, part, keep, nbr, d2, message_mid, message_in, x, dfirst, sel, sources, late_depths, table_len, slabs
    )
    gwin, gmid, gmout, gexp, gcon, guin, gumid, guout, gv, ge = unpack_all(sums, len(sources), feat, hidden, edge_w)
    native = lambda a: jnp.transpose(a, (2, 0, 1))[None]
    return (node[None], native(edge_new), ngrad[None], native(egrad), gwin, gmid, gmout, gv[0], gv[1], gexp, gcon, gv[2], gv[3],
            jnp.transpose(guin), gumid, guout, ge[0], ge[1])


def solution(mesh):
    grouped, placed, copied = P("tm", "res", None), P("res", None), P()
    wide = P("tm", "res", None, None)
    arguments = (grouped, wide, grouped, wide, placed, placed, P("res", None, None), P("res"), P("res")) + (copied,) * 14
    return jax.shard_map(
        functools.partial(local, mesh.shape["res"]),
        mesh=mesh,
        in_specs=arguments,
        out_specs=(grouped, wide, grouped, wide) + (copied,) * 14,
        check_vma=False,
    )
```

```python
import functools
import jax
import jax.numpy as jnp
from jax import lax
from jax.experimental import pallas as pl
from jax.experimental.pallas import tpu as pltpu
from jax.sharding import PartitionSpec as P

EPSILON = 1e-05
CURVE = 0.7978845608028654
CUBIC = 0.044715
F32 = jnp.float32
BF16 = jnp.bfloat16
VMEM_LIMIT = 60 * 1024 * 1024
MESH = pl.DeviceIdType.MESH


def nn(a, b):
    return lax.dot_general(a, b, (((1,), (0,)), ((), ())), preferred_element_type=F32)


def nt(a, b):
    return lax.dot_general(a, b, (((1,), (1,)), ((), ())), preferred_element_type=F32)


def tn(a, b):
    return lax.dot_general(a, b, (((0,), (0,)), ((), ())), preferred_element_type=F32)


def gelu_parts(v):
    square = v * v
    t = jnp.tanh(v * (CURVE + (CURVE * CUBIC) * square))
    half = 0.5 + 0.5 * t
    slope = half + (half - half * half) * (v * (2.0 * CURVE + (6.0 * CURVE * CUBIC) * square))
    return v * half, slope


def tile_lanes(block, count):
    return jnp.concatenate([block] * count, axis=1) if count > 1 else block


def edge_operand(table_len, slabs, base, e_ref, nbr_ref):
    columns = []
    for j in range(slabs):
        row = nbr_ref[pl.ds(base + j, 1), :]
        ids = lax.broadcasted_iota(jnp.int32, (table_len, row.shape[1]), 0)
        hot = jnp.where(ids == row, 1.0, 0.0).astype(BF16)
        columns.append(jnp.concatenate([hot, e_ref[j]], axis=0))
    return jnp.concatenate(columns, axis=1) if slabs > 1 else columns[0]


def message_forward_body(table_len, feat, slabs, e_ref, nbr_ref, mask_ref, own_ref, lhs_ref, self_ref, mid_ref,
                         h1_ref, gp1_ref, gp2_ref, s_ref, keep_ref, cnt_ref):
    step = pl.program_id(0)
    base = step * slabs
    rows = nbr_ref.shape[1]

    @pl.when(step == 0)
    def _():
        s_ref[...] = jnp.zeros_like(s_ref)
        cnt_ref[...] = jnp.zeros_like(cnt_ref)

    own = own_ref[...]
    own_chain = own // 2
    own_flag = own % 2
    pre = nn(lhs_ref[...], edge_operand(table_len, slabs, base, e_ref, nbr_ref))
    hidden, slope = gelu_parts(pre[:feat] + tile_lanes(self_ref[...], slabs))
    hidden = hidden.astype(BF16)
    slope = slope.astype(BF16)
    total = s_ref[...]
    count = cnt_ref[...]
    keeps = []
    for j in range(slabs):
        cut = slice(j * rows, (j + 1) * rows)
        h1_ref[j] = hidden[:, cut]
        gp1_ref[j] = slope[:, cut]
        other = pre[feat : feat + 1, cut].astype(jnp.int32)
        joined = jnp.logical_or(own_chain == other // 2, own_flag * (other % 2) > 0)
        keep = jnp.where(joined, 1.0, 0.0) * mask_ref[pl.ds(base + j, 1), :].astype(F32)
        keep_ref[j] = keep
        keeps.append(keep)
        count = count + keep
    hidden, slope = gelu_parts(nn(mid_ref[...], hidden))
    slope = slope.astype(BF16)
    for j in range(slabs):
        cut = slice(j * rows, (j + 1) * rows)
        gp2_ref[j] = slope[:, cut]
        total = total + hidden[:, cut] * keeps[j]
    s_ref[...] = total
    cnt_ref[...] = count


def message_forward(e, nbr, mask, own_tag, lhs, self_t, mid_t, slabs):
    fan, edge_w, rows = e.shape
    feat = self_t.shape[0]
    table_len = lhs.shape[1] - edge_w
    whole = lambda a: pl.BlockSpec(a.shape, lambda i: (0,) * a.ndim)
    slab = lambda f: pl.BlockSpec((slabs, f, rows), lambda i: (i, 0, 0))
    big = pltpu.HBM((fan, feat, rows), BF16)
    e, nbr, mask = far_off(e, nbr, mask)
    return pl.pallas_call(
        functools.partial(message_forward_body, table_len, feat, slabs),
        grid=(fan // slabs,),
        in_specs=[slab(edge_w), whole(nbr), whole(mask), whole(own_tag), whole(lhs), whole(self_t), whole(mid_t)],
        out_specs=[slab(feat), slab(feat), slab(feat), pl.BlockSpec((feat, rows), lambda i: (0, 0)), slab(1),
                   pl.BlockSpec((1, rows), lambda i: (0, 0))],
        out_shape=[big, big, big, jax.ShapeDtypeStruct((feat, rows), F32), pltpu.HBM((fan, 1, rows), F32),
                   jax.ShapeDtypeStruct((1, rows), F32)],
        compiler_params=pltpu.CompilerParams(vmem_limit_bytes=30 * 1024 * 1024),
        name="message_forward",
    )(e, nbr, mask, own_tag, lhs, self_t, mid_t)


def edge_body(table_len, slabs, e_ref, cot_ref, nbr_ref, lhs_ref, self_ref, mid_t_ref, out_t_ref, mid_ref, out_ref, edge_ref,
              gain_ref, offset_ref,
              new_ref, part_ref, gout_ref, gmid_ref, gin_ref, dself_ref, ggain_ref, goff_ref):
    step = pl.program_id(0)
    base = step * slabs
    rows = nbr_ref.shape[1]

    @pl.when(step == 0)
    def _():
        for ref in (gout_ref, gmid_ref, gin_ref, dself_ref, ggain_ref, goff_ref):
            ref[...] = jnp.zeros_like(ref)

    x = edge_operand(table_len, slabs, base, e_ref, nbr_ref)
    self_t = tile_lanes(self_ref[...], slabs)
    hidden_three, slope_three = gelu_parts(nn(lhs_ref[...], x) + self_t)
    hidden_three = hidden_three.astype(BF16)
    hidden_four, slope_four = gelu_parts(nn(mid_t_ref[...], hidden_three))
    hidden_four = hidden_four.astype(BF16)
    branch = nn(out_t_ref[...], hidden_four)
    gain = gain_ref[...]
    offset = offset_ref[...]
    scale = 1.0 / e_ref.shape[1]
    resid = []
    ggain = ggain_ref[...]
    goff = goff_ref[...]
    for j in range(slabs):
        z = e_ref[j].astype(F32) + branch[:, j * rows : (j + 1) * rows]
        z = z - jnp.sum(z, axis=0, keepdims=True) * scale
        r = lax.rsqrt(jnp.sum(z * z, axis=0, keepdims=True) * scale + EPSILON)
        h = z * r
        new_ref[j] = (h * gain + offset).astype(BF16)
        dy = cot_ref[j].astype(F32)
        ggain = ggain + dy * h
        goff = goff + dy
        dh = dy * gain
        one = jnp.sum(dh, axis=0, keepdims=True) * scale
        two = jnp.sum(dh * h, axis=0, keepdims=True) * scale
        resid.append(r * (dh - one - h * two))
    ggain_ref[...] = ggain
    goff_ref[...] = goff
    resid = jnp.concatenate(resid, axis=1) if slabs > 1 else resid[0]
    delta = resid.astype(BF16)
    gout_ref[...] += nt(hidden_four, delta)
    delta_four = (nn(out_ref[...], delta) * slope_four).astype(BF16)
    gmid_ref[...] += nt(hidden_three, delta_four)
    delta_three = nn(mid_ref[...], delta_four) * slope_three
    low = delta_three.astype(BF16)
    gin_ref[...] += nt(x, low)
    part = resid + nn(edge_ref[...], low)
    dself = dself_ref[...]
    for j in range(slabs):
        cut = slice(j * rows, (j + 1) * rows)
        part_ref[j] = part[:, cut]
        dself = dself + low[:, cut].astype(F32)
    dself_ref[...] = dself


def edge_pass(e, cot, nbr, lhs, self_t, mid_t, out_t, mid, out, edge, gain, offset, slabs):
    fan, edge_w, rows = e.shape
    table_len = lhs.shape[1] - edge_w
    whole = lambda a: pl.BlockSpec(a.shape, lambda i: (0,) * a.ndim)
    slab = pl.BlockSpec((slabs, edge_w, rows), lambda i: (i, 0, 0))
    keep = lambda *s: (pl.BlockSpec(s, lambda i: (0,) * len(s)), jax.ShapeDtypeStruct(s, F32))
    sums = [keep(edge_w, edge_w), keep(edge_w, edge_w), keep(table_len + edge_w, edge_w), keep(edge_w, rows), keep(edge_w, rows),
            keep(edge_w, rows)]
    e, cot, nbr, mid, out = far_off(e, cot, nbr, mid, out)
    consts = (nbr, lhs, self_t, mid_t, out_t, mid, out, edge, gain, offset)
    return pl.pallas_call(
        functools.partial(edge_body, table_len, slabs),
        grid=(fan // slabs,),
        in_specs=[slab, slab] + [whole(a) for a in consts],
        out_specs=[slab, slab] + [s for s, _ in sums],
        out_shape=[pltpu.HBM(e.shape, BF16), pltpu.HBM(e.shape, F32)] + [s for _, s in sums],
        compiler_params=pltpu.CompilerParams(vmem_limit_bytes=30 * 1024 * 1024),
        name="edge_pass",
    )(e, cot, *consts)


LANES = 512


def spot():
    group, place = lax.axis_index("tm"), lax.axis_index("res")
    return group, place, lax.rem(place, 2), place // 2, lax.rem(group, 2), group // 2


def grain(places):
    return 16 * max(1, places // 4)


def piece(places, depth, index):
    across = min(places, 4)
    rows, wide = piece_shape(places, depth)
    top = pl.multiple_of((index // across) * rows, rows)
    left = pl.multiple_of(lax.rem(index, across) * wide, wide)
    return pl.ds(top, rows), pl.ds(left, wide)


def piece_shape(places, depth):
    across = min(places, 4)
    return depth // (places // across), LANES // across


def remote(source, target, send, recv, group, place):
    return pltpu.make_async_remote_copy(
        src_ref=source, dst_ref=target, send_sem=send, recv_sem=recv, device_id={"tm": group, "res": place}, device_id_type=MESH
    )


class Chunk:
    def __init__(self, places, source, result, acc, from_core, from_first, from_second, from_line, stage, out, sends, recvs, local):
        self.places, self.source, self.result, self.acc = places, source, result, acc
        self.from_core, self.from_first, self.from_second = from_core, from_first, from_second
        self.from_line, self.stage, self.out = from_line, stage, out
        self.sends, self.recvs, self.local = sends, recvs, local
        self.depth = acc.shape[1]

    def run(self, stage):
        (self.spread, self.halve, self.quarter, self.scatter, self.settle, self.gather, self.widen, self.share, self.store,
         self.close)[stage]()

    def link(self, slot, source, target, group, place):
        return functools.partial(remote, source, target, self.sends.at[slot], self.recvs.at[slot], group, place)

    def core_copy(self):
        group, place, core, lane, x, y = spot()
        theirs = pl.multiple_of((1 - core) * 8, 8)
        return self.link(0, self.source.at[pl.ds(theirs, 8)], self.from_core, group, place + 1 - 2 * core)

    def load_copy(self):
        core = spot()[2]
        return pltpu.make_async_copy(self.source.at[pl.ds(pl.multiple_of(core * 8, 8), 8)], self.acc, self.local.at[0])

    def half_copies(self):
        group, place, core, lane, x, y = spot()
        return [
            self.link(1, self.acc.at[pl.ds((1 - x) * 2, 2)], self.from_first.at[pl.ds(0, 2)], group + 1 - 2 * x, place),
            self.link(2, self.acc.at[pl.ds(4 + (1 - y) * 2, 2)], self.from_first.at[pl.ds(2, 2)], group + 2 - 4 * y, place),
        ]

    def quarter_copies(self):
        group, place, core, lane, x, y = spot()
        return [
            self.link(3, self.acc.at[x * 2 + 1 - y], self.from_second.at[0], group + 2 - 4 * y, place),
            self.link(4, self.acc.at[4 + y * 2 + 1 - x], self.from_second.at[1], group + 1 - 2 * x, place),
        ]

    def line_copies(self):
        group, place, core, lane, x, y = spot()
        copies = []
        for s in range(1, self.places):
            ahead, behind = lax.rem(lane + s, self.places), lax.rem(lane + self.places - s, self.places)
            rows, wide = piece(self.places, self.depth, ahead)
            view = self.stage.at[:, rows, wide]
            copies.append((self.link(4 + s, view, self.from_line.at[lane], group, ahead * 2 + core),
                           self.link(4 + s, view, self.from_line.at[behind], group, behind * 2 + core)))
        return copies

    def own(self):
        group, place, core, lane, x, y = spot()
        return core * 8 + x * 2 + y, core * 8 + 4 + y * 2 + x

    def spread_copies(self):
        group, place, core, lane, x, y = spot()
        copies = []
        slot = 4 + self.places
        for own in self.own():
            for s in range(1, self.places):
                ahead, behind = lax.rem(lane + s, self.places), lax.rem(lane + self.places - s, self.places)
                rows, wide = piece(self.places, self.depth, lane)
                back_rows, back_wide = piece(self.places, self.depth, behind)
                view, back = self.out.at[own, rows, wide], self.out.at[own, back_rows, back_wide]
                copies.append((self.link(slot, view, view, group, ahead * 2 + core), self.link(slot, back, back, group, behind * 2 + core)))
                slot += 1
        return copies

    def both(self, slot, view, back, group, place):
        return self.link(slot, view, view, group, place), self.link(slot, back, back, group, place)

    def gather_copies(self):
        group, place, core, lane, x, y = spot()
        slot = 2 + 3 * self.places
        first, second = self.own()
        return [
            self.both(slot, self.out.at[first], self.out.at[core * 8 + x * 2 + 1 - y], group + 2 - 4 * y, place),
            self.both(slot + 1, self.out.at[second], self.out.at[core * 8 + 4 + y * 2 + 1 - x], group + 1 - 2 * x, place),
        ]

    def widen_copies(self):
        group, place, core, lane, x, y = spot()
        slot = 4 + 3 * self.places
        two = lambda start: self.out.at[pl.ds(start, 2)]
        return [
            self.both(slot, two(core * 8 + x * 2), two(core * 8 + 2 - x * 2), group + 1 - 2 * x, place),
            self.both(slot + 1, two(core * 8 + 4 + y * 2), two(core * 8 + 6 - y * 2), group + 2 - 4 * y, place),
        ]

    def share_copy(self):
        group, place, core, lane, x, y = spot()
        eight = lambda which: self.out.at[pl.ds(pl.multiple_of(which * 8, 8), 8)]
        return self.both(6 + 3 * self.places, eight(core), eight(1 - core), group, place + 1 - 2 * core)

    def store_copy(self, which, slot):
        eight = pl.ds(pl.multiple_of(which * 8, 8), 8)
        return pltpu.make_async_copy(self.out.at[eight], self.result.at[eight], self.local.at[slot])

    def spread(self):
        self.core_copy()().start()
        self.load_copy().start()

    def halve(self):
        group, place, core, lane, x, y = spot()
        self.load_copy().wait()
        self.core_copy()().wait()
        acc, extra = self.acc, self.from_core
        give = [(1 - x) * 2, 4 + (1 - y) * 2]
        keep = [x * 2, 4 + y * 2]
        for start in give:
            for i in range(2):
                acc[start + i] = acc[start + i] + extra[start + i]
        for copy in self.half_copies():
            copy().start()
        for start in keep:
            for i in range(2):
                acc[start + i] = acc[start + i] + extra[start + i]

    def quarter(self):
        group, place, core, lane, x, y = spot()
        for copy in self.half_copies():
            copy().wait()
        acc, extra = self.acc, self.from_first
        acc[x * 2 + 1 - y] = acc[x * 2 + 1 - y] + extra[1 - y]
        acc[4 + y * 2 + 1 - x] = acc[4 + y * 2 + 1 - x] + extra[3 - x]
        for copy in self.quarter_copies():
            copy().start()
        self.stage[0] = acc[x * 2 + y] + extra[y]
        self.stage[1] = acc[4 + y * 2 + x] + extra[2 + x]

    def scatter(self):
        for copy in self.quarter_copies():
            copy().wait()
        for s in range(2):
            self.stage[s] = self.stage[s] + self.from_second[s]
        for send, arrive in self.line_copies():
            send().start()

    def settle(self):
        group, place, core, lane, x, y = spot()
        rows, wide = piece(self.places, self.depth, lane)
        total = self.stage[:, rows, wide].astype(F32)
        pairs = self.line_copies()
        for s in range(1, self.places):
            pairs[s - 1][1]().wait_recv()
            total = total + self.from_line[lax.rem(lane + self.places - s, self.places)].astype(F32)
        first, second = self.own()
        total = total.astype(BF16)
        self.out[first, rows, wide] = total[0]
        self.out[second, rows, wide] = total[1]
        for send, arrive in self.spread_copies():
            send().start()
        for send, arrive in pairs:
            send().wait_send()

    def finish(self, pairs):
        for send, arrive in pairs:
            arrive().wait_recv()
        for send, arrive in pairs:
            send().wait_send()

    def gather(self):
        self.finish(self.spread_copies())
        for send, arrive in self.gather_copies():
            send().start()

    def widen(self):
        self.finish(self.gather_copies())
        for send, arrive in self.widen_copies():
            send().start()

    def share(self):
        core = spot()[2]
        self.finish(self.widen_copies())
        self.share_copy()[0]().start()
        self.store_copy(core, 1).start()

    def store(self):
        core = spot()[2]
        self.share_copy()[1]().wait_recv()
        self.store_copy(1 - core, 2).start()

    def close(self):
        core = spot()[2]
        self.share_copy()[0]().wait_send()
        self.store_copy(core, 1).wait()
        self.store_copy(1 - core, 2).wait()


CHUNK_REFS = 10


def chunk_scratch(places, depth):
    rows, wide = piece_shape(places, depth)
    shapes = [(8, depth, LANES), (8, depth, LANES), (4, depth, LANES), (2, depth, LANES), (places, 2, rows, wide), (2, depth, LANES),
              (16, depth, LANES)]
    links = 7 + 3 * places
    return [pltpu.VMEM(s, BF16) for s in shapes] + [pltpu.SemaphoreType.DMA((links,))] * 2 + [pltpu.SemaphoreType.DMA((3,))]


def greet_all(n):
    group, place, core, lane, x, y = spot()
    barrier = pltpu.get_barrier_semaphore()
    partners = [(group + 1 - 2 * x, place), (group + 2 - 4 * y, place)]
    partners += [(group, lax.rem(place + s, n)) for s in range(1, n)]
    for near, far in partners:
        pl.semaphore_signal(barrier, inc=1, device_id={"tm": near, "res": far}, device_id_type=MESH)


def chunk_plan(places, early_rows, late_rows):
    unit = grain(places)
    depth = lambda rows: -(-rows // (16 * unit)) * unit
    total = depth(early_rows)
    size = min(-(-total // (4 * unit)) * unit, (total - unit) // (3 * unit) * unit)
    late = depth(late_rows)
    half = late // 2 // unit * unit
    return [size, size, size, total - 3 * size], [half, late - half]


def pack(bufs, row, value):
    start = 0
    value = value.astype(BF16)
    for buf in bufs:
        size = buf.shape[0] * buf.shape[1]
        depth = buf.shape[1]
        low, high = max(row, start), min(row + value.shape[0], start + size)
        while low < high:
            slot, inner = divmod(low - start, depth)
            step = min(high - low, depth - inner)
            buf[slot, inner : inner + step, : value.shape[1]] = value[low - row : low - row + step]
            low += step
        start += size


def fill(bufs, row, values):
    for value in values:
        pack(bufs, row, value)
        row += value.shape[0]
    spare = sum(b.shape[0] * b.shape[1] for b in bufs) - row
    if spare:
        pack(bufs, row, jnp.zeros((spare, bufs[0].shape[2]), F32))


def unpack(bufs, row, count, width):
    pieces = []
    start = 0
    for buf in bufs:
        depth = buf.shape[1]
        size = buf.shape[0] * depth
        low, high = max(row, start), min(row + count, start + size)
        while low < high:
            slot, inner = divmod(low - start, depth)
            step = min(high - low, depth - inner)
            pieces.append((buf[slot, inner : inner + step, : width], low - row))
            low += step
        start += size
    return pieces


def ring_place(n):
    me = lax.axis_index("res")
    return me, [lax.rem(me + s, n) for s in range(n)]


def greet_start(peers):
    barrier = pltpu.get_barrier_semaphore()
    for peer in peers[1:]:
        pl.semaphore_signal(barrier, inc=1, device_id={"res": peer}, device_id_type=MESH)


def greet_end(peers):
    pl.semaphore_wait(pltpu.get_barrier_semaphore(), len(peers) - 1)


def copy_to(peer, source, target, send, recv):
    return pltpu.make_async_remote_copy(
        src_ref=source, dst_ref=target, send_sem=send, recv_sem=recv, device_id={"res": peer}, device_id_type=MESH
    )


def swap(n, me, peers, source, target, send, recv, placed=False):
    view = lambda s: source.at[peers[s] if placed else s]
    sent = [copy_to(peers[s], view(s), target.at[me], send.at[s], recv.at[me]) for s in range(1, n)]
    back = [copy_to(peers[s], view(s), target.at[peers[s]], send.at[s], recv.at[peers[s]]) for s in range(1, n)]
    return sent, back


def row_norm(values):
    values = values - jnp.mean(values, axis=1, keepdims=True)
    r = lax.rsqrt(jnp.mean(values * values, axis=1, keepdims=True) + EPSILON)
    return values * r, r


def row_norm_back(dh, h, r):
    return r * (dh - jnp.mean(dh, axis=1, keepdims=True) - h * jnp.mean(dh * h, axis=1, keepdims=True))


def table_rows_body(n, fetch_ref, x_ref, chain_ref, flag_ref, win_ref, mid_ref, umid_ref, uout_ref, uin_ref, gain_ref, off_ref,
                    lhs_ref, self_ref, midt_ref, umidt_ref, uoutt_ref, uedge_ref, sel_ref, tag_ref, gaint_ref, offt_ref, far_ref,
                    idx_out, idx_in, row_out, far, wants, asked, send_a, recv_a, send_b, recv_b):
    me, peers = ring_place(n)
    greet_start(peers)
    rows, feat = x_ref.shape
    cap = fetch_ref.shape[1]
    edge_w = win_ref.shape[0] - 2 * feat
    tag = chain_ref[...].reshape(1, rows) * 2 + flag_ref[...].reshape(1, rows)
    tag_ref[...] = tag
    for s in range(n):
        idx_out[s] = jnp.full((8, 128), -1, jnp.int32)
        idx_out[s, 0:1, 0:cap] = fetch_ref[pl.ds(peers[s], 1), :]
        idx_out[s, 1:2, 0:rows] = tag
    greet_end(peers)
    sent, back = swap(n, me, peers, idx_out, idx_in, send_a, recv_a)
    for copy in sent:
        copy.start()
    idx_in[me] = idx_out[0]
    x = x_ref[...]
    for p in range(n):
        wants[0:1, p * cap : (p + 1) * cap] = fetch_ref[p : p + 1, :]
    self_ref[...] = jnp.transpose(nn(x, win_ref[:feat, :]))

    copies, backs = swap(n, me, peers, row_out, far, send_b, recv_b, True)
    for copy in back:
        copy.wait_recv()
    for p in range(n):
        asked[0:1, p * cap : (p + 1) * cap] = idx_in[p, 0:1, 0:cap]
    spots = lax.broadcasted_iota(jnp.int32, (rows, n * cap), 0)
    hot = jnp.where(spots + me * rows == asked[...], 1.0, 0.0).astype(BF16)
    row_out[...] = tn(hot, x).astype(BF16).reshape(n, cap, feat)
    for copy in copies:
        copy.start()
    sel_ref[...] = hot
    far[me] = row_out[me]
    midt_ref[...] = jnp.transpose(mid_ref[...])
    umidt_ref[...] = jnp.transpose(umid_ref[...])
    uoutt_ref[...] = jnp.transpose(uout_ref[...])
    uedge_ref[...] = jnp.transpose(uin_ref[:, 2 * feat :])
    for source, target in ((gain_ref, gaint_ref), (off_ref, offt_ref)):
        target[...] = jnp.transpose(jnp.broadcast_to(source[...].astype(F32).reshape(1, edge_w), (rows, edge_w)))
    neigh = win_ref[feat : 2 * feat, :]
    extra = lhs_ref.shape[0] - feat
    table_len = rows + n * cap
    lhs_ref[feat:, table_len:] = jnp.zeros((extra, edge_w), BF16)
    lhs_ref[:feat, table_len:] = jnp.transpose(win_ref[2 * feat :, :])
    lhs_ref[:feat, :rows] = jnp.transpose(nn(x, neigh)).astype(BF16)
    lhs_ref[feat:, :rows] = jnp.broadcast_to(tag.astype(F32), (extra, rows)).astype(BF16)
    tags = jnp.concatenate([idx_in[p, 1:2, 0:rows] for p in range(n)] + [jnp.zeros((-n % 16, rows), jnp.int32)] * (n % 16 > 0), axis=0)
    want = wants[...]
    picked = nn(tags.astype(F32).astype(BF16), jnp.where(spots == lax.rem(want, rows), 1.0, 0.0).astype(BF16))
    owner = lax.broadcasted_iota(jnp.int32, picked.shape, 0) == want // rows
    far_tag = jnp.sum(jnp.where(owner, picked, 0.0), axis=0, keepdims=True)
    lhs_ref[feat:, rows:table_len] = jnp.broadcast_to(far_tag, (extra, n * cap)).astype(BF16)
    for copy in backs:
        copy.wait_recv()
    got = far[...].reshape(n * cap, feat)
    lhs_ref[:feat, rows:table_len] = jnp.transpose(nn(got, neigh)).astype(BF16)
    far_ref[...] = got
    for copy in sent + copies:
        copy.wait_send()


def far_off(*arrays):
    return [pltpu.with_memory_space_constraint(a, pltpu.HBM) for a in arrays]


def vmem_call(body, args, outs, scratch, collective, name, outside=()):
    whole = pl.BlockSpec(memory_space=pltpu.VMEM)
    return pl.pallas_call(
        body,
        out_shape=[pltpu.HBM(s, d) if i in outside else jax.ShapeDtypeStruct(s, d) for i, (s, d) in enumerate(outs)],
        in_specs=[whole] * len(args),
        out_specs=[whole] * len(outs),
        scratch_shapes=scratch,
        compiler_params=pltpu.CompilerParams(vmem_limit_bytes=30 * 1024 * 1024, collective_id=collective, has_side_effects=True),
        name=name,
    )(*args)


def table_rows(n, fetch, x, chain, flag, win, mid, umid, uout, uin, gain, off):
    rows, feat = x.shape
    cap = fetch.shape[1]
    edge_w = win.shape[0] - 2 * feat
    table_len = rows + n * cap
    outs = [((feat + 16, table_len + edge_w), BF16), ((feat, rows), F32), (mid.shape, BF16), (umid.shape, BF16), (uout.shape, BF16),
            ((edge_w, edge_w), BF16), ((rows, n * cap), BF16), ((1, rows), jnp.int32), ((edge_w, rows), F32), ((edge_w, rows), F32),
            ((n * cap, feat), BF16)]
    sems = [pltpu.SemaphoreType.DMA((n,))] * 4
    scratch = [pltpu.VMEM((n, 8, 128), jnp.int32)] * 2 + [pltpu.VMEM((n, cap, feat), BF16)] * 2 + [pltpu.VMEM((1, n * cap), jnp.int32)] * 2
    return vmem_call(functools.partial(table_rows_body, n), far_off(fetch, x, chain, flag, win, mid, umid, uout, uin, gain, off), outs,
                     scratch + sems, 0, "table_rows", (10,))


def node_forward_body(n, s_ref, cnt_ref, x_ref, mout_ref, gain_ref, off_ref, exp_ref, con_ref, gain2_ref, off2_ref, sel_ref, uin_ref,
                      node_ref, lhs_ref, self_ref, h1_ref, r1_ref, h2_ref, r2_ref, acted_ref, slope_ref,
                      row_out, far, send_a, recv_a):
    me, peers = ring_place(n)
    greet_start(peers)
    rows, feat = x_ref.shape
    cap = sel_ref.shape[1] // n
    edge_w = uin_ref.shape[0]
    line = lambda ref: ref[...].astype(F32).reshape(1, feat)
    mean = jnp.transpose(s_ref[...] / jnp.maximum(cnt_ref[...], 1.0))
    upper = mean.astype(BF16)
    lower = (mean - upper.astype(F32)).astype(BF16)
    aggregate = nn(upper, mout_ref[...]) + nn(lower, mout_ref[...])
    h, r = row_norm(x_ref[...].astype(F32) + aggregate)
    h1_ref[...] = h
    r1_ref[...] = r
    first = h * line(gain_ref) + line(off_ref)
    hidden, slope = gelu_parts(nn(first.astype(BF16), exp_ref[...]))
    acted = hidden.astype(BF16)
    acted_ref[...] = acted
    slope_ref[...] = slope
    h, r = row_norm(first + nn(acted, con_ref[...]))
    h2_ref[...] = h
    r2_ref[...] = r
    low = (h * line(gain2_ref) + line(off2_ref)).astype(BF16)
    node_ref[...] = low
    neigh = nt(low, uin_ref[:, feat : 2 * feat])
    packed = neigh.astype(BF16)
    greet_end(peers)
    copies, backs = swap(n, me, peers, row_out, far, send_a, recv_a, True)
    row_out[...] = tn(sel_ref[...], packed).astype(BF16).reshape(n, cap, edge_w)
    for copy in copies:
        copy.start()
    far[me] = row_out[me]
    self_ref[...] = nt(uin_ref[:, :feat], low)
    table_len = rows + n * cap
    lhs_ref[:, :rows] = jnp.transpose(neigh).astype(BF16)
    lhs_ref[:, table_len:] = uin_ref[:, 2 * feat :]
    for copy in backs:
        copy.wait_recv()
    lhs_ref[:, rows:table_len] = jnp.transpose(far[...].reshape(n * cap, edge_w))
    for copy in copies:
        copy.wait_send()


def node_forward(n, s, cnt, x, mout, gain, off, expand, contract, gain2, off2, sel, uin):
    rows, feat = x.shape
    cap = sel.shape[1] // n
    edge_w = uin.shape[0]
    table_len = rows + n * cap
    hidden = expand.shape[1]
    outs = [(x.shape, BF16), ((edge_w, table_len + edge_w), BF16), ((edge_w, rows), F32), (x.shape, F32), ((rows, 1), F32),
            (x.shape, F32), ((rows, 1), F32), ((rows, hidden), BF16), ((rows, hidden), F32)]
    scratch = [pltpu.VMEM((n, cap, edge_w), BF16)] * 2 + [pltpu.SemaphoreType.DMA((n,))] * 2
    return vmem_call(functools.partial(node_forward_body, n),
                     [s, cnt] + far_off(x, mout, gain, off) + [expand, contract] + far_off(gain2, off2) + [sel, uin], outs, scratch, 1,
                     "node_forward")


def swap_back_start(n, me, peers, gin, sel_ref, row_out, far, send, recv, rows):
    cap = sel_ref.shape[1] // n
    copies, backs = swap(n, me, peers, row_out, far, send, recv, True)
    row_out[...] = gin[pl.ds(rows, n * cap), :].astype(BF16).reshape(n, cap, gin.shape[1])
    for copy in copies:
        copy.start()
    far[me] = row_out[me]
    return copies, backs


def swap_back_finish(n, copies, gin, sel_ref, far, rows):
    for copy in copies[1]:
        copy.wait_recv()
    total = gin[:rows, :] + nn(sel_ref[...], far[...].reshape(sel_ref.shape[1], gin.shape[1]))
    for copy in copies[0]:
        copy.wait_send()
    return total.astype(BF16)


def node_backward_body(n, gin_ref, dself_ref, sel_ref, node_ref, cot_ref, uin_ref, h1_ref, r1_ref, h2_ref, r2_ref, acted_ref, slope_ref,
                       gain_ref, off_ref, gain2_ref, exp_ref, con_ref, s_ref, cnt_ref, mout_ref, ggain_ref, goff_ref,
                       gumid_ref, guout_ref, dfirst_ref, d2_ref, *rest):
    chunks, (row_out, far, send_a, recv_a) = rest[:-4], rest[-4:]
    me, peers = ring_place(n)
    rows, feat = node_ref.shape
    edge_w = uin_ref.shape[0]
    greet_start(peers)
    line = lambda ref: ref[...].astype(F32).reshape(1, feat)
    table_len = gin_ref.shape[0] - edge_w
    dself_t = dself_ref[...].astype(BF16)
    dself = jnp.transpose(dself_ref[...]).astype(BF16)
    greet_end(peers)
    copies = swap_back_start(n, me, peers, gin_ref, sel_ref, row_out, far, send_a, recv_a, rows)
    node = node_ref[...]
    at = early_rows(feat, acted_ref.shape[1], edge_w)
    pack(chunks, at["update_self"], nn(dself_t, node))
    gap = jnp.zeros((edge_w, 256 - edge_w), F32)
    pack(chunks, at["update_edge"], jnp.concatenate([jnp.transpose(gin_ref[table_len:, :]), gap, gumid_ref[...], gap], axis=1))
    pack(chunks, at["update_out"], jnp.concatenate([guout_ref[...], jnp.zeros((edge_w, feat - edge_w), F32)], axis=1))
    side = jnp.zeros((1, feat - edge_w), F32)
    edge_sums = [jnp.concatenate([jnp.sum(jnp.transpose(ref[...]), axis=0, keepdims=True), side], axis=1) for ref in (ggain_ref, goff_ref)]
    used = at["end"]
    spare = sum(c.shape[0] * c.shape[1] for c in chunks) - used
    if spare:
        pack(chunks, used, jnp.zeros((spare, feat), F32))
    dy = cot_ref[...].astype(F32) + nn(dself, uin_ref[:, :feat])
    own = swap_back_finish(n, copies, gin_ref, sel_ref, far, rows)
    dy = dy + nn(own, uin_ref[:, feat : 2 * feat])
    pack(chunks, at["update_neigh"], tn(own, node))
    h2 = h2_ref[...]
    ffn_sums = [jnp.sum(dy * h2, axis=0, keepdims=True), jnp.sum(dy, axis=0, keepdims=True)]
    second = row_norm_back(dy * line(gain2_ref), h2, r2_ref[...])
    dffn = second.astype(BF16)
    for b in range(acted_ref.shape[1] // feat):
        pack(chunks, at["contract"] + b * feat, tn(acted_ref[:, b * feat : (b + 1) * feat], dffn))
    dinner = (nt(dffn, con_ref[...]) * slope_ref[...]).astype(BF16)
    h1 = h1_ref[...]
    gain = line(gain_ref)
    first_low = (h1 * gain + line(off_ref)).astype(BF16)
    for b in range(acted_ref.shape[1] // feat):
        pack(chunks, at["expand"] + b * feat, tn(first_low, dinner[:, b * feat : (b + 1) * feat]))
    dy = second + nt(dinner, exp_ref[...])
    sums = [jnp.sum(dy * h1, axis=0, keepdims=True), jnp.sum(dy, axis=0, keepdims=True)] + ffn_sums
    dfirst = row_norm_back(dy * gain, h1, r1_ref[...])
    dfirst_ref[...] = dfirst
    back = (jnp.transpose(dfirst) / jnp.maximum(cnt_ref[...], 1.0)).astype(BF16)
    d2_ref[...] = nn(mout_ref[...], back)
    pack(chunks, at["message_out"], nt(s_ref[...].astype(BF16), back))
    pack(chunks, at["vectors"], jnp.concatenate(sums + edge_sums + [jnp.zeros((10, feat), F32)], axis=0))


def early_rows(feat, hidden, edge_w):
    at, row = {}, 0
    for name, count in (("contract", hidden), ("expand", hidden), ("message_out", feat), ("update_self", edge_w),
                        ("update_neigh", edge_w), ("update_edge", edge_w), ("update_out", edge_w), ("vectors", 16)):
        at[name] = row
        row += count
    at["end"] = row
    return at


def node_backward(n, gin, dself, sel, node, cot, uin, h1, r1, h2, r2, acted, slope, gain, off, gain2, expand, contract, s, cnt, mout,
                  ggain, goff, gumid, guout, depths):
    rows, feat = node.shape
    cap = sel.shape[1] // n
    edge_w = uin.shape[0]
    outs = [(node.shape, F32), ((feat, rows), F32)] + [((16, d, LANES), BF16) for d in depths]
    scratch = [pltpu.VMEM((n, cap, edge_w), BF16)] * 2 + [pltpu.SemaphoreType.DMA((n,))] * 2
    return vmem_call(functools.partial(node_backward_body, n),
                     [gin, dself, sel, node] + far_off(cot) + [uin, h1, r1, h2, r2, acted, slope] + far_off(gain, off, gain2)
                     + [expand, contract, s, cnt] + far_off(mout) + [ggain, goff, gumid, guout], outs, scratch, 2, "node_backward",
                     (0, 1))


EARLY_ORDER = (
    ((0, 0),),
    ((3, 0), (0, 1)),
    (),
    ((2, 0), (3, 1), (1, 0)),
    ((0, 2), (1, 1)),
    ((3, 2),),
    ((0, 3), (2, 1)),
    (),
    ((3, 3), (1, 2)),
    ((0, 4),),
    ((2, 2),),
    (),
)
LATE_ORDER = (
    (1, 3), (5, 0), (0, 5), (2, 3), (5, 1), (3, 4), (4, 0), (4, 1), (5, 2), (1, 4), (0, 6), (3, 5), (4, 2), (2, 4), (1, 5),
    (5, 3), (3, 6), (2, 5), (4, 3), (5, 4), (1, 6), (2, 6), (4, 4), (5, 5), (0, 7), (3, 7), (0, 8), (4, 5), (1, 7), (5, 6),
    (2, 7), (4, 6), (-1, 0), (3, 8), (2, 8), (0, 9), (5, 7), (3, 9), (4, 7), (1, 8), (2, 9), (5, 8), (4, 8), (5, 9), (1, 9),
    (4, 9),
)


def message_backward_body(n, table_len, slabs, early, late, *refs):
    (e_ref, h1_ref, gp1_ref, gp2_ref, part_ref, keep_ref, nbr_ref, d2_ref, mid_ref, win_ref, x_ref, far_ref, dfirst_ref, sel_ref) = refs[:14]
    refs = refs[14:]
    sources, refs = refs[:early], refs[early:]
    egrad_ref, grad_ref, results, refs = refs[0], refs[1], refs[2 : 2 + early + late], refs[2 + early + late :]
    (gmid, gin, dself_sum, row_out, far, send_a, recv_a), refs = refs[:7], refs[7:]
    late_sources, refs = refs[:late], refs[late:]
    places = n // 2
    chunks = [Chunk(places, (list(sources) + list(late_sources))[i], results[i], *refs[CHUNK_REFS * i : CHUNK_REFS * (i + 1)])
              for i in range(early + late)]
    step = pl.program_id(0)
    base = step * slabs
    steps = pl.num_programs(0)
    rows = nbr_ref.shape[1]
    feat = d2_ref.shape[0]

    @pl.when(step == 0)
    def _():
        greet_all(n)
        for ref in (gmid, gin, dself_sum):
            ref[...] = jnp.zeros_like(ref)

    count = nbr_ref.shape[0] // slabs
    def slot(half):
        for at in range(count):
            which = EARLY_ORDER[2 * at + half]
            if which:

                @pl.when(step == at)
                def _(which=which):
                    for i, stage in which:
                        chunks[i].run(stage)

    x = edge_operand(table_len, slabs, base, e_ref, nbr_ref)
    back = d2_ref[...]
    wide = lambda ref: jnp.concatenate([ref[j] for j in range(slabs)], axis=1)
    two = jnp.concatenate([(back * keep_ref[j] * gp2_ref[j].astype(F32)).astype(BF16) for j in range(slabs)], axis=1)
    gmid[...] += nt(wide(h1_ref), two)

    @pl.when(step == 0)
    def _():
        pl.semaphore_wait(pltpu.get_barrier_semaphore(), n + 1)

    slot(0)
    one = (nn(mid_ref[...], two) * wide(gp1_ref).astype(F32)).astype(BF16)
    gin[...] += nt(x, one)
    part = nn(win_ref[2 * feat :, :], one)
    total = dself_sum[...]
    for j in range(slabs):
        cut = slice(j * rows, (j + 1) * rows)
        egrad_ref[j] = (part_ref[j] + part[:, cut]).astype(BF16)
        total = total + one[:, cut].astype(F32)
    dself_sum[...] = total
    slot(1)

    @pl.when(step == steps - 1)
    def _():
        nodes = x_ref[...]
        dself = jnp.transpose(dself_sum[...]).astype(BF16)
        near = gin[:rows, :].astype(BF16)
        beyond = gin[rows:table_len, :].astype(BF16)
        fill(late_sources, 0, [gmid[...], gin[table_len:, :], tn(nodes, dself), tn(nodes, near) + tn(far_ref[...], beyond)])
        me, peers = ring_place(n)
        copies = swap_back_start(n, me, peers, gin, sel_ref, row_out, far, send_a, recv_a, rows)
        for i, stage in LATE_ORDER:
            if i < 0:
                own = swap_back_finish(n, copies, gin, sel_ref, far, rows)
                grad_ref[...] = dfirst_ref[...] + nt(dself, win_ref[:feat, :]) + nt(own, win_ref[feat : 2 * feat, :])
            else:
                chunks[i].run(stage)


def message_backward(n, e, h1, gp1, gp2, part, keep, nbr, d2, mid, win, x, far_x, dfirst, sel, sources, late_depths, table_len, slabs):
    fan, edge_w, rows = e.shape
    feat = d2.shape[0]
    cap = sel.shape[1] // n
    places = n // 2
    whole = lambda a: pl.BlockSpec(a.shape, lambda i: (0,) * a.ndim)
    slab = lambda f: pl.BlockSpec((slabs, f, rows), lambda i: (i, 0, 0))
    anywhere = pl.BlockSpec(memory_space=pl.ANY)
    consts = (nbr, d2, mid, win, x, far_x, dfirst, sel)
    roomy = table_len <= 512
    place = pltpu.VMEM if roomy else pltpu.HBM
    sources = [pltpu.with_memory_space_constraint(c, place) for c in sources]
    depths = [s.shape[1] for s in sources] + list(late_depths)
    scratch = [pltpu.VMEM((feat, feat), F32), pltpu.VMEM((table_len + edge_w, feat), F32), pltpu.VMEM((feat, rows), F32)]
    scratch += [pltpu.VMEM((n, cap, feat), BF16)] * 2 + [pltpu.SemaphoreType.DMA((n,))] * 2
    scratch += [pltpu.VMEM((16, d, LANES), BF16) for d in late_depths]
    for d in depths:
        scratch += chunk_scratch(places, d)
    return pl.pallas_call(
        functools.partial(message_backward_body, n, table_len, slabs, len(sources), len(late_depths)),
        grid=(fan // slabs,),
        in_specs=[slab(edge_w), slab(feat), slab(feat), slab(feat), slab(edge_w), slab(1)] + [whole(a) for a in consts]
        + [anywhere] * len(sources),
        out_specs=[slab(edge_w), whole(x)] + [anywhere] * len(depths),
        out_shape=[pltpu.HBM(e.shape, BF16), pltpu.HBM(x.shape, F32)]
        + [place((16, d, LANES), BF16) for d in depths],
        scratch_shapes=scratch,
        compiler_params=pltpu.CompilerParams(vmem_limit_bytes=(42 if roomy else 58) * 1024 * 1024, collective_id=3, has_side_effects=True),
        name="message_backward",
    )(e, h1, gp1, gp2, part, keep, *consts, *sources)


def unpack_body(early, late, feat, hidden, edge_w, *refs):
    count = early + late
    sources, refs = refs[:count], refs[count:]
    (egrad, grad, node), refs = refs[:3], refs[3:]
    (gwin, gmid, gmout, gexp, gcon, guin, egrad_out, grad_out, node_out, gumid, guout), refs = refs[:11], refs[11:]
    vectors_out, refs = refs[:6], refs[6:]
    held = sources
    (swin, smid, smout, sexp, scon, suin, segrad, narrow), load, send = refs[:8], refs[8], refs[9]
    slab = narrow.shape[0] // 4
    edges = [pltpu.make_async_copy(egrad.at[pl.ds(b * slab, slab)], narrow.at[pl.ds(b * slab, slab)], load.at[b]) for b in range(4)]
    for copy in edges:
        copy.start()
    at = early_rows(feat, hidden, edge_w)
    sent = []

    def push(source, target):
        copy = pltpu.make_async_copy(source, target, send.at[len(sent)])
        copy.start()
        sent.append(copy)

    push(grad, grad_out)
    push(node, node_out)

    def section(bufs, row, size, width, target, top=0, left=0, lane=0):
        for value, offset in unpack(bufs, row, size, LANES):
            target[top + offset : top + offset + value.shape[0], left : left + width] = value[:, lane : lane + width].astype(F32)

    for b in range(4):
        edges[b].wait()
        for k in range(b * slab, (b + 1) * slab):
            segrad[k] = narrow[k].astype(F32)
        push(segrad.at[pl.ds(b * slab, slab)], egrad_out.at[pl.ds(b * slab, slab)])
    front, back = held[:early], held[early:]
    for b in range(hidden // feat):
        section(front, at["contract"] + b * feat, feat, feat, scon, top=b * feat)
        push(scon.at[pl.ds(b * feat, feat)], gcon.at[pl.ds(b * feat, feat)])
    for b in range(hidden // feat):
        section(front, at["expand"] + b * feat, feat, feat, sexp, left=b * feat)
        push(sexp.at[:, pl.ds(b * feat, feat)], gexp.at[:, pl.ds(b * feat, feat)])
    section(front, at["message_out"], feat, feat, smout)
    push(smout, gmout)
    section(front, at["update_self"], edge_w, feat, suin)
    section(front, at["update_neigh"], edge_w, feat, suin, left=feat)
    section(front, at["update_edge"], edge_w, edge_w, suin, left=2 * feat)
    push(suin, guin)
    section(front, at["update_edge"], edge_w, edge_w, gumid, lane=256)
    section(front, at["update_out"], edge_w, edge_w, guout)
    vectors = unpack(front, at["vectors"], 16, LANES)[0][0].astype(F32)
    for k in range(6):
        size = vectors_out[k].shape[0]
        vectors_out[k][...] = vectors[k : k + 1, :size].reshape(size)
    section(back, 0, feat, feat, smid)
    push(smid, gmid)
    section(back, feat, edge_w, feat, swin, top=2 * feat)
    section(back, feat + edge_w, 2 * feat, feat, swin)
    push(swin, gwin)
    for copy in sent:
        copy.wait()


def unpack_all(chunks, egrad, grad, node, early, feat, hidden, edge_w):
    whole, anywhere = pl.BlockSpec(memory_space=pltpu.VMEM), pl.BlockSpec(memory_space=pl.ANY)
    big = [(2 * feat + edge_w, feat), (feat, feat), (feat, feat), (feat, hidden), (hidden, feat), (edge_w, 2 * feat + edge_w), egrad.shape]
    small = [(edge_w, edge_w), (edge_w, edge_w), (feat,), (feat,), (feat,), (feat,), (edge_w,), (edge_w,)]
    shapes = [jax.ShapeDtypeStruct(s, F32) for s in big] + [jax.ShapeDtypeStruct(grad.shape, F32), jax.ShapeDtypeStruct(node.shape, BF16)]
    return pl.pallas_call(
        functools.partial(unpack_body, early, len(chunks) - early, feat, hidden, edge_w),
        in_specs=[whole] * len(chunks) + [anywhere] * 3,
        out_specs=[anywhere] * 9 + [whole] * 8,
        out_shape=shapes + [jax.ShapeDtypeStruct(s, F32) for s in small],
        scratch_shapes=[pltpu.VMEM(s, F32) for s in big]
        + [pltpu.VMEM(egrad.shape, BF16), pltpu.SemaphoreType.DMA((4,)), pltpu.SemaphoreType.DMA((24,))],
        compiler_params=pltpu.CompilerParams(vmem_limit_bytes=46 * 1024 * 1024),
        name="unpack_all",
    )(*chunks, *far_off(egrad, grad, node))


def local(n, node_feats, edge_feats, node_cotan, edge_cotan, neighbour, edge_mask, fetch_rows, chain_ids, complex_flag, message_in,
          message_mid, message_out, gain_node, offset_node, expand_weight, contract_weight, gain_ffn, offset_ffn, update_in, update_mid,
          update_out, gain_edge, offset_edge):
    x = node_feats[0]
    rows, feat = x.shape
    fan = neighbour.shape[1]
    edge_w = edge_feats.shape[3]
    e = jnp.transpose(edge_feats[0], (1, 2, 0))
    cot = jnp.transpose(edge_cotan[0], (1, 2, 0))
    nbr = jnp.transpose(neighbour)
    mask = jnp.transpose(edge_mask)
    uin = jnp.transpose(update_in)
    lhs, self_t, mid_t, umid_t, uout_t, uedge, sel, tag, gain_t, offset_t, far_x = table_rows(
        n, fetch_rows[0], x, chain_ids, complex_flag, message_in, message_mid, update_mid, update_out, uin, gain_edge, offset_edge
    )
    table_len = lhs.shape[1] - edge_w
    slabs = next(c for c in (10, 6, 4, 2, 1) if fan % c == 0)
    h1, gp1, gp2, s, keep, cnt = message_forward(e, nbr, mask, tag, lhs, self_t, mid_t, slabs)
    node, lhs3, self3, n1, r1, n2, r2, acted, slope = node_forward(
        n, s, cnt, x, message_out, gain_node, offset_node, expand_weight, contract_weight, gain_ffn, offset_ffn,
        sel, uin
    )
    edge_new, part, guout, gumid, gin3, dself3, ggain, goff = edge_pass(
        e, cot, nbr, lhs3, self3, umid_t, uout_t, update_mid, update_out, uedge, gain_t, offset_t, slabs
    )
    hidden = expand_weight.shape[1]
    early_depths, late_depths = chunk_plan(n // 2, early_rows(feat, hidden, edge_w)["end"], 3 * feat + edge_w)
    dfirst, d2, *sources = node_backward(
        n, gin3, dself3, sel, node, node_cotan[0], uin, n1, r1, n2, r2, acted, slope, gain_node, offset_node, gain_ffn,
        expand_weight, contract_weight, s, cnt, message_out, ggain, goff, gumid, guout, early_depths
    )
    egrad, ngrad, *sums = message_backward(
        n, e, h1, gp1, gp2, part, keep, nbr, d2, message_mid, message_in, x, far_x, dfirst, sel, sources, late_depths, table_len, slabs
    )
    gwin, gmid, gmout, gexp, gcon, guin, egrad, ngrad, node, gumid, guout, gnode, onode, gffn, offn, gedge, oedge = unpack_all(
        sums, egrad, ngrad, node, len(sources), feat, hidden, edge_w
    )
    native = lambda a: jnp.transpose(a, (2, 0, 1))[None]
    return (node[None], native(edge_new), ngrad[None], native(egrad), gwin, gmid, gmout, gnode, onode, gexp, gcon, gffn, offn,
            jnp.transpose(guin), gumid, guout, gedge, oedge)


def solution(mesh):
    grouped, placed, copied = P("tm", "res", None), P("res", None), P()
    wide = P("tm", "res", None, None)
    arguments = (grouped, wide, grouped, wide, placed, placed, P("res", None, None), P("res"), P("res")) + (copied,) * 14
    return jax.shard_map(
        functools.partial(local, mesh.shape["res"]),
        mesh=mesh,
        in_specs=arguments,
        out_specs=(grouped, wide, grouped, wide) + (copied,) * 14,
        check_vma=False,
    )
```

```python
import functools
import jax
import jax.numpy as jnp
from jax import lax
from jax.experimental import pallas as pl
from jax.experimental.pallas import tpu as pltpu
from jax.sharding import PartitionSpec as P

EPSILON = 1e-05
CURVE = 0.7978845608028654
CUBIC = 0.044715
F32 = jnp.float32
BF16 = jnp.bfloat16
VMEM_LIMIT = 60 * 1024 * 1024
MESH = pl.DeviceIdType.MESH


def nn(a, b):
    return lax.dot_general(a, b, (((1,), (0,)), ((), ())), preferred_element_type=F32)


def nt(a, b):
    return lax.dot_general(a, b, (((1,), (1,)), ((), ())), preferred_element_type=F32)


def tn(a, b):
    return lax.dot_general(a, b, (((0,), (0,)), ((), ())), preferred_element_type=F32)


def narrow_gelu(v):
    v = v.astype(BF16)
    square = v * v
    t = jnp.tanh(v * (BF16(CURVE) + BF16(CURVE * CUBIC) * square))
    half = BF16(0.5) + BF16(0.5) * t
    slope = half + (half - half * half) * (v * (BF16(2.0 * CURVE) + BF16(6.0 * CURVE * CUBIC) * square))
    return v * half, slope


def gelu_parts(v):
    square = v * v
    t = jnp.tanh(v * (CURVE + (CURVE * CUBIC) * square))
    half = 0.5 + 0.5 * t
    slope = half + (half - half * half) * (v * (2.0 * CURVE + (6.0 * CURVE * CUBIC) * square))
    return v * half, slope


def tile_lanes(block, count):
    return jnp.concatenate([block] * count, axis=1) if count > 1 else block


def edge_operand(table_len, slabs, base, e_ref, nbr_ref):
    columns = []
    for j in range(slabs):
        row = nbr_ref[pl.ds(base + j, 1), :]
        ids = lax.broadcasted_iota(jnp.int32, (table_len, row.shape[1]), 0)
        hot = jnp.where(ids == row, 1.0, 0.0).astype(BF16)
        columns.append(jnp.concatenate([hot, e_ref[j]], axis=0))
    return jnp.concatenate(columns, axis=1) if slabs > 1 else columns[0]


def message_forward_body(table_len, feat, slabs, e_ref, nbr_ref, mask_ref, own_ref, lhs_ref, self_ref, mid_ref,
                         h1_ref, gp1_ref, gp2_ref, s_ref, keep_ref, cnt_ref):
    step = pl.program_id(0)
    base = step * slabs
    rows = nbr_ref.shape[1]

    @pl.when(step == 0)
    def _():
        s_ref[...] = jnp.zeros_like(s_ref)
        cnt_ref[...] = jnp.zeros_like(cnt_ref)

    own = own_ref[...]
    own_chain = own // 2
    own_flag = own % 2
    pre = nn(lhs_ref[...], edge_operand(table_len, slabs, base, e_ref, nbr_ref))
    hidden, slope = narrow_gelu(pre[:feat] + tile_lanes(self_ref[...], slabs))
    total = s_ref[...]
    count = cnt_ref[...]
    keeps = []
    for j in range(slabs):
        cut = slice(j * rows, (j + 1) * rows)
        h1_ref[j] = hidden[:, cut]
        gp1_ref[j] = slope[:, cut]
        other = pre[feat : feat + 1, cut].astype(jnp.int32)
        joined = jnp.logical_or(own_chain == other // 2, own_flag * (other % 2) > 0)
        keep = jnp.where(joined, 1.0, 0.0) * mask_ref[pl.ds(base + j, 1), :].astype(F32)
        keep_ref[j] = keep
        keeps.append(keep)
        count = count + keep
    hidden, slope = narrow_gelu(nn(mid_ref[...], hidden))
    hidden = hidden.astype(F32)
    for j in range(slabs):
        cut = slice(j * rows, (j + 1) * rows)
        gp2_ref[j] = slope[:, cut]
        total = total + hidden[:, cut] * keeps[j]
    s_ref[...] = total
    cnt_ref[...] = count


def message_forward(e, nbr, mask, own_tag, lhs, self_t, mid_t, slabs):
    fan, edge_w, rows = e.shape
    feat = self_t.shape[0]
    table_len = lhs.shape[1] - edge_w
    whole = lambda a: pl.BlockSpec(a.shape, lambda i: (0,) * a.ndim)
    slab = lambda f: pl.BlockSpec((slabs, f, rows), lambda i: (i, 0, 0))
    big = pltpu.HBM((fan, feat, rows), BF16)
    e, nbr, mask = far_off(e, nbr, mask)
    return pl.pallas_call(
        functools.partial(message_forward_body, table_len, feat, slabs),
        grid=(fan // slabs,),
        in_specs=[slab(edge_w), whole(nbr), whole(mask), whole(own_tag), whole(lhs), whole(self_t), whole(mid_t)],
        out_specs=[slab(feat), slab(feat), slab(feat), pl.BlockSpec((feat, rows), lambda i: (0, 0)), slab(1),
                   pl.BlockSpec((1, rows), lambda i: (0, 0))],
        out_shape=[big, big, big, jax.ShapeDtypeStruct((feat, rows), F32), pltpu.HBM((fan, 1, rows), F32),
                   jax.ShapeDtypeStruct((1, rows), F32)],
        compiler_params=pltpu.CompilerParams(vmem_limit_bytes=30 * 1024 * 1024),
        name="message_forward",
    )(e, nbr, mask, own_tag, lhs, self_t, mid_t)


def edge_body(table_len, slabs, e_ref, cot_ref, nbr_ref, lhs_ref, self_ref, mid_t_ref, out_t_ref, mid_ref, out_ref, edge_ref,
              gain_ref, offset_ref,
              new_ref, part_ref, gout_ref, gmid_ref, gin_ref, dself_ref, ggain_ref, goff_ref):
    step = pl.program_id(0)
    base = step * slabs
    rows = nbr_ref.shape[1]

    @pl.when(step == 0)
    def _():
        for ref in (gout_ref, gmid_ref, gin_ref, dself_ref, ggain_ref, goff_ref):
            ref[...] = jnp.zeros_like(ref)

    x = edge_operand(table_len, slabs, base, e_ref, nbr_ref)
    self_t = tile_lanes(self_ref[...], slabs)
    hidden_three, slope_three = narrow_gelu(nn(lhs_ref[...], x) + self_t)
    hidden_four, slope_four = narrow_gelu(nn(mid_t_ref[...], hidden_three))
    branch = nn(out_t_ref[...], hidden_four)
    gain = gain_ref[...]
    offset = offset_ref[...]
    scale = 1.0 / e_ref.shape[1]
    resid = []
    ggain = ggain_ref[...]
    goff = goff_ref[...]
    for j in range(slabs):
        z = e_ref[j].astype(F32) + branch[:, j * rows : (j + 1) * rows]
        z = z - jnp.sum(z, axis=0, keepdims=True) * scale
        r = lax.rsqrt(jnp.sum(z * z, axis=0, keepdims=True) * scale + EPSILON)
        h = z * r
        new_ref[j] = (h * gain + offset).astype(BF16)
        dy = cot_ref[j].astype(F32)
        ggain = ggain + dy * h
        goff = goff + dy
        dh = dy * gain
        one = jnp.sum(dh, axis=0, keepdims=True) * scale
        two = jnp.sum(dh * h, axis=0, keepdims=True) * scale
        resid.append(r * (dh - one - h * two))
    ggain_ref[...] = ggain
    goff_ref[...] = goff
    resid = jnp.concatenate(resid, axis=1) if slabs > 1 else resid[0]
    delta = resid.astype(BF16)
    gout_ref[...] += nt(hidden_four, delta)
    delta_four = (nn(out_ref[...], delta) * slope_four.astype(F32)).astype(BF16)
    gmid_ref[...] += nt(hidden_three, delta_four)
    delta_three = nn(mid_ref[...], delta_four) * slope_three.astype(F32)
    low = delta_three.astype(BF16)
    gin_ref[...] += nt(x, low)
    part = resid + nn(edge_ref[...], low)
    dself = dself_ref[...]
    for j in range(slabs):
        cut = slice(j * rows, (j + 1) * rows)
        part_ref[j] = part[:, cut]
        dself = dself + low[:, cut].astype(F32)
    dself_ref[...] = dself


def edge_pass(e, cot, nbr, lhs, self_t, mid_t, out_t, mid, out, edge, gain, offset, slabs):
    fan, edge_w, rows = e.shape
    table_len = lhs.shape[1] - edge_w
    whole = lambda a: pl.BlockSpec(a.shape, lambda i: (0,) * a.ndim)
    slab = pl.BlockSpec((slabs, edge_w, rows), lambda i: (i, 0, 0))
    keep = lambda *s: (pl.BlockSpec(s, lambda i: (0,) * len(s)), jax.ShapeDtypeStruct(s, F32))
    sums = [keep(edge_w, edge_w), keep(edge_w, edge_w), keep(table_len + edge_w, edge_w), keep(edge_w, rows), keep(edge_w, rows),
            keep(edge_w, rows)]
    e, cot, nbr, mid, out = far_off(e, cot, nbr, mid, out)
    consts = (nbr, lhs, self_t, mid_t, out_t, mid, out, edge, gain, offset)
    return pl.pallas_call(
        functools.partial(edge_body, table_len, slabs),
        grid=(fan // slabs,),
        in_specs=[slab, slab] + [whole(a) for a in consts],
        out_specs=[slab, slab] + [s for s, _ in sums],
        out_shape=[pltpu.HBM(e.shape, BF16), pltpu.HBM(e.shape, F32)] + [s for _, s in sums],
        compiler_params=pltpu.CompilerParams(vmem_limit_bytes=30 * 1024 * 1024),
        name="edge_pass",
    )(e, cot, *consts)


LANES = 512


def spot():
    group, place = lax.axis_index("tm"), lax.axis_index("res")
    return group, place, lax.rem(place, 2), place // 2, lax.rem(group, 2), group // 2


def grain(places):
    return 16 * max(1, places // 4)


def piece(places, depth, index):
    across = min(places, 4)
    rows, wide = piece_shape(places, depth)
    top = pl.multiple_of((index // across) * rows, rows)
    left = pl.multiple_of(lax.rem(index, across) * wide, wide)
    return pl.ds(top, rows), pl.ds(left, wide)


def piece_shape(places, depth):
    across = min(places, 4)
    return depth // (places // across), LANES // across


def remote(source, target, send, recv, group, place):
    return pltpu.make_async_remote_copy(
        src_ref=source, dst_ref=target, send_sem=send, recv_sem=recv, device_id={"tm": group, "res": place}, device_id_type=MESH
    )


class Chunk:
    def __init__(self, places, source, result, acc, from_core, from_first, from_second, from_line, stage, out, sends, recvs, local):
        self.places, self.source, self.result, self.acc = places, source, result, acc
        self.from_core, self.from_first, self.from_second = from_core, from_first, from_second
        self.from_line, self.stage, self.out = from_line, stage, out
        self.sends, self.recvs, self.local = sends, recvs, local
        self.depth = acc.shape[1]

    def run(self, stage):
        (self.spread, self.halve, self.quarter, self.scatter, self.settle, self.gather, self.widen, self.share, self.store,
         self.close)[stage]()

    def link(self, slot, source, target, group, place):
        return functools.partial(remote, source, target, self.sends.at[slot], self.recvs.at[slot], group, place)

    def core_copy(self):
        group, place, core, lane, x, y = spot()
        theirs = pl.multiple_of((1 - core) * 8, 8)
        return self.link(0, self.source.at[pl.ds(theirs, 8)], self.from_core, group, place + 1 - 2 * core)

    def load_copy(self):
        core = spot()[2]
        return pltpu.make_async_copy(self.source.at[pl.ds(pl.multiple_of(core * 8, 8), 8)], self.acc, self.local.at[0])

    def half_copies(self):
        group, place, core, lane, x, y = spot()
        return [
            self.link(1, self.acc.at[pl.ds((1 - x) * 2, 2)], self.from_first.at[pl.ds(0, 2)], group + 1 - 2 * x, place),
            self.link(2, self.acc.at[pl.ds(4 + (1 - y) * 2, 2)], self.from_first.at[pl.ds(2, 2)], group + 2 - 4 * y, place),
        ]

    def quarter_copies(self):
        group, place, core, lane, x, y = spot()
        return [
            self.link(3, self.acc.at[x * 2 + 1 - y], self.from_second.at[0], group + 2 - 4 * y, place),
            self.link(4, self.acc.at[4 + y * 2 + 1 - x], self.from_second.at[1], group + 1 - 2 * x, place),
        ]

    def line_copies(self):
        group, place, core, lane, x, y = spot()
        copies = []
        for s in range(1, self.places):
            ahead, behind = lax.rem(lane + s, self.places), lax.rem(lane + self.places - s, self.places)
            rows, wide = piece(self.places, self.depth, ahead)
            view = self.stage.at[:, rows, wide]
            copies.append((self.link(4 + s, view, self.from_line.at[lane], group, ahead * 2 + core),
                           self.link(4 + s, view, self.from_line.at[behind], group, behind * 2 + core)))
        return copies

    def own(self):
        group, place, core, lane, x, y = spot()
        return core * 8 + x * 2 + y, core * 8 + 4 + y * 2 + x

    def spread_copies(self):
        group, place, core, lane, x, y = spot()
        copies = []
        slot = 4 + self.places
        for own in self.own():
            for s in range(1, self.places):
                ahead, behind = lax.rem(lane + s, self.places), lax.rem(lane + self.places - s, self.places)
                rows, wide = piece(self.places, self.depth, lane)
                back_rows, back_wide = piece(self.places, self.depth, behind)
                view, back = self.out.at[own, rows, wide], self.out.at[own, back_rows, back_wide]
                copies.append((self.link(slot, view, view, group, ahead * 2 + core), self.link(slot, back, back, group, behind * 2 + core)))
                slot += 1
        return copies

    def both(self, slot, view, back, group, place):
        return self.link(slot, view, view, group, place), self.link(slot, back, back, group, place)

    def gather_copies(self):
        group, place, core, lane, x, y = spot()
        slot = 2 + 3 * self.places
        first, second = self.own()
        return [
            self.both(slot, self.out.at[first], self.out.at[core * 8 + x * 2 + 1 - y], group + 2 - 4 * y, place),
            self.both(slot + 1, self.out.at[second], self.out.at[core * 8 + 4 + y * 2 + 1 - x], group + 1 - 2 * x, place),
        ]

    def widen_copies(self):
        group, place, core, lane, x, y = spot()
        slot = 4 + 3 * self.places
        two = lambda start: self.out.at[pl.ds(start, 2)]
        return [
            self.both(slot, two(core * 8 + x * 2), two(core * 8 + 2 - x * 2), group + 1 - 2 * x, place),
            self.both(slot + 1, two(core * 8 + 4 + y * 2), two(core * 8 + 6 - y * 2), group + 2 - 4 * y, place),
        ]

    def share_copy(self):
        group, place, core, lane, x, y = spot()
        eight = lambda which: self.out.at[pl.ds(pl.multiple_of(which * 8, 8), 8)]
        return self.both(6 + 3 * self.places, eight(core), eight(1 - core), group, place + 1 - 2 * core)

    def store_copy(self, which, slot):
        eight = pl.ds(pl.multiple_of(which * 8, 8), 8)
        return pltpu.make_async_copy(self.out.at[eight], self.result.at[eight], self.local.at[slot])

    def spread(self):
        self.core_copy()().start()
        self.load_copy().start()

    def halve(self):
        group, place, core, lane, x, y = spot()
        self.load_copy().wait()
        self.core_copy()().wait()
        acc, extra = self.acc, self.from_core
        give = [(1 - x) * 2, 4 + (1 - y) * 2]
        keep = [x * 2, 4 + y * 2]
        for start in give:
            for i in range(2):
                acc[start + i] = acc[start + i] + extra[start + i]
        for copy in self.half_copies():
            copy().start()
        for start in keep:
            for i in range(2):
                acc[start + i] = acc[start + i] + extra[start + i]

    def quarter(self):
        group, place, core, lane, x, y = spot()
        for copy in self.half_copies():
            copy().wait()
        acc, extra = self.acc, self.from_first
        acc[x * 2 + 1 - y] = acc[x * 2 + 1 - y] + extra[1 - y]
        acc[4 + y * 2 + 1 - x] = acc[4 + y * 2 + 1 - x] + extra[3 - x]
        for copy in self.quarter_copies():
            copy().start()
        self.stage[0] = acc[x * 2 + y] + extra[y]
        self.stage[1] = acc[4 + y * 2 + x] + extra[2 + x]

    def scatter(self):
        for copy in self.quarter_copies():
            copy().wait()
        for s in range(2):
            self.stage[s] = self.stage[s] + self.from_second[s]
        for send, arrive in self.line_copies():
            send().start()

    def settle(self):
        group, place, core, lane, x, y = spot()
        rows, wide = piece(self.places, self.depth, lane)
        total = self.stage[:, rows, wide].astype(F32)
        pairs = self.line_copies()
        for s in range(1, self.places):
            pairs[s - 1][1]().wait_recv()
            total = total + self.from_line[lax.rem(lane + self.places - s, self.places)].astype(F32)
        first, second = self.own()
        total = total.astype(BF16)
        self.out[first, rows, wide] = total[0]
        self.out[second, rows, wide] = total[1]
        for send, arrive in self.spread_copies():
            send().start()
        for send, arrive in pairs:
            send().wait_send()

    def finish(self, pairs):
        for send, arrive in pairs:
            arrive().wait_recv()
        for send, arrive in pairs:
            send().wait_send()

    def gather(self):
        self.finish(self.spread_copies())
        for send, arrive in self.gather_copies():
            send().start()

    def widen(self):
        self.finish(self.gather_copies())
        for send, arrive in self.widen_copies():
            send().start()

    def share(self):
        core = spot()[2]
        self.finish(self.widen_copies())
        self.share_copy()[0]().start()
        self.store_copy(core, 1).start()

    def store(self):
        core = spot()[2]
        self.share_copy()[1]().wait_recv()
        self.store_copy(1 - core, 2).start()

    def close(self):
        core = spot()[2]
        self.share_copy()[0]().wait_send()
        self.store_copy(core, 1).wait()
        self.store_copy(1 - core, 2).wait()


CHUNK_REFS = 10
ROOMY = 512


def chunk_scratch(places, depth):
    rows, wide = piece_shape(places, depth)
    shapes = [(8, depth, LANES), (8, depth, LANES), (4, depth, LANES), (2, depth, LANES), (places, 2, rows, wide), (2, depth, LANES),
              (16, depth, LANES)]
    links = 7 + 3 * places
    return [pltpu.VMEM(s, BF16) for s in shapes] + [pltpu.SemaphoreType.DMA((links,))] * 2 + [pltpu.SemaphoreType.DMA((3,))]


def greet_all(n):
    group, place, core, lane, x, y = spot()
    barrier = pltpu.get_barrier_semaphore()
    partners = [(group + 1 - 2 * x, place), (group + 2 - 4 * y, place)]
    partners += [(group, lax.rem(place + s, n)) for s in range(1, n)]
    for near, far in partners:
        pl.semaphore_signal(barrier, inc=1, device_id={"tm": near, "res": far}, device_id_type=MESH)


def chunk_plan(places, early_rows, late_rows):
    unit = grain(places)
    depth = lambda rows: -(-rows // (16 * unit)) * unit
    total = depth(early_rows)
    steps = total // unit
    late = depth(late_rows)
    half = late // 2 // unit * unit
    return [(steps + k) // 4 * unit for k in range(4)], [half, late - half]


def pack(bufs, row, value):
    start = 0
    value = value.astype(BF16)
    for buf in bufs:
        size = buf.shape[0] * buf.shape[1]
        depth = buf.shape[1]
        low, high = max(row, start), min(row + value.shape[0], start + size)
        while low < high:
            slot, inner = divmod(low - start, depth)
            step = min(high - low, depth - inner)
            buf[slot, inner : inner + step, : value.shape[1]] = value[low - row : low - row + step]
            low += step
        start += size


def fill(bufs, row, values):
    for value in values:
        pack(bufs, row, value)
        row += value.shape[0]
    spare = sum(b.shape[0] * b.shape[1] for b in bufs) - row
    if spare:
        pack(bufs, row, jnp.zeros((spare, bufs[0].shape[2]), F32))


def unpack(bufs, row, count, width):
    pieces = []
    start = 0
    for buf in bufs:
        depth = buf.shape[1]
        size = buf.shape[0] * depth
        low, high = max(row, start), min(row + count, start + size)
        while low < high:
            slot, inner = divmod(low - start, depth)
            step = min(high - low, depth - inner)
            pieces.append((buf[slot, inner : inner + step, : width], low - row))
            low += step
        start += size
    return pieces


def ring_place(n):
    me = lax.axis_index("res")
    return me, [lax.rem(me + s, n) for s in range(n)]


def greet_start(peers):
    barrier = pltpu.get_barrier_semaphore()
    for peer in peers[1:]:
        pl.semaphore_signal(barrier, inc=1, device_id={"res": peer}, device_id_type=MESH)


def greet_end(peers):
    pl.semaphore_wait(pltpu.get_barrier_semaphore(), len(peers) - 1)


def copy_to(peer, source, target, send, recv):
    return pltpu.make_async_remote_copy(
        src_ref=source, dst_ref=target, send_sem=send, recv_sem=recv, device_id={"res": peer}, device_id_type=MESH
    )


def swap(n, me, peers, source, target, send, recv, placed=False):
    view = lambda s: source.at[peers[s] if placed else s]
    sent = [copy_to(peers[s], view(s), target.at[me], send.at[s], recv.at[me]) for s in range(1, n)]
    back = [copy_to(peers[s], view(s), target.at[peers[s]], send.at[s], recv.at[peers[s]]) for s in range(1, n)]
    return sent, back


def row_norm(values):
    values = values - jnp.mean(values, axis=1, keepdims=True)
    r = lax.rsqrt(jnp.mean(values * values, axis=1, keepdims=True) + EPSILON)
    return values * r, r


def row_norm_back(dh, h, r):
    return r * (dh - jnp.mean(dh, axis=1, keepdims=True) - h * jnp.mean(dh * h, axis=1, keepdims=True))


def table_rows_body(n, fetch_ref, x_ref, chain_ref, flag_ref, win_hbm, mid_hbm, umid_hbm, uout_hbm, uin_hbm, gain_ref, off_ref,
                    lhs_ref, self_ref, midt_ref, umidt_ref, uoutt_ref, uedge_ref, sel_ref, tag_ref, gaint_ref, offt_ref, far_ref,
                    idx_out, idx_in, row_out, far, wants, asked, win_ref, mid_ref, umid_ref, uout_ref, uin_ref, send_a, recv_a, send_b, recv_b,
                    load):
    me, peers = ring_place(n)
    greet_start(peers)
    pairs = ((win_hbm, win_ref), (mid_hbm, mid_ref), (umid_hbm, umid_ref), (uout_hbm, uout_ref), (uin_hbm, uin_ref))
    loads = [pltpu.make_async_copy(pairs[k][0], pairs[k][1], load.at[k]) for k in range(5)]
    for copy in loads:
        copy.start()
    rows, feat = x_ref.shape
    cap = fetch_ref.shape[1]
    edge_w = win_ref.shape[0] - 2 * feat
    tag = chain_ref[...].reshape(1, rows) * 2 + flag_ref[...].reshape(1, rows)
    tag_ref[...] = tag
    for s in range(n):
        idx_out[s] = jnp.full((8, 128), -1, jnp.int32)
        idx_out[s, 0:1, 0:cap] = fetch_ref[pl.ds(peers[s], 1), :]
        idx_out[s, 1:2, 0:rows] = tag
    greet_end(peers)
    sent, back = swap(n, me, peers, idx_out, idx_in, send_a, recv_a)
    for copy in sent:
        copy.start()
    idx_in[me] = idx_out[0]
    x = x_ref[...]
    for p in range(n):
        wants[0:1, p * cap : (p + 1) * cap] = fetch_ref[p : p + 1, :]
    loads[0].wait()
    self_ref[...] = jnp.transpose(nn(x, win_ref[:feat, :]))

    copies, backs = swap(n, me, peers, row_out, far, send_b, recv_b, True)
    for copy in back:
        copy.wait_recv()
    for p in range(n):
        asked[0:1, p * cap : (p + 1) * cap] = idx_in[p, 0:1, 0:cap]
    spots = lax.broadcasted_iota(jnp.int32, (rows, n * cap), 0)
    hot = jnp.where(spots + me * rows == asked[...], 1.0, 0.0).astype(BF16)
    row_out[...] = tn(hot, x).astype(BF16).reshape(n, cap, feat)
    for copy in copies:
        copy.start()
    sel_ref[...] = hot
    far[me] = row_out[me]
    for copy in loads[1:]:
        copy.wait()
    midt_ref[...] = jnp.transpose(mid_ref[...])
    umidt_ref[...] = jnp.transpose(umid_ref[...])
    uoutt_ref[...] = jnp.transpose(uout_ref[...])
    uedge_ref[...] = jnp.transpose(uin_ref[:, 2 * feat :])
    for source, target in ((gain_ref, gaint_ref), (off_ref, offt_ref)):
        target[...] = jnp.transpose(jnp.broadcast_to(source[...].astype(F32).reshape(1, edge_w), (rows, edge_w)))
    neigh = win_ref[feat : 2 * feat, :]
    extra = lhs_ref.shape[0] - feat
    table_len = rows + n * cap
    lhs_ref[feat:, table_len:] = jnp.zeros((extra, edge_w), BF16)
    lhs_ref[:feat, table_len:] = jnp.transpose(win_ref[2 * feat :, :])
    lhs_ref[:feat, :rows] = jnp.transpose(nn(x, neigh)).astype(BF16)
    lhs_ref[feat:, :rows] = jnp.broadcast_to(tag.astype(F32), (extra, rows)).astype(BF16)
    tags = jnp.concatenate([idx_in[p, 1:2, 0:rows] for p in range(n)] + [jnp.zeros((-n % 16, rows), jnp.int32)] * (n % 16 > 0), axis=0)
    want = wants[...]
    picked = nn(tags.astype(F32).astype(BF16), jnp.where(spots == lax.rem(want, rows), 1.0, 0.0).astype(BF16))
    owner = lax.broadcasted_iota(jnp.int32, picked.shape, 0) == want // rows
    far_tag = jnp.sum(jnp.where(owner, picked, 0.0), axis=0, keepdims=True)
    lhs_ref[feat:, rows:table_len] = jnp.broadcast_to(far_tag, (extra, n * cap)).astype(BF16)
    for copy in backs:
        copy.wait_recv()
    got = far[...].reshape(n * cap, feat)
    lhs_ref[:feat, rows:table_len] = jnp.transpose(nn(got, neigh)).astype(BF16)
    far_ref[...] = got
    for copy in sent + copies:
        copy.wait_send()


def far_off(*arrays):
    return [pltpu.with_memory_space_constraint(a, pltpu.HBM) for a in arrays]


def vmem_call(body, args, outs, scratch, collective, name, outside=(), raw=()):
    whole = pl.BlockSpec(memory_space=pltpu.VMEM)
    return pl.pallas_call(
        body,
        out_shape=[pltpu.HBM(s, d) if i in outside else jax.ShapeDtypeStruct(s, d) for i, (s, d) in enumerate(outs)],
        in_specs=[pl.BlockSpec(memory_space=pl.ANY) if i in raw else whole for i in range(len(args))],
        out_specs=[whole] * len(outs),
        scratch_shapes=scratch,
        compiler_params=pltpu.CompilerParams(vmem_limit_bytes=30 * 1024 * 1024, collective_id=collective, has_side_effects=True),
        name=name,
    )(*args)


def table_rows(n, fetch, x, chain, flag, win, mid, umid, uout, uin, gain, off):
    rows, feat = x.shape
    cap = fetch.shape[1]
    edge_w = win.shape[0] - 2 * feat
    table_len = rows + n * cap
    outs = [((feat + 16, table_len + edge_w), BF16), ((feat, rows), F32), (mid.shape, BF16), (umid.shape, BF16), (uout.shape, BF16),
            ((edge_w, edge_w), BF16), ((rows, n * cap), BF16), ((1, rows), jnp.int32), ((edge_w, rows), F32), ((edge_w, rows), F32),
            ((n * cap, feat), BF16)]
    sems = [pltpu.SemaphoreType.DMA((n,))] * 4 + [pltpu.SemaphoreType.DMA((5,))]
    scratch = [pltpu.VMEM((n, 8, 128), jnp.int32)] * 2 + [pltpu.VMEM((n, cap, feat), BF16)] * 2 + [pltpu.VMEM((1, n * cap), jnp.int32)] * 2
    scratch += [pltpu.VMEM(w.shape, BF16) for w in (win, mid, umid, uout, uin)]
    return vmem_call(functools.partial(table_rows_body, n), far_off(fetch, x, chain, flag, win, mid, umid, uout, uin, gain, off), outs,
                     scratch + sems, 0, "table_rows", (10,), range(4, 9))


def node_forward_body(n, s_ref, cnt_ref, x_ref, mout_ref, gain_ref, off_ref, exp_ref, con_ref, gain2_ref, off2_ref, sel_ref, uin_ref,
                      node_ref, lhs_ref, self_ref, h1_ref, r1_ref, h2_ref, r2_ref, acted_ref, slope_ref,
                      row_out, far, send_a, recv_a):
    me, peers = ring_place(n)
    greet_start(peers)
    rows, feat = x_ref.shape
    cap = sel_ref.shape[1] // n
    edge_w = uin_ref.shape[0]
    line = lambda ref: ref[...].astype(F32).reshape(1, feat)
    mean = jnp.transpose(s_ref[...] / jnp.maximum(cnt_ref[...], 1.0))
    upper = mean.astype(BF16)
    lower = (mean - upper.astype(F32)).astype(BF16)
    aggregate = nn(upper, mout_ref[...]) + nn(lower, mout_ref[...])
    h, r = row_norm(x_ref[...].astype(F32) + aggregate)
    h1_ref[...] = h
    r1_ref[...] = r
    first = h * line(gain_ref) + line(off_ref)
    hidden, slope = gelu_parts(nn(first.astype(BF16), exp_ref[...]))
    acted = hidden.astype(BF16)
    acted_ref[...] = acted
    slope_ref[...] = slope
    h, r = row_norm(first + nn(acted, con_ref[...]))
    h2_ref[...] = h
    r2_ref[...] = r
    low = (h * line(gain2_ref) + line(off2_ref)).astype(BF16)
    node_ref[...] = low
    neigh = nt(low, uin_ref[:, feat : 2 * feat])
    packed = neigh.astype(BF16)
    greet_end(peers)
    copies, backs = swap(n, me, peers, row_out, far, send_a, recv_a, True)
    row_out[...] = tn(sel_ref[...], packed).astype(BF16).reshape(n, cap, edge_w)
    for copy in copies:
        copy.start()
    far[me] = row_out[me]
    self_ref[...] = nt(uin_ref[:, :feat], low)
    table_len = rows + n * cap
    lhs_ref[:, :rows] = jnp.transpose(neigh).astype(BF16)
    lhs_ref[:, table_len:] = uin_ref[:, 2 * feat :]
    for copy in backs:
        copy.wait_recv()
    lhs_ref[:, rows:table_len] = jnp.transpose(far[...].reshape(n * cap, edge_w))
    for copy in copies:
        copy.wait_send()


def node_forward(n, s, cnt, x, mout, gain, off, expand, contract, gain2, off2, sel, uin):
    rows, feat = x.shape
    cap = sel.shape[1] // n
    edge_w = uin.shape[0]
    table_len = rows + n * cap
    hidden = expand.shape[1]
    outs = [(x.shape, BF16), ((edge_w, table_len + edge_w), BF16), ((edge_w, rows), F32), (x.shape, F32), ((rows, 1), F32),
            (x.shape, F32), ((rows, 1), F32), ((rows, hidden), BF16), ((rows, hidden), F32)]
    scratch = [pltpu.VMEM((n, cap, edge_w), BF16)] * 2 + [pltpu.SemaphoreType.DMA((n,))] * 2
    return vmem_call(functools.partial(node_forward_body, n),
                     [s, cnt] + far_off(x, mout, gain, off) + [expand, contract] + far_off(gain2, off2) + [sel, uin], outs, scratch, 1,
                     "node_forward")


def swap_back_start(n, me, peers, gin, sel_ref, row_out, far, send, recv, rows):
    cap = sel_ref.shape[1] // n
    copies, backs = swap(n, me, peers, row_out, far, send, recv, True)
    row_out[...] = gin[pl.ds(rows, n * cap), :].astype(BF16).reshape(n, cap, gin.shape[1])
    for copy in copies:
        copy.start()
    far[me] = row_out[me]
    return copies, backs


def swap_back_finish(n, copies, gin, sel_ref, far, rows):
    for copy in copies[1]:
        copy.wait_recv()
    total = gin[:rows, :] + nn(sel_ref[...], far[...].reshape(sel_ref.shape[1], gin.shape[1]))
    for copy in copies[0]:
        copy.wait_send()
    return total.astype(BF16)


def node_backward_body(n, gin_ref, dself_ref, sel_ref, node_ref, cot_ref, uin_ref, h1_ref, r1_ref, h2_ref, r2_ref, acted_ref, slope_ref,
                       gain_ref, off_ref, gain2_ref, exp_ref, con_ref, s_ref, cnt_ref, mout_ref, ggain_ref, goff_ref,
                       gumid_ref, guout_ref, dfirst_ref, d2_ref, *rest):
    chunks, (row_out, far, send_a, recv_a) = rest[:-4], rest[-4:]
    me, peers = ring_place(n)
    rows, feat = node_ref.shape
    edge_w = uin_ref.shape[0]
    greet_start(peers)
    line = lambda ref: ref[...].astype(F32).reshape(1, feat)
    table_len = gin_ref.shape[0] - edge_w
    dself_t = dself_ref[...].astype(BF16)
    dself = jnp.transpose(dself_ref[...]).astype(BF16)
    greet_end(peers)
    copies = swap_back_start(n, me, peers, gin_ref, sel_ref, row_out, far, send_a, recv_a, rows)
    node = node_ref[...]
    at = early_rows(feat, acted_ref.shape[1], edge_w)
    pack(chunks, at["update_self"], nn(dself_t, node))
    gap = jnp.zeros((edge_w, 256 - edge_w), F32)
    pack(chunks, at["update_edge"], jnp.concatenate([jnp.transpose(gin_ref[table_len:, :]), gap, gumid_ref[...], gap], axis=1))
    pack(chunks, at["update_out"], jnp.concatenate([guout_ref[...], jnp.zeros((edge_w, feat - edge_w), F32)], axis=1))
    side = jnp.zeros((1, feat - edge_w), F32)
    edge_sums = [jnp.concatenate([jnp.sum(jnp.transpose(ref[...]), axis=0, keepdims=True), side], axis=1) for ref in (ggain_ref, goff_ref)]
    used = at["end"]
    spare = sum(c.shape[0] * c.shape[1] for c in chunks) - used
    if spare:
        pack(chunks, used, jnp.zeros((spare, feat), F32))
    dy = cot_ref[...].astype(F32) + nn(dself, uin_ref[:, :feat])
    own = swap_back_finish(n, copies, gin_ref, sel_ref, far, rows)
    dy = dy + nn(own, uin_ref[:, feat : 2 * feat])
    pack(chunks, at["update_neigh"], tn(own, node))
    h2 = h2_ref[...]
    ffn_sums = [jnp.sum(dy * h2, axis=0, keepdims=True), jnp.sum(dy, axis=0, keepdims=True)]
    second = row_norm_back(dy * line(gain2_ref), h2, r2_ref[...])
    dffn = second.astype(BF16)
    for b in range(acted_ref.shape[1] // feat):
        pack(chunks, at["contract"] + b * feat, tn(acted_ref[:, b * feat : (b + 1) * feat], dffn))
    dinner = (nt(dffn, con_ref[...]) * slope_ref[...]).astype(BF16)
    h1 = h1_ref[...]
    gain = line(gain_ref)
    first_low = (h1 * gain + line(off_ref)).astype(BF16)
    for b in range(acted_ref.shape[1] // feat):
        pack(chunks, at["expand"] + b * feat, tn(first_low, dinner[:, b * feat : (b + 1) * feat]))
    dy = second + nt(dinner, exp_ref[...])
    sums = [jnp.sum(dy * h1, axis=0, keepdims=True), jnp.sum(dy, axis=0, keepdims=True)] + ffn_sums
    dfirst = row_norm_back(dy * gain, h1, r1_ref[...])
    dfirst_ref[...] = dfirst
    back = (jnp.transpose(dfirst) / jnp.maximum(cnt_ref[...], 1.0)).astype(BF16)
    d2_ref[...] = nn(mout_ref[...], back)
    pack(chunks, at["message_out"], nt(s_ref[...].astype(BF16), back))
    pack(chunks, at["vectors"], jnp.concatenate(sums + edge_sums + [jnp.zeros((10, feat), F32)], axis=0))


def early_rows(feat, hidden, edge_w):
    at, row = {}, 0
    for name, count in (("contract", hidden), ("expand", hidden), ("message_out", feat), ("update_self", edge_w),
                        ("update_neigh", edge_w), ("update_edge", edge_w), ("update_out", edge_w), ("vectors", 16)):
        at[name] = row
        row += count
    at["end"] = row
    return at


def node_backward(n, gin, dself, sel, node, cot, uin, h1, r1, h2, r2, acted, slope, gain, off, gain2, expand, contract, s, cnt, mout,
                  ggain, goff, gumid, guout, depths):
    rows, feat = node.shape
    cap = sel.shape[1] // n
    edge_w = uin.shape[0]
    outs = [(node.shape, F32), ((feat, rows), F32)] + [((16, d, LANES), BF16) for d in depths]
    scratch = [pltpu.VMEM((n, cap, edge_w), BF16)] * 2 + [pltpu.SemaphoreType.DMA((n,))] * 2
    return vmem_call(functools.partial(node_backward_body, n),
                     [gin, dself, sel, node] + far_off(cot) + [uin, h1, r1, h2, r2, acted, slope] + far_off(gain, off, gain2)
                     + [expand, contract, s, cnt] + far_off(mout) + [ggain, goff, gumid, guout], outs, scratch, 2, "node_backward",
                     (0, 1))


EARLY_ORDER = (
    ((2, 0),),
    ((1, 0), (2, 1)),
    (),
    ((1, 1), (0, 0)),
    ((2, 2),),
    (),
    ((1, 2), (3, 0), (0, 1), (2, 3)),
    (),
    ((1, 3), (3, 1)),
    ((2, 4),),
    ((0, 2),),
    (),
)
LATE_ORDER = (
    (1, 4), (3, 2), (5, 0), (0, 3), (2, 5), (5, 1), (4, 0), (3, 3), (4, 1), (1, 5), (0, 4), (2, 6), (5, 2), (3, 4), (4, 2),
    (1, 6), (5, 3), (0, 5), (4, 3), (3, 5), (5, 4), (2, 7), (0, 6), (2, 8), (1, 7), (3, 6), (4, 4), (5, 5), (4, 5), (0, 7),
    (5, 6), (-1, 0), (0, 8), (3, 7), (4, 6), (3, 8), (1, 8), (5, 7), (1, 9), (4, 7), (0, 9), (5, 8), (2, 9), (4, 8), (5, 9),
    (3, 9), (4, 9),
)


def message_backward_body(n, table_len, slabs, early, late, *refs):
    (e_ref, h1_ref, gp1_ref, gp2_ref, part_ref, keep_ref, nbr_ref, d2_ref, mid_ref, win_ref, x_ref, far_ref, dfirst_ref, sel_ref) = refs[:14]
    refs = refs[14:]
    sources, refs = refs[:early], refs[early:]
    egrad_ref, grad_ref, results, refs = refs[0], refs[1], refs[2 : 2 + early + late], refs[2 + early + late :]
    (gmid, gin, dself_sum, row_out, far, send_a, recv_a), refs = refs[:7], refs[7:]
    late_sources, refs = refs[:late], refs[late:]
    places = n // 2
    chunks = [Chunk(places, (list(sources) + list(late_sources))[i], results[i], *refs[CHUNK_REFS * i : CHUNK_REFS * (i + 1)])
              for i in range(early + late)]
    step = pl.program_id(0)
    base = step * slabs
    steps = pl.num_programs(0)
    rows = nbr_ref.shape[1]
    feat = d2_ref.shape[0]

    @pl.when(step == 0)
    def _():
        greet_all(n)
        for ref in (gmid, gin, dself_sum):
            ref[...] = jnp.zeros_like(ref)

    count = nbr_ref.shape[0] // slabs
    def slot(half):
        for at in range(count):
            which = EARLY_ORDER[2 * at + half]
            if which:

                @pl.when(step == at)
                def _(which=which):
                    for i, stage in which:
                        chunks[i].run(stage)

    x = edge_operand(table_len, slabs, base, e_ref, nbr_ref)
    back = d2_ref[...]
    wide = lambda ref: jnp.concatenate([ref[j] for j in range(slabs)], axis=1)
    two = jnp.concatenate([(back * keep_ref[j] * gp2_ref[j].astype(F32)).astype(BF16) for j in range(slabs)], axis=1)
    gmid[...] += nt(wide(h1_ref), two)

    @pl.when(step == 0)
    def _():
        pl.semaphore_wait(pltpu.get_barrier_semaphore(), n + 1)

    slot(0)
    one = (nn(mid_ref[...], two) * wide(gp1_ref).astype(F32)).astype(BF16)
    gin[...] += nt(x, one)
    part = nn(win_ref[2 * feat :, :], one)
    total = dself_sum[...]
    for j in range(slabs):
        cut = slice(j * rows, (j + 1) * rows)
        egrad_ref[j] = (part_ref[j] + part[:, cut]).astype(BF16)
        total = total + one[:, cut].astype(F32)
    dself_sum[...] = total
    slot(1)

    @pl.when(step == steps - 1)
    def _():
        nodes = x_ref[...]
        dself = jnp.transpose(dself_sum[...]).astype(BF16)
        near = gin[:rows, :].astype(BF16)
        beyond = gin[rows:table_len, :].astype(BF16)
        fill(late_sources, 0, [gmid[...], gin[table_len:, :], tn(nodes, dself), tn(nodes, near) + tn(far_ref[...], beyond)])
        me, peers = ring_place(n)
        copies = swap_back_start(n, me, peers, gin, sel_ref, row_out, far, send_a, recv_a, rows)
        for i, stage in LATE_ORDER:
            if i < 0:
                own = swap_back_finish(n, copies, gin, sel_ref, far, rows)
                grad_ref[...] = dfirst_ref[...] + nt(dself, win_ref[:feat, :]) + nt(own, win_ref[feat : 2 * feat, :])
            else:
                chunks[i].run(stage)


def message_backward(n, e, h1, gp1, gp2, part, keep, nbr, d2, mid, win, x, far_x, dfirst, sel, sources, late_depths, table_len, slabs):
    fan, edge_w, rows = e.shape
    feat = d2.shape[0]
    cap = sel.shape[1] // n
    places = n // 2
    whole = lambda a: pl.BlockSpec(a.shape, lambda i: (0,) * a.ndim)
    slab = lambda f: pl.BlockSpec((slabs, f, rows), lambda i: (i, 0, 0))
    anywhere = pl.BlockSpec(memory_space=pl.ANY)
    consts = (nbr, d2, mid, win, x, far_x, dfirst, sel)
    roomy = table_len <= ROOMY
    place = pltpu.VMEM if roomy else pltpu.HBM
    sources = [pltpu.with_memory_space_constraint(c, place) for c in sources]
    depths = [s.shape[1] for s in sources] + list(late_depths)
    scratch = [pltpu.VMEM((feat, feat), F32), pltpu.VMEM((table_len + edge_w, feat), F32), pltpu.VMEM((feat, rows), F32)]
    scratch += [pltpu.VMEM((n, cap, feat), BF16)] * 2 + [pltpu.SemaphoreType.DMA((n,))] * 2
    scratch += [pltpu.VMEM((16, d, LANES), BF16) for d in late_depths]
    for d in depths:
        scratch += chunk_scratch(places, d)
    return pl.pallas_call(
        functools.partial(message_backward_body, n, table_len, slabs, len(sources), len(late_depths)),
        grid=(fan // slabs,),
        in_specs=[slab(edge_w), slab(feat), slab(feat), slab(feat), slab(edge_w), slab(1)] + [whole(a) for a in consts]
        + [anywhere] * len(sources),
        out_specs=[slab(edge_w), whole(x)] + [anywhere] * len(depths),
        out_shape=[place(e.shape, BF16), place(x.shape, F32)]
        + [place((16, d, LANES), BF16) for d in depths],
        scratch_shapes=scratch,
        compiler_params=pltpu.CompilerParams(vmem_limit_bytes=(42 if roomy else 58) * 1024 * 1024, collective_id=3, has_side_effects=True),
        name="message_backward",
    )(e, h1, gp1, gp2, part, keep, *consts, *sources)


def unpack_body(early, late, feat, hidden, edge_w, *refs):
    count = early + late
    sources, refs = refs[:count], refs[count:]
    (egrad, grad, node), refs = refs[:3], refs[3:]
    (gwin, gmid, gmout, gexp, gcon, guin, egrad_out, grad_out, node_out, gumid, guout), refs = refs[:11], refs[11:]
    vectors_out, refs = refs[:6], refs[6:]
    held = sources
    (swin, smid, smout, sexp, scon, suin, segrad), send = refs[:7], refs[7]
    at = early_rows(feat, hidden, edge_w)
    sent = []

    def push(source, target):
        copy = pltpu.make_async_copy(source, target, send.at[len(sent)])
        copy.start()
        sent.append(copy)

    push(grad, grad_out)
    push(node, node_out)

    def section(bufs, row, size, width, target, top=0, left=0, lane=0):
        for value, offset in unpack(bufs, row, size, LANES):
            target[top + offset : top + offset + value.shape[0], left : left + width] = value[:, lane : lane + width].astype(F32)

    front, back = held[:early], held[early:]
    for b in range(hidden // feat):
        section(front, at["contract"] + b * feat, feat, feat, scon, top=b * feat)
        push(scon.at[pl.ds(b * feat, feat)], gcon.at[pl.ds(b * feat, feat)])
    for b in range(hidden // feat):
        section(front, at["expand"] + b * feat, feat, feat, sexp, left=b * feat)
        push(sexp.at[:, pl.ds(b * feat, feat)], gexp.at[:, pl.ds(b * feat, feat)])
    section(front, at["message_out"], feat, feat, smout)
    push(smout, gmout)
    section(front, at["update_self"], edge_w, feat, suin)
    section(front, at["update_neigh"], edge_w, feat, suin, left=feat)
    section(front, at["update_edge"], edge_w, edge_w, suin, left=2 * feat)
    push(suin, guin)
    section(front, at["update_edge"], edge_w, edge_w, gumid, lane=256)
    section(front, at["update_out"], edge_w, edge_w, guout)
    vectors = unpack(front, at["vectors"], 16, LANES)[0][0].astype(F32)
    for k in range(6):
        size = vectors_out[k].shape[0]
        vectors_out[k][...] = vectors[k : k + 1, :size].reshape(size)
    section(back, 0, feat, feat, smid)
    push(smid, gmid)
    section(back, feat, edge_w, feat, swin, top=2 * feat)
    section(back, feat + edge_w, 2 * feat, feat, swin)
    push(swin, gwin)
    slab = egrad.shape[0] // 4
    for b in range(4):
        for k in range(b * slab, (b + 1) * slab):
            segrad[k] = egrad[k].astype(F32)
        push(segrad.at[pl.ds(b * slab, slab)], egrad_out.at[pl.ds(b * slab, slab)])
    for copy in sent:
        copy.wait()


def unpack_all(chunks, egrad, grad, node, early, feat, hidden, edge_w, roomy):
    whole, anywhere = pl.BlockSpec(memory_space=pltpu.VMEM), pl.BlockSpec(memory_space=pl.ANY)
    big = [(2 * feat + edge_w, feat), (feat, feat), (feat, feat), (feat, hidden), (hidden, feat), (edge_w, 2 * feat + edge_w), egrad.shape]
    small = [(edge_w, edge_w), (edge_w, edge_w), (feat,), (feat,), (feat,), (feat,), (edge_w,), (edge_w,)]
    shapes = [jax.ShapeDtypeStruct(s, F32) for s in big] + [jax.ShapeDtypeStruct(grad.shape, F32), jax.ShapeDtypeStruct(node.shape, BF16)]
    return pl.pallas_call(
        functools.partial(unpack_body, early, len(chunks) - early, feat, hidden, edge_w),
        in_specs=[whole] * (len(chunks) + 3),
        out_specs=[anywhere] * 9 + [whole] * 8,
        out_shape=shapes + [jax.ShapeDtypeStruct(s, F32) for s in small],
        scratch_shapes=[pltpu.VMEM(s, F32) for s in big]
        + [pltpu.SemaphoreType.DMA((24,))],
        compiler_params=pltpu.CompilerParams(vmem_limit_bytes=(30 if roomy else 46) * 1024 * 1024),
        name="unpack_all",
    )(*chunks, egrad, grad, node)


def local(n, node_feats, edge_feats, node_cotan, edge_cotan, neighbour, edge_mask, fetch_rows, chain_ids, complex_flag, message_in,
          message_mid, message_out, gain_node, offset_node, expand_weight, contract_weight, gain_ffn, offset_ffn, update_in, update_mid,
          update_out, gain_edge, offset_edge):
    x = node_feats[0]
    rows, feat = x.shape
    fan = neighbour.shape[1]
    edge_w = edge_feats.shape[3]
    e = jnp.transpose(edge_feats[0], (1, 2, 0))
    cot = jnp.transpose(edge_cotan[0], (1, 2, 0))
    nbr = jnp.transpose(neighbour)
    mask = jnp.transpose(edge_mask)
    uin = jnp.transpose(update_in)
    lhs, self_t, mid_t, umid_t, uout_t, uedge, sel, tag, gain_t, offset_t, far_x = table_rows(
        n, fetch_rows[0], x, chain_ids, complex_flag, message_in, message_mid, update_mid, update_out, uin, gain_edge, offset_edge
    )
    table_len = lhs.shape[1] - edge_w
    slabs = next(c for c in (10, 6, 4, 2, 1) if fan % c == 0)
    h1, gp1, gp2, s, keep, cnt = message_forward(e, nbr, mask, tag, lhs, self_t, mid_t, slabs)
    node, lhs3, self3, n1, r1, n2, r2, acted, slope = node_forward(
        n, s, cnt, x, message_out, gain_node, offset_node, expand_weight, contract_weight, gain_ffn, offset_ffn,
        sel, uin
    )
    edge_new, part, guout, gumid, gin3, dself3, ggain, goff = edge_pass(
        e, cot, nbr, lhs3, self3, umid_t, uout_t, update_mid, update_out, uedge, gain_t, offset_t, slabs
    )
    hidden = expand_weight.shape[1]
    early_depths, late_depths = chunk_plan(n // 2, early_rows(feat, hidden, edge_w)["end"], 3 * feat + edge_w)
    dfirst, d2, *sources = node_backward(
        n, gin3, dself3, sel, node, node_cotan[0], uin, n1, r1, n2, r2, acted, slope, gain_node, offset_node, gain_ffn,
        expand_weight, contract_weight, s, cnt, message_out, ggain, goff, gumid, guout, early_depths
    )
    egrad, ngrad, *sums = message_backward(
        n, e, h1, gp1, gp2, part, keep, nbr, d2, message_mid, message_in, x, far_x, dfirst, sel, sources, late_depths, table_len, slabs
    )
    gwin, gmid, gmout, gexp, gcon, guin, egrad, ngrad, node, gumid, guout, gnode, onode, gffn, offn, gedge, oedge = unpack_all(
        sums, egrad, ngrad, node, len(sources), feat, hidden, edge_w, table_len <= ROOMY
    )
    native = lambda a: jnp.transpose(a, (2, 0, 1))[None]
    return (node[None], native(edge_new), ngrad[None], native(egrad), gwin, gmid, gmout, gnode, onode, gexp, gcon, gffn, offn,
            jnp.transpose(guin), gumid, guout, gedge, oedge)


def solution(mesh):
    grouped, placed, copied = P("tm", "res", None), P("res", None), P()
    wide = P("tm", "res", None, None)
    arguments = (grouped, wide, grouped, wide, placed, placed, P("res", None, None), P("res"), P("res")) + (copied,) * 14
    return jax.shard_map(
        functools.partial(local, mesh.shape["res"]),
        mesh=mesh,
        in_specs=arguments,
        out_specs=(grouped, wide, grouped, wide) + (copied,) * 14,
        check_vma=False,
    )
```

```python
import functools
import jax
import jax.numpy as jnp
from jax import lax
from jax.experimental import pallas as pl
from jax.experimental.pallas import tpu as pltpu
from jax.sharding import PartitionSpec as P

EPSILON = 1e-05
CURVE = 0.7978845608028654
CUBIC = 0.044715
F32 = jnp.float32
BF16 = jnp.bfloat16
VMEM_LIMIT = 60 * 1024 * 1024
MESH = pl.DeviceIdType.MESH


def nn(a, b):
    return lax.dot_general(a, b, (((1,), (0,)), ((), ())), preferred_element_type=F32)


def nt(a, b):
    return lax.dot_general(a, b, (((1,), (1,)), ((), ())), preferred_element_type=F32)


def tn(a, b):
    return lax.dot_general(a, b, (((0,), (0,)), ((), ())), preferred_element_type=F32)


def narrow_gelu(v):
    v = v.astype(BF16)
    square = v * v
    t = jnp.tanh(v * (BF16(CURVE) + BF16(CURVE * CUBIC) * square))
    half = BF16(0.5) + BF16(0.5) * t
    slope = half + (half - half * half) * (v * (BF16(2.0 * CURVE) + BF16(6.0 * CURVE * CUBIC) * square))
    return v * half, slope


def gelu_parts(v):
    square = v * v
    t = jnp.tanh(v * (CURVE + (CURVE * CUBIC) * square))
    half = 0.5 + 0.5 * t
    slope = half + (half - half * half) * (v * (2.0 * CURVE + (6.0 * CURVE * CUBIC) * square))
    return v * half, slope


def tile_lanes(block, count):
    return jnp.concatenate([block] * count, axis=1) if count > 1 else block


def edge_operand(table_len, slabs, base, e_ref, nbr_ref):
    columns = []
    for j in range(slabs):
        row = nbr_ref[pl.ds(base + j, 1), :]
        ids = lax.broadcasted_iota(jnp.int16, (table_len, row.shape[1]), 0)
        hot = jnp.where(ids == jnp.broadcast_to(row, (16, row.shape[1])).astype(jnp.int16)[:1], BF16(1.0), BF16(0.0))
        columns.append(jnp.concatenate([hot, e_ref[j]], axis=0))
    return jnp.concatenate(columns, axis=1) if slabs > 1 else columns[0]


def message_forward_body(table_len, feat, slabs, e_ref, nbr_ref, mask_ref, own_ref, lhs_ref, self_ref, mid_ref,
                         h1_ref, gp1_ref, gp2_ref, s_ref, keep_ref, cnt_ref):
    step = pl.program_id(0)
    base = step * slabs
    rows = nbr_ref.shape[1]

    @pl.when(step == 0)
    def _():
        s_ref[...] = jnp.zeros_like(s_ref)
        cnt_ref[...] = jnp.zeros_like(cnt_ref)

    own = own_ref[...]
    own_chain = own // 2
    own_flag = own % 2
    pre = nn(lhs_ref[...], edge_operand(table_len, slabs, base, e_ref, nbr_ref))
    hidden, slope = narrow_gelu(pre[:feat] + tile_lanes(self_ref[...], slabs))
    total = s_ref[...]
    count = cnt_ref[...]
    keeps = []
    for j in range(slabs):
        cut = slice(j * rows, (j + 1) * rows)
        h1_ref[j] = hidden[:, cut]
        gp1_ref[j] = slope[:, cut]
        other = pre[feat : feat + 1, cut].astype(jnp.int32)
        joined = jnp.logical_or(own_chain == other // 2, own_flag * (other % 2) > 0)
        keep = jnp.where(joined, 1.0, 0.0) * mask_ref[pl.ds(base + j, 1), :].astype(F32)
        keep_ref[j] = keep
        keeps.append(keep)
        count = count + keep
    hidden, slope = narrow_gelu(nn(mid_ref[...], hidden))
    hidden = hidden.astype(F32)
    for j in range(slabs):
        cut = slice(j * rows, (j + 1) * rows)
        gp2_ref[j] = slope[:, cut]
        total = total + hidden[:, cut] * keeps[j]
    s_ref[...] = total
    cnt_ref[...] = count


def message_forward(e, nbr, mask, own_tag, lhs, self_t, mid_t, slabs):
    fan, edge_w, rows = e.shape
    feat = self_t.shape[0]
    table_len = lhs.shape[1] - edge_w
    whole = lambda a: pl.BlockSpec(a.shape, lambda i: (0,) * a.ndim)
    slab = lambda f: pl.BlockSpec((slabs, f, rows), lambda i: (i, 0, 0))
    big = pltpu.HBM((fan, feat, rows), BF16)
    e, nbr, mask = far_off(e, nbr, mask)
    return pl.pallas_call(
        functools.partial(message_forward_body, table_len, feat, slabs),
        grid=(fan // slabs,),
        in_specs=[slab(edge_w), whole(nbr), whole(mask), whole(own_tag), whole(lhs), whole(self_t), whole(mid_t)],
        out_specs=[slab(feat), slab(feat), slab(feat), pl.BlockSpec((feat, rows), lambda i: (0, 0)), slab(1),
                   pl.BlockSpec((1, rows), lambda i: (0, 0))],
        out_shape=[big, big, big, jax.ShapeDtypeStruct((feat, rows), F32), pltpu.HBM((fan, 1, rows), F32),
                   jax.ShapeDtypeStruct((1, rows), F32)],
        compiler_params=pltpu.CompilerParams(vmem_limit_bytes=30 * 1024 * 1024),
        name="message_forward",
    )(e, nbr, mask, own_tag, lhs, self_t, mid_t)


def edge_body(table_len, slabs, e_ref, cot_ref, nbr_ref, lhs_ref, self_ref, mid_t_ref, out_t_ref, mid_ref, out_ref, edge_ref,
              gain_ref, offset_ref,
              new_ref, part_ref, gout_ref, gmid_ref, gin_ref, dself_ref, ggain_ref, goff_ref):
    step = pl.program_id(0)
    base = step * slabs
    rows = nbr_ref.shape[1]

    @pl.when(step == 0)
    def _():
        for ref in (gout_ref, gmid_ref, gin_ref, dself_ref, ggain_ref, goff_ref):
            ref[...] = jnp.zeros_like(ref)

    x = edge_operand(table_len, slabs, base, e_ref, nbr_ref)
    self_t = tile_lanes(self_ref[...], slabs)
    hidden_three, slope_three = narrow_gelu(nn(lhs_ref[...], x) + self_t)
    hidden_four, slope_four = narrow_gelu(nn(mid_t_ref[...], hidden_three))
    branch = nn(out_t_ref[...], hidden_four)
    gain = gain_ref[...]
    offset = offset_ref[...]
    scale = 1.0 / e_ref.shape[1]
    resid = []
    ggain = ggain_ref[...]
    goff = goff_ref[...]
    for j in range(slabs):
        z = e_ref[j].astype(F32) + branch[:, j * rows : (j + 1) * rows]
        z = z - jnp.sum(z, axis=0, keepdims=True) * scale
        r = lax.rsqrt(jnp.sum(z * z, axis=0, keepdims=True) * scale + EPSILON)
        h = z * r
        new_ref[j] = (h * gain + offset).astype(BF16)
        dy = cot_ref[j].astype(F32)
        ggain = ggain + dy * h
        goff = goff + dy
        dh = dy * gain
        one = jnp.sum(dh, axis=0, keepdims=True) * scale
        two = jnp.sum(dh * h, axis=0, keepdims=True) * scale
        resid.append(r * (dh - one - h * two))
    ggain_ref[...] = ggain
    goff_ref[...] = goff
    resid = jnp.concatenate(resid, axis=1) if slabs > 1 else resid[0]
    delta = resid.astype(BF16)
    gout_ref[...] += nt(hidden_four, delta)
    delta_four = (nn(out_ref[...], delta) * slope_four.astype(F32)).astype(BF16)
    gmid_ref[...] += nt(hidden_three, delta_four)
    delta_three = nn(mid_ref[...], delta_four) * slope_three.astype(F32)
    low = delta_three.astype(BF16)
    gin_ref[...] += nt(x, low)
    part = resid + nn(edge_ref[...], low)
    dself = dself_ref[...]
    for j in range(slabs):
        cut = slice(j * rows, (j + 1) * rows)
        part_ref[j] = part[:, cut]
        dself = dself + low[:, cut].astype(F32)
    dself_ref[...] = dself


def edge_pass(e, cot, nbr, lhs, self_t, mid_t, out_t, mid, out, edge, gain, offset, slabs):
    fan, edge_w, rows = e.shape
    table_len = lhs.shape[1] - edge_w
    whole = lambda a: pl.BlockSpec(a.shape, lambda i: (0,) * a.ndim)
    slab = pl.BlockSpec((slabs, edge_w, rows), lambda i: (i, 0, 0))
    keep = lambda *s: (pl.BlockSpec(s, lambda i: (0,) * len(s)), jax.ShapeDtypeStruct(s, F32))
    sums = [keep(edge_w, edge_w), keep(edge_w, edge_w), keep(table_len + edge_w, edge_w), keep(edge_w, rows), keep(edge_w, rows),
            keep(edge_w, rows)]
    e, cot, nbr, mid, out = far_off(e, cot, nbr, mid, out)
    consts = (nbr, lhs, self_t, mid_t, out_t, mid, out, edge, gain, offset)
    return pl.pallas_call(
        functools.partial(edge_body, table_len, slabs),
        grid=(fan // slabs,),
        in_specs=[slab, slab] + [whole(a) for a in consts],
        out_specs=[slab, slab] + [s for s, _ in sums],
        out_shape=[pltpu.HBM(e.shape, BF16), pltpu.HBM(e.shape, F32)] + [s for _, s in sums],
        compiler_params=pltpu.CompilerParams(vmem_limit_bytes=42 * 1024 * 1024),
        name="edge_pass",
    )(e, cot, *consts)


LANES = 512


def spot():
    group, place = lax.axis_index("tm"), lax.axis_index("res")
    return group, place, lax.rem(place, 2), place // 2, lax.rem(group, 2), group // 2


def grain(places):
    return 16 * max(1, places // 4)


def piece(places, depth, index):
    across = min(places, 4)
    rows, wide = piece_shape(places, depth)
    top = pl.multiple_of((index // across) * rows, rows)
    left = pl.multiple_of(lax.rem(index, across) * wide, wide)
    return pl.ds(top, rows), pl.ds(left, wide)


def piece_shape(places, depth):
    across = min(places, 4)
    return depth // (places // across), LANES // across


def remote(source, target, send, recv, group, place):
    return pltpu.make_async_remote_copy(
        src_ref=source, dst_ref=target, send_sem=send, recv_sem=recv, device_id={"tm": group, "res": place}, device_id_type=MESH
    )


class Chunk:
    def __init__(self, places, source, result, acc, from_core, from_first, from_second, from_line, stage, out, sends, recvs, local):
        self.places, self.source, self.result, self.acc = places, source, result, acc
        self.from_core, self.from_first, self.from_second = from_core, from_first, from_second
        self.from_line, self.stage, self.out = from_line, stage, out
        self.sends, self.recvs, self.local = sends, recvs, local
        self.depth = acc.shape[1]

    def run(self, stage):
        (self.spread, self.halve, self.quarter, self.scatter, self.settle, self.gather, self.widen, self.share, self.store,
         self.close)[stage]()

    def link(self, slot, source, target, group, place):
        return functools.partial(remote, source, target, self.sends.at[slot], self.recvs.at[slot], group, place)

    def core_copy(self):
        group, place, core, lane, x, y = spot()
        theirs = pl.multiple_of((1 - core) * 8, 8)
        return self.link(0, self.source.at[pl.ds(theirs, 8)], self.from_core, group, place + 1 - 2 * core)

    def load_copy(self):
        core = spot()[2]
        return pltpu.make_async_copy(self.source.at[pl.ds(pl.multiple_of(core * 8, 8), 8)], self.acc, self.local.at[0])

    def half_copies(self):
        group, place, core, lane, x, y = spot()
        return [
            self.link(1, self.acc.at[pl.ds((1 - x) * 2, 2)], self.from_first.at[pl.ds(0, 2)], group + 1 - 2 * x, place),
            self.link(2, self.acc.at[pl.ds(4 + (1 - y) * 2, 2)], self.from_first.at[pl.ds(2, 2)], group + 2 - 4 * y, place),
        ]

    def quarter_copies(self):
        group, place, core, lane, x, y = spot()
        return [
            self.link(3, self.acc.at[x * 2 + 1 - y], self.from_second.at[0], group + 2 - 4 * y, place),
            self.link(4, self.acc.at[4 + y * 2 + 1 - x], self.from_second.at[1], group + 1 - 2 * x, place),
        ]

    def line_copies(self):
        group, place, core, lane, x, y = spot()
        copies = []
        for s in range(1, self.places):
            ahead, behind = lax.rem(lane + s, self.places), lax.rem(lane + self.places - s, self.places)
            rows, wide = piece(self.places, self.depth, ahead)
            view = self.stage.at[:, rows, wide]
            copies.append((self.link(4 + s, view, self.from_line.at[lane], group, ahead * 2 + core),
                           self.link(4 + s, view, self.from_line.at[behind], group, behind * 2 + core)))
        return copies

    def own(self):
        group, place, core, lane, x, y = spot()
        return core * 8 + x * 2 + y, core * 8 + 4 + y * 2 + x

    def spread_copies(self):
        group, place, core, lane, x, y = spot()
        copies = []
        slot = 4 + self.places
        for own in self.own():
            for s in range(1, self.places):
                ahead, behind = lax.rem(lane + s, self.places), lax.rem(lane + self.places - s, self.places)
                rows, wide = piece(self.places, self.depth, lane)
                back_rows, back_wide = piece(self.places, self.depth, behind)
                view, back = self.out.at[own, rows, wide], self.out.at[own, back_rows, back_wide]
                copies.append((self.link(slot, view, view, group, ahead * 2 + core), self.link(slot, back, back, group, behind * 2 + core)))
                slot += 1
        return copies

    def both(self, slot, view, back, group, place):
        return self.link(slot, view, view, group, place), self.link(slot, back, back, group, place)

    def gather_copies(self):
        group, place, core, lane, x, y = spot()
        slot = 2 + 3 * self.places
        first, second = self.own()
        return [
            self.both(slot, self.out.at[first], self.out.at[core * 8 + x * 2 + 1 - y], group + 2 - 4 * y, place),
            self.both(slot + 1, self.out.at[second], self.out.at[core * 8 + 4 + y * 2 + 1 - x], group + 1 - 2 * x, place),
        ]

    def widen_copies(self):
        group, place, core, lane, x, y = spot()
        slot = 4 + 3 * self.places
        two = lambda start: self.out.at[pl.ds(start, 2)]
        return [
            self.both(slot, two(core * 8 + x * 2), two(core * 8 + 2 - x * 2), group + 1 - 2 * x, place),
            self.both(slot + 1, two(core * 8 + 4 + y * 2), two(core * 8 + 6 - y * 2), group + 2 - 4 * y, place),
        ]

    def share_copy(self):
        group, place, core, lane, x, y = spot()
        eight = lambda which: self.out.at[pl.ds(pl.multiple_of(which * 8, 8), 8)]
        return self.both(6 + 3 * self.places, eight(core), eight(1 - core), group, place + 1 - 2 * core)

    def store_copy(self, which, slot):
        eight = pl.ds(pl.multiple_of(which * 8, 8), 8)
        return pltpu.make_async_copy(self.out.at[eight], self.result.at[eight], self.local.at[slot])

    def spread(self):
        self.core_copy()().start()
        self.load_copy().start()

    def halve(self):
        group, place, core, lane, x, y = spot()
        self.load_copy().wait()
        self.core_copy()().wait()
        acc, extra = self.acc, self.from_core
        give = [(1 - x) * 2, 4 + (1 - y) * 2]
        keep = [x * 2, 4 + y * 2]
        for start in give:
            for i in range(2):
                acc[start + i] = acc[start + i] + extra[start + i]
        for copy in self.half_copies():
            copy().start()
        for start in keep:
            for i in range(2):
                acc[start + i] = acc[start + i] + extra[start + i]

    def quarter(self):
        group, place, core, lane, x, y = spot()
        for copy in self.half_copies():
            copy().wait()
        acc, extra = self.acc, self.from_first
        acc[x * 2 + 1 - y] = acc[x * 2 + 1 - y] + extra[1 - y]
        acc[4 + y * 2 + 1 - x] = acc[4 + y * 2 + 1 - x] + extra[3 - x]
        for copy in self.quarter_copies():
            copy().start()
        self.stage[0] = acc[x * 2 + y] + extra[y]
        self.stage[1] = acc[4 + y * 2 + x] + extra[2 + x]

    def scatter(self):
        for copy in self.quarter_copies():
            copy().wait()
        for s in range(2):
            self.stage[s] = self.stage[s] + self.from_second[s]
        for send, arrive in self.line_copies():
            send().start()

    def settle(self):
        group, place, core, lane, x, y = spot()
        rows, wide = piece(self.places, self.depth, lane)
        total = self.stage[:, rows, wide].astype(F32)
        pairs = self.line_copies()
        for s in range(1, self.places):
            pairs[s - 1][1]().wait_recv()
            total = total + self.from_line[lax.rem(lane + self.places - s, self.places)].astype(F32)
        first, second = self.own()
        total = total.astype(BF16)
        self.out[first, rows, wide] = total[0]
        self.out[second, rows, wide] = total[1]
        for send, arrive in self.spread_copies():
            send().start()
        for send, arrive in pairs:
            send().wait_send()

    def finish(self, pairs):
        for send, arrive in pairs:
            arrive().wait_recv()
        for send, arrive in pairs:
            send().wait_send()

    def gather(self):
        self.finish(self.spread_copies())
        for send, arrive in self.gather_copies():
            send().start()

    def widen(self):
        self.finish(self.gather_copies())
        for send, arrive in self.widen_copies():
            send().start()

    def share(self):
        core = spot()[2]
        self.finish(self.widen_copies())
        self.share_copy()[0]().start()
        self.store_copy(core, 1).start()

    def store(self):
        core = spot()[2]
        self.share_copy()[1]().wait_recv()
        self.store_copy(1 - core, 2).start()

    def close(self):
        core = spot()[2]
        self.share_copy()[0]().wait_send()
        self.store_copy(core, 1).wait()
        self.store_copy(1 - core, 2).wait()


CHUNK_REFS = 10
ROOMY = 512


def chunk_scratch(places, depth):
    rows, wide = piece_shape(places, depth)
    shapes = [(8, depth, LANES), (8, depth, LANES), (4, depth, LANES), (2, depth, LANES), (places, 2, rows, wide), (2, depth, LANES),
              (16, depth, LANES)]
    links = 7 + 3 * places
    return [pltpu.VMEM(s, BF16) for s in shapes] + [pltpu.SemaphoreType.DMA((links,))] * 2 + [pltpu.SemaphoreType.DMA((3,))]


def greet_all(n):
    group, place, core, lane, x, y = spot()
    barrier = pltpu.get_barrier_semaphore()
    partners = [(group + 1 - 2 * x, place), (group + 2 - 4 * y, place)]
    partners += [(group, lax.rem(place + s, n)) for s in range(1, n)]
    for near, far in partners:
        pl.semaphore_signal(barrier, inc=1, device_id={"tm": near, "res": far}, device_id_type=MESH)


def chunk_plan(places, early_rows, late_first, late_second):
    unit = grain(places)
    depth = lambda rows: -(-rows // (16 * unit)) * unit
    total = depth(early_rows)
    steps = total // unit
    return [(steps + k) // 4 * unit for k in range(4)], [depth(late_first), depth(late_second)]


def pack(bufs, row, value):
    start = 0
    value = value.astype(BF16)
    for buf in bufs:
        size = buf.shape[0] * buf.shape[1]
        depth = buf.shape[1]
        low, high = max(row, start), min(row + value.shape[0], start + size)
        while low < high:
            slot, inner = divmod(low - start, depth)
            step = min(high - low, depth - inner)
            buf[slot, inner : inner + step, : value.shape[1]] = value[low - row : low - row + step]
            low += step
        start += size


def fill(bufs, row, values):
    for value in values:
        pack(bufs, row, value)
        row += value.shape[0]
    spare = sum(b.shape[0] * b.shape[1] for b in bufs) - row
    if spare:
        pack(bufs, row, jnp.zeros((spare, bufs[0].shape[2]), F32))


def unpack(bufs, row, count, width):
    pieces = []
    start = 0
    for buf in bufs:
        depth = buf.shape[1]
        size = buf.shape[0] * depth
        low, high = max(row, start), min(row + count, start + size)
        while low < high:
            slot, inner = divmod(low - start, depth)
            step = min(high - low, depth - inner)
            pieces.append((buf[slot, inner : inner + step, : width], low - row))
            low += step
        start += size
    return pieces


def ring_place(n):
    me = lax.axis_index("res")
    return me, [lax.rem(me + s, n) for s in range(n)]


def greet_start(peers):
    barrier = pltpu.get_barrier_semaphore()
    for peer in peers[1:]:
        pl.semaphore_signal(barrier, inc=1, device_id={"res": peer}, device_id_type=MESH)


def greet_end(peers):
    pl.semaphore_wait(pltpu.get_barrier_semaphore(), len(peers) - 1)


def copy_to(peer, source, target, send, recv):
    return pltpu.make_async_remote_copy(
        src_ref=source, dst_ref=target, send_sem=send, recv_sem=recv, device_id={"res": peer}, device_id_type=MESH
    )


def swap(n, me, peers, source, target, send, recv, placed=False):
    view = lambda s: source.at[peers[s] if placed else s]
    sent = [copy_to(peers[s], view(s), target.at[me], send.at[s], recv.at[me]) for s in range(1, n)]
    back = [copy_to(peers[s], view(s), target.at[peers[s]], send.at[s], recv.at[peers[s]]) for s in range(1, n)]
    return sent, back


def row_norm(values):
    values = values - jnp.mean(values, axis=1, keepdims=True)
    r = lax.rsqrt(jnp.mean(values * values, axis=1, keepdims=True) + EPSILON)
    return values * r, r


def row_norm_back(dh, h, r):
    return r * (dh - jnp.mean(dh, axis=1, keepdims=True) - h * jnp.mean(dh * h, axis=1, keepdims=True))


def table_rows_body(n, fetch_ref, x_ref, chain_ref, flag_ref, win_hbm, mid_hbm, umid_hbm, uout_hbm, uin_hbm, gain_ref, off_ref,
                    lhs_ref, self_ref, midt_ref, umidt_ref, uoutt_ref, uedge_ref, sel_ref, tag_ref, gaint_ref, offt_ref, far_ref,
                    idx_out, idx_in, row_out, far, wants, asked, win_ref, mid_ref, umid_ref, uout_ref, uin_ref, send_a, recv_a, send_b, recv_b,
                    load):
    me, peers = ring_place(n)
    greet_start(peers)
    pairs = ((win_hbm, win_ref), (mid_hbm, mid_ref), (umid_hbm, umid_ref), (uout_hbm, uout_ref), (uin_hbm, uin_ref))
    loads = [pltpu.make_async_copy(pairs[k][0], pairs[k][1], load.at[k]) for k in range(5)]
    for copy in loads:
        copy.start()
    rows, feat = x_ref.shape
    cap = fetch_ref.shape[1]
    edge_w = win_ref.shape[0] - 2 * feat
    tag = chain_ref[...].reshape(1, rows) * 2 + flag_ref[...].reshape(1, rows)
    tag_ref[...] = tag
    for s in range(n):
        idx_out[s] = jnp.full((8, 128), -1, jnp.int32)
        idx_out[s, 0:1, 0:cap] = fetch_ref[pl.ds(peers[s], 1), :]
        idx_out[s, 1:2, 0:rows] = tag
    greet_end(peers)
    sent, back = swap(n, me, peers, idx_out, idx_in, send_a, recv_a)
    for copy in sent:
        copy.start()
    idx_in[me] = idx_out[0]
    x = x_ref[...]
    for p in range(n):
        wants[0:1, p * cap : (p + 1) * cap] = fetch_ref[p : p + 1, :]
    loads[0].wait()
    self_ref[...] = jnp.transpose(nn(x, win_ref[:feat, :]))

    copies, backs = swap(n, me, peers, row_out, far, send_b, recv_b, True)
    for copy in back:
        copy.wait_recv()
    for p in range(n):
        asked[0:1, p * cap : (p + 1) * cap] = idx_in[p, 0:1, 0:cap]
    spots = lax.broadcasted_iota(jnp.int32, (rows, n * cap), 0)
    hot = jnp.where(spots + me * rows == asked[...], 1.0, 0.0).astype(BF16)
    row_out[...] = tn(hot, x).astype(BF16).reshape(n, cap, feat)
    for copy in copies:
        copy.start()
    sel_ref[...] = hot
    far[me] = row_out[me]
    for copy in loads[1:]:
        copy.wait()
    midt_ref[...] = jnp.transpose(mid_ref[...])
    umidt_ref[...] = jnp.transpose(umid_ref[...])
    uoutt_ref[...] = jnp.transpose(uout_ref[...])
    uedge_ref[...] = jnp.transpose(uin_ref[:, 2 * feat :])
    for source, target in ((gain_ref, gaint_ref), (off_ref, offt_ref)):
        target[...] = jnp.transpose(jnp.broadcast_to(source[...].astype(F32).reshape(1, edge_w), (rows, edge_w)))
    neigh = win_ref[feat : 2 * feat, :]
    extra = lhs_ref.shape[0] - feat
    table_len = rows + n * cap
    lhs_ref[feat:, table_len:] = jnp.zeros((extra, edge_w), BF16)
    lhs_ref[:feat, table_len:] = jnp.transpose(win_ref[2 * feat :, :])
    lhs_ref[:feat, :rows] = jnp.transpose(nn(x, neigh)).astype(BF16)
    lhs_ref[feat:, :rows] = jnp.broadcast_to(tag.astype(F32), (extra, rows)).astype(BF16)
    tags = jnp.concatenate([idx_in[p, 1:2, 0:rows] for p in range(n)] + [jnp.zeros((-n % 16, rows), jnp.int32)] * (n % 16 > 0), axis=0)
    want = wants[...]
    picked = nn(tags.astype(F32).astype(BF16), jnp.where(spots == lax.rem(want, rows), 1.0, 0.0).astype(BF16))
    owner = lax.broadcasted_iota(jnp.int32, picked.shape, 0) == want // rows
    far_tag = jnp.sum(jnp.where(owner, picked, 0.0), axis=0, keepdims=True)
    lhs_ref[feat:, rows:table_len] = jnp.broadcast_to(far_tag, (extra, n * cap)).astype(BF16)
    for copy in backs:
        copy.wait_recv()
    got = far[...].reshape(n * cap, feat)
    lhs_ref[:feat, rows:table_len] = jnp.transpose(nn(got, neigh)).astype(BF16)
    far_ref[...] = got
    for copy in sent + copies:
        copy.wait_send()


def far_off(*arrays):
    return [pltpu.with_memory_space_constraint(a, pltpu.HBM) for a in arrays]


def vmem_call(body, args, outs, scratch, collective, name, outside=(), raw=()):
    whole = pl.BlockSpec(memory_space=pltpu.VMEM)
    return pl.pallas_call(
        body,
        out_shape=[pltpu.HBM(s, d) if i in outside else jax.ShapeDtypeStruct(s, d) for i, (s, d) in enumerate(outs)],
        in_specs=[pl.BlockSpec(memory_space=pl.ANY) if i in raw else whole for i in range(len(args))],
        out_specs=[whole] * len(outs),
        scratch_shapes=scratch,
        compiler_params=pltpu.CompilerParams(vmem_limit_bytes=30 * 1024 * 1024, collective_id=collective, has_side_effects=True),
        name=name,
    )(*args)


def table_rows(n, fetch, x, chain, flag, win, mid, umid, uout, uin, gain, off):
    rows, feat = x.shape
    cap = fetch.shape[1]
    edge_w = win.shape[0] - 2 * feat
    table_len = rows + n * cap
    outs = [((feat + 16, table_len + edge_w), BF16), ((feat, rows), F32), (mid.shape, BF16), (umid.shape, BF16), (uout.shape, BF16),
            ((edge_w, edge_w), BF16), ((rows, n * cap), BF16), ((1, rows), jnp.int32), ((edge_w, rows), F32), ((edge_w, rows), F32),
            ((n * cap, feat), BF16)]
    sems = [pltpu.SemaphoreType.DMA((n,))] * 4 + [pltpu.SemaphoreType.DMA((5,))]
    scratch = [pltpu.VMEM((n, 8, 128), jnp.int32)] * 2 + [pltpu.VMEM((n, cap, feat), BF16)] * 2 + [pltpu.VMEM((1, n * cap), jnp.int32)] * 2
    scratch += [pltpu.VMEM(w.shape, BF16) for w in (win, mid, umid, uout, uin)]
    return vmem_call(functools.partial(table_rows_body, n), far_off(fetch, x, chain, flag, win, mid, umid, uout, uin, gain, off), outs,
                     scratch + sems, 0, "table_rows", (10,), range(4, 9))


def node_forward_body(n, s_ref, cnt_ref, x_ref, mout_ref, gain_ref, off_ref, exp_ref, con_ref, gain2_ref, off2_ref, sel_ref, uin_ref,
                      node_ref, lhs_ref, self_ref, h1_ref, r1_ref, h2_ref, r2_ref, acted_ref, slope_ref,
                      row_out, far, send_a, recv_a):
    me, peers = ring_place(n)
    greet_start(peers)
    rows, feat = x_ref.shape
    cap = sel_ref.shape[1] // n
    edge_w = uin_ref.shape[0]
    line = lambda ref: ref[...].astype(F32).reshape(1, feat)
    mean = jnp.transpose(s_ref[...] / jnp.maximum(cnt_ref[...], 1.0))
    upper = mean.astype(BF16)
    lower = (mean - upper.astype(F32)).astype(BF16)
    aggregate = nn(upper, mout_ref[...]) + nn(lower, mout_ref[...])
    h, r = row_norm(x_ref[...].astype(F32) + aggregate)
    h1_ref[...] = h
    r1_ref[...] = r
    first = h * line(gain_ref) + line(off_ref)
    hidden, slope = gelu_parts(nn(first.astype(BF16), exp_ref[...]))
    acted = hidden.astype(BF16)
    acted_ref[...] = acted
    slope_ref[...] = slope
    h, r = row_norm(first + nn(acted, con_ref[...]))
    h2_ref[...] = h
    r2_ref[...] = r
    low = (h * line(gain2_ref) + line(off2_ref)).astype(BF16)
    node_ref[...] = low
    neigh = nt(low, uin_ref[:, feat : 2 * feat])
    packed = neigh.astype(BF16)
    greet_end(peers)
    copies, backs = swap(n, me, peers, row_out, far, send_a, recv_a, True)
    row_out[...] = tn(sel_ref[...], packed).astype(BF16).reshape(n, cap, edge_w)
    for copy in copies:
        copy.start()
    far[me] = row_out[me]
    self_ref[...] = nt(uin_ref[:, :feat], low)
    table_len = rows + n * cap
    lhs_ref[:, :rows] = jnp.transpose(neigh).astype(BF16)
    lhs_ref[:, table_len:] = uin_ref[:, 2 * feat :]
    for copy in backs:
        copy.wait_recv()
    lhs_ref[:, rows:table_len] = jnp.transpose(far[...].reshape(n * cap, edge_w))
    for copy in copies:
        copy.wait_send()


def node_forward(n, s, cnt, x, mout, gain, off, expand, contract, gain2, off2, sel, uin):
    rows, feat = x.shape
    cap = sel.shape[1] // n
    edge_w = uin.shape[0]
    table_len = rows + n * cap
    hidden = expand.shape[1]
    outs = [(x.shape, BF16), ((edge_w, table_len + edge_w), BF16), ((edge_w, rows), F32), (x.shape, F32), ((rows, 1), F32),
            (x.shape, F32), ((rows, 1), F32), ((rows, hidden), BF16), ((rows, hidden), F32)]
    scratch = [pltpu.VMEM((n, cap, edge_w), BF16)] * 2 + [pltpu.SemaphoreType.DMA((n,))] * 2
    return vmem_call(functools.partial(node_forward_body, n),
                     [s, cnt] + far_off(x, mout, gain, off) + [expand, contract] + far_off(gain2, off2) + [sel, uin], outs, scratch, 1,
                     "node_forward")


def swap_back_start(n, me, peers, gin, sel_ref, row_out, far, send, recv, rows):
    cap = sel_ref.shape[1] // n
    copies, backs = swap(n, me, peers, row_out, far, send, recv, True)
    row_out[...] = gin[pl.ds(rows, n * cap), :].astype(BF16).reshape(n, cap, gin.shape[1])
    for copy in copies:
        copy.start()
    far[me] = row_out[me]
    return copies, backs


def swap_back_finish(n, copies, gin, sel_ref, far, rows):
    for copy in copies[1]:
        copy.wait_recv()
    total = gin[:rows, :] + nn(sel_ref[...], far[...].reshape(sel_ref.shape[1], gin.shape[1]))
    for copy in copies[0]:
        copy.wait_send()
    return total.astype(BF16)


def node_backward_body(n, gin_ref, dself_ref, sel_ref, node_ref, cot_ref, uin_ref, h1_ref, r1_ref, h2_ref, r2_ref, acted_ref, slope_ref,
                       gain_ref, off_ref, gain2_ref, exp_ref, con_ref, s_ref, cnt_ref, mout_ref, ggain_ref, goff_ref,
                       gumid_ref, guout_ref, dfirst_ref, d2_ref, vec_ref, *rest):
    chunks, (row_out, far, send_a, recv_a) = rest[:-4], rest[-4:]
    me, peers = ring_place(n)
    rows, feat = node_ref.shape
    edge_w = uin_ref.shape[0]
    greet_start(peers)
    line = lambda ref: ref[...].astype(F32).reshape(1, feat)
    table_len = gin_ref.shape[0] - edge_w
    dself_t = dself_ref[...].astype(BF16)
    dself = jnp.transpose(dself_ref[...]).astype(BF16)
    greet_end(peers)
    copies = swap_back_start(n, me, peers, gin_ref, sel_ref, row_out, far, send_a, recv_a, rows)
    node = node_ref[...]
    at = early_rows(feat, acted_ref.shape[1], edge_w)
    pack(chunks, at["update_self"], nn(dself_t, node))
    gap = jnp.zeros((edge_w, 256 - edge_w), F32)
    pack(chunks, at["update_edge"], jnp.concatenate([jnp.transpose(gin_ref[table_len:, :]), gap, gumid_ref[...], gap], axis=1))
    pack(chunks, at["update_out"], jnp.concatenate([guout_ref[...], jnp.zeros((edge_w, feat - edge_w), F32)], axis=1))
    side = jnp.zeros((1, feat - edge_w), F32)
    edge_sums = [jnp.concatenate([jnp.sum(jnp.transpose(ref[...]), axis=0, keepdims=True), side], axis=1) for ref in (ggain_ref, goff_ref)]
    used = at["end"]
    spare = sum(c.shape[0] * c.shape[1] for c in chunks) - used
    if spare:
        pack(chunks, used, jnp.zeros((spare, feat), F32))
    dy = cot_ref[...].astype(F32) + nn(dself, uin_ref[:, :feat])
    own = swap_back_finish(n, copies, gin_ref, sel_ref, far, rows)
    dy = dy + nn(own, uin_ref[:, feat : 2 * feat])
    pack(chunks, at["update_neigh"], tn(own, node))
    h2 = h2_ref[...]
    ffn_sums = [jnp.sum(dy * h2, axis=0, keepdims=True), jnp.sum(dy, axis=0, keepdims=True)]
    second = row_norm_back(dy * line(gain2_ref), h2, r2_ref[...])
    dffn = second.astype(BF16)
    for b in range(acted_ref.shape[1] // feat):
        pack(chunks, at["contract"] + b * feat, tn(acted_ref[:, b * feat : (b + 1) * feat], dffn))
    dinner = (nt(dffn, con_ref[...]) * slope_ref[...]).astype(BF16)
    h1 = h1_ref[...]
    gain = line(gain_ref)
    first_low = (h1 * gain + line(off_ref)).astype(BF16)
    for b in range(acted_ref.shape[1] // feat):
        pack(chunks, at["expand"] + b * feat, tn(first_low, dinner[:, b * feat : (b + 1) * feat]))
    dy = second + nt(dinner, exp_ref[...])
    sums = [jnp.sum(dy * h1, axis=0, keepdims=True), jnp.sum(dy, axis=0, keepdims=True)] + ffn_sums
    dfirst = row_norm_back(dy * gain, h1, r1_ref[...])
    dfirst_ref[...] = dfirst
    back = (jnp.transpose(dfirst) / jnp.maximum(cnt_ref[...], 1.0)).astype(BF16)
    d2_ref[...] = nn(mout_ref[...], back)
    pack(chunks, at["message_out"], nt(s_ref[...].astype(BF16), back))
    vec_ref[...] = jnp.concatenate(sums + edge_sums + [jnp.zeros((10, feat), F32)], axis=0)


def early_rows(feat, hidden, edge_w):
    at, row = {}, 0
    for name, count in (("contract", hidden), ("expand", hidden), ("message_out", feat), ("update_self", edge_w),
                        ("update_neigh", edge_w), ("update_edge", edge_w), ("update_out", edge_w)):
        at[name] = row
        row += count
    at["end"] = row
    return at


def node_backward(n, gin, dself, sel, node, cot, uin, h1, r1, h2, r2, acted, slope, gain, off, gain2, expand, contract, s, cnt, mout,
                  ggain, goff, gumid, guout, depths):
    rows, feat = node.shape
    cap = sel.shape[1] // n
    edge_w = uin.shape[0]
    outs = [(node.shape, F32), ((feat, rows), F32), ((16, feat), F32)] + [((16, d, LANES), BF16) for d in depths]
    scratch = [pltpu.VMEM((n, cap, edge_w), BF16)] * 2 + [pltpu.SemaphoreType.DMA((n,))] * 2
    return vmem_call(functools.partial(node_backward_body, n),
                     [gin, dself, sel, node] + far_off(cot) + [uin, h1, r1, h2, r2, acted, slope] + far_off(gain, off, gain2)
                     + [expand, contract, s, cnt] + far_off(mout) + [ggain, goff, gumid, guout], outs, scratch, 2, "node_backward",
                     (0, 1, 2))


EARLY_ORDER = (
    ((2, 0),),
    ((1, 0), (2, 1)),
    (),
    ((1, 1), (0, 0)),
    ((2, 2),),
    (),
    ((1, 2), (3, 0), (0, 1), (2, 3)),
    (),
    ((1, 3), (3, 1)),
    ((2, 4),),
    ((0, 2),),
    (),
)
LATE_ORDER = (
    (1, 4), (3, 2), (5, 0), (0, 3), (2, 5), (5, 1), (3, 3), (4, 1), (1, 5), (0, 4), (2, 6), (5, 2), (3, 4), (4, 2),
    (1, 6), (5, 3), (0, 5), (4, 3), (3, 5), (5, 4), (2, 7), (0, 6), (2, 8), (1, 7), (3, 6), (4, 4), (5, 5), (4, 5), (0, 7),
    (5, 6), (-1, 0), (0, 8), (3, 7), (4, 6), (3, 8), (1, 8), (5, 7), (1, 9), (4, 7), (0, 9), (5, 8), (2, 9), (4, 8), (5, 9),
    (3, 9), (4, 9),
)


def message_backward_body(n, table_len, slabs, early, late, *refs):
    (e_ref, h1_ref, gp1_ref, gp2_ref, part_ref, keep_ref, nbr_ref, d2_ref, mid_ref, win_ref, x_ref, far_ref, dfirst_ref, vec_ref, sel_ref) = refs[:15]
    refs = refs[15:]
    sources, refs = refs[:early], refs[early:]
    egrad_ref, grad_ref, results, refs = refs[0], refs[1], refs[2 : 2 + early + late], refs[2 + early + late :]
    (gmid, gin, dself_sum, row_out, far, send_a, recv_a), refs = refs[:7], refs[7:]
    late_sources, refs = refs[:late], refs[late:]
    places = n // 2
    chunks = [Chunk(places, (list(sources) + list(late_sources))[i], results[i], *refs[CHUNK_REFS * i : CHUNK_REFS * (i + 1)])
              for i in range(early + late)]
    step = pl.program_id(0)
    base = step * slabs
    steps = pl.num_programs(0)
    rows = nbr_ref.shape[1]
    feat = d2_ref.shape[0]

    @pl.when(step == 0)
    def _():
        greet_all(n)
        for ref in (gmid, gin, dself_sum):
            ref[...] = jnp.zeros_like(ref)

    count = nbr_ref.shape[0] // slabs
    def slot(half):
        for at in range(count):
            which = EARLY_ORDER[2 * at + half]
            if which:

                @pl.when(step == at)
                def _(which=which):
                    for i, stage in which:
                        chunks[i].run(stage)

    x = edge_operand(table_len, slabs, base, e_ref, nbr_ref)
    back = d2_ref[...]
    wide = lambda ref: jnp.concatenate([ref[j] for j in range(slabs)], axis=1)
    two = jnp.concatenate([(back * keep_ref[j] * gp2_ref[j].astype(F32)).astype(BF16) for j in range(slabs)], axis=1)
    gmid[...] += nt(wide(h1_ref), two)

    @pl.when(step == 0)
    def _():
        pl.semaphore_wait(pltpu.get_barrier_semaphore(), n + 1)

    slot(0)
    one = (nn(mid_ref[...], two) * wide(gp1_ref).astype(F32)).astype(BF16)
    gin[...] += nt(x, one)
    part = nn(win_ref[2 * feat :, :], one)
    total = dself_sum[...]
    for j in range(slabs):
        cut = slice(j * rows, (j + 1) * rows)
        egrad_ref[j] = (part_ref[j] + part[:, cut]).astype(BF16)
        total = total + one[:, cut].astype(F32)
    dself_sum[...] = total
    slot(1)

    @pl.when(step == steps - 1)
    def _():
        nodes = x_ref[...]
        dself = jnp.transpose(dself_sum[...]).astype(BF16)
        near = gin[:rows, :].astype(BF16)
        beyond = gin[rows:table_len, :].astype(BF16)
        fill(late_sources[:1], 0, [gmid[...], gin[table_len:, :], vec_ref[...]])
        chunks[early].run(0)
        fill(late_sources[1:], 0, [tn(nodes, dself), tn(nodes, near) + tn(far_ref[...], beyond)])
        me, peers = ring_place(n)
        copies = swap_back_start(n, me, peers, gin, sel_ref, row_out, far, send_a, recv_a, rows)
        for i, stage in LATE_ORDER:
            if i < 0:
                own = swap_back_finish(n, copies, gin, sel_ref, far, rows)
                grad_ref[...] = dfirst_ref[...] + nt(dself, win_ref[:feat, :]) + nt(own, win_ref[feat : 2 * feat, :])
            else:
                chunks[i].run(stage)


def message_backward(n, e, h1, gp1, gp2, part, keep, nbr, d2, mid, win, x, far_x, dfirst, vectors, sel, sources, late_depths, table_len, slabs):
    fan, edge_w, rows = e.shape
    feat = d2.shape[0]
    cap = sel.shape[1] // n
    places = n // 2
    whole = lambda a: pl.BlockSpec(a.shape, lambda i: (0,) * a.ndim)
    slab = lambda f: pl.BlockSpec((slabs, f, rows), lambda i: (i, 0, 0))
    anywhere = pl.BlockSpec(memory_space=pl.ANY)
    consts = (nbr, d2, mid, win, x, far_x, dfirst, vectors, sel)
    roomy = table_len <= ROOMY
    place = pltpu.VMEM if roomy else pltpu.HBM
    sources = [pltpu.with_memory_space_constraint(c, place) for c in sources]
    depths = [s.shape[1] for s in sources] + list(late_depths)
    scratch = [pltpu.VMEM((feat, feat), F32), pltpu.VMEM((table_len + edge_w, feat), F32), pltpu.VMEM((feat, rows), F32)]
    scratch += [pltpu.VMEM((n, cap, feat), BF16)] * 2 + [pltpu.SemaphoreType.DMA((n,))] * 2
    scratch += [pltpu.VMEM((16, d, LANES), BF16) for d in late_depths]
    for d in depths:
        scratch += chunk_scratch(places, d)
    return pl.pallas_call(
        functools.partial(message_backward_body, n, table_len, slabs, len(sources), len(late_depths)),
        grid=(fan // slabs,),
        in_specs=[slab(edge_w), slab(feat), slab(feat), slab(feat), slab(edge_w), slab(1)] + [whole(a) for a in consts]
        + [anywhere] * len(sources),
        out_specs=[slab(edge_w), whole(x)] + [anywhere] * len(depths),
        out_shape=[place(e.shape, BF16), place(x.shape, F32)]
        + [place((16, d, LANES), BF16) for d in depths],
        scratch_shapes=scratch,
        compiler_params=pltpu.CompilerParams(vmem_limit_bytes=(42 if roomy else 58) * 1024 * 1024, collective_id=3, has_side_effects=True),
        name="message_backward",
    )(e, h1, gp1, gp2, part, keep, *consts, *sources)


def unpack_body(early, late, feat, hidden, edge_w, *refs):
    count = early + late
    sources, refs = refs[:count], refs[count:]
    (egrad, grad, node), refs = refs[:3], refs[3:]
    (gwin, gmid, gmout, gexp, gcon, guin, egrad_out, grad_out, node_out, gumid, guout), refs = refs[:11], refs[11:]
    vectors_out, refs = refs[:6], refs[6:]
    held = sources
    (swin, smid, smout, sexp, scon, suin, segrad), send = refs[:7], refs[7]
    at = early_rows(feat, hidden, edge_w)
    sent = []

    def push(source, target):
        copy = pltpu.make_async_copy(source, target, send.at[len(sent)])
        copy.start()
        sent.append(copy)

    push(grad, grad_out)
    push(node, node_out)

    def section(bufs, row, size, width, target, top=0, left=0, lane=0):
        for value, offset in unpack(bufs, row, size, LANES):
            target[top + offset : top + offset + value.shape[0], left : left + width] = value[:, lane : lane + width].astype(F32)

    front, back = held[:early], held[early:]
    for b in range(hidden // feat):
        section(front, at["contract"] + b * feat, feat, feat, scon, top=b * feat)
        push(scon.at[pl.ds(b * feat, feat)], gcon.at[pl.ds(b * feat, feat)])
    for b in range(hidden // feat):
        section(front, at["expand"] + b * feat, feat, feat, sexp, left=b * feat)
        push(sexp.at[:, pl.ds(b * feat, feat)], gexp.at[:, pl.ds(b * feat, feat)])
    section(front, at["message_out"], feat, feat, smout)
    push(smout, gmout)
    section(front, at["update_self"], edge_w, feat, suin)
    section(front, at["update_neigh"], edge_w, feat, suin, left=feat)
    section(front, at["update_edge"], edge_w, edge_w, suin, left=2 * feat)
    push(suin, guin)
    section(front, at["update_edge"], edge_w, edge_w, gumid, lane=256)
    section(front, at["update_out"], edge_w, edge_w, guout)
    vectors = unpack(back[:1], feat + edge_w, 16, LANES)[0][0].astype(F32)
    for k in range(6):
        size = vectors_out[k].shape[0]
        vectors_out[k][...] = vectors[k : k + 1, :size].reshape(size)
    section(back[:1], 0, feat, feat, smid)
    push(smid, gmid)
    section(back[:1], feat, edge_w, feat, swin, top=2 * feat)
    section(back[1:], 0, 2 * feat, feat, swin)
    push(swin, gwin)
    slab = egrad.shape[0] // 4
    for b in range(4):
        for k in range(b * slab, (b + 1) * slab):
            segrad[k] = egrad[k].astype(F32)
        push(segrad.at[pl.ds(b * slab, slab)], egrad_out.at[pl.ds(b * slab, slab)])
    for copy in sent:
        copy.wait()


def unpack_all(chunks, egrad, grad, node, early, feat, hidden, edge_w, roomy):
    whole, anywhere = pl.BlockSpec(memory_space=pltpu.VMEM), pl.BlockSpec(memory_space=pl.ANY)
    big = [(2 * feat + edge_w, feat), (feat, feat), (feat, feat), (feat, hidden), (hidden, feat), (edge_w, 2 * feat + edge_w), egrad.shape]
    small = [(edge_w, edge_w), (edge_w, edge_w), (feat,), (feat,), (feat,), (feat,), (edge_w,), (edge_w,)]
    shapes = [jax.ShapeDtypeStruct(s, F32) for s in big] + [jax.ShapeDtypeStruct(grad.shape, F32), jax.ShapeDtypeStruct(node.shape, BF16)]
    return pl.pallas_call(
        functools.partial(unpack_body, early, len(chunks) - early, feat, hidden, edge_w),
        in_specs=[whole] * (len(chunks) + 3),
        out_specs=[anywhere] * 9 + [whole] * 8,
        out_shape=shapes + [jax.ShapeDtypeStruct(s, F32) for s in small],
        scratch_shapes=[pltpu.VMEM(s, F32) for s in big]
        + [pltpu.SemaphoreType.DMA((24,))],
        compiler_params=pltpu.CompilerParams(vmem_limit_bytes=(30 if roomy else 46) * 1024 * 1024),
        name="unpack_all",
    )(*chunks, egrad, grad, node)


def local(n, node_feats, edge_feats, node_cotan, edge_cotan, neighbour, edge_mask, fetch_rows, chain_ids, complex_flag, message_in,
          message_mid, message_out, gain_node, offset_node, expand_weight, contract_weight, gain_ffn, offset_ffn, update_in, update_mid,
          update_out, gain_edge, offset_edge):
    x = node_feats[0]
    rows, feat = x.shape
    fan = neighbour.shape[1]
    edge_w = edge_feats.shape[3]
    e = jnp.transpose(edge_feats[0], (1, 2, 0))
    cot = jnp.transpose(edge_cotan[0], (1, 2, 0))
    nbr = jnp.transpose(neighbour)
    mask = jnp.transpose(edge_mask)
    uin = jnp.transpose(update_in)
    lhs, self_t, mid_t, umid_t, uout_t, uedge, sel, tag, gain_t, offset_t, far_x = table_rows(
        n, fetch_rows[0], x, chain_ids, complex_flag, message_in, message_mid, update_mid, update_out, uin, gain_edge, offset_edge
    )
    table_len = lhs.shape[1] - edge_w
    fit = lambda *options: next(c for c in options + (6, 4, 2, 1) if fan % c == 0)
    slabs = fit(10)
    h1, gp1, gp2, s, keep, cnt = message_forward(e, nbr, mask, tag, lhs, self_t, mid_t, slabs)
    node, lhs3, self3, n1, r1, n2, r2, acted, slope = node_forward(
        n, s, cnt, x, message_out, gain_node, offset_node, expand_weight, contract_weight, gain_ffn, offset_ffn,
        sel, uin
    )
    edge_new, part, guout, gumid, gin3, dself3, ggain, goff = edge_pass(
        e, cot, nbr, lhs3, self3, umid_t, uout_t, update_mid, update_out, uedge, gain_t, offset_t, fit(20, 10)
    )
    hidden = expand_weight.shape[1]
    early_depths, late_depths = chunk_plan(n // 2, early_rows(feat, hidden, edge_w)["end"], feat + edge_w + 16, 2 * feat)
    dfirst, d2, sums, *sources = node_backward(
        n, gin3, dself3, sel, node, node_cotan[0], uin, n1, r1, n2, r2, acted, slope, gain_node, offset_node, gain_ffn,
        expand_weight, contract_weight, s, cnt, message_out, ggain, goff, gumid, guout, early_depths
    )
    egrad, ngrad, *sums = message_backward(
        n, e, h1, gp1, gp2, part, keep, nbr, d2, message_mid, message_in, x, far_x, dfirst, sums, sel, sources, late_depths, table_len, slabs
    )
    gwin, gmid, gmout, gexp, gcon, guin, egrad, ngrad, node, gumid, guout, gnode, onode, gffn, offn, gedge, oedge = unpack_all(
        sums, egrad, ngrad, node, len(sources), feat, hidden, edge_w, table_len <= ROOMY
    )
    native = lambda a: jnp.transpose(a, (2, 0, 1))[None]
    return (node[None], native(edge_new), ngrad[None], native(egrad), gwin, gmid, gmout, gnode, onode, gexp, gcon, gffn, offn,
            jnp.transpose(guin), gumid, guout, gedge, oedge)


def solution(mesh):
    grouped, placed, copied = P("tm", "res", None), P("res", None), P()
    wide = P("tm", "res", None, None)
    arguments = (grouped, wide, grouped, wide, placed, placed, P("res", None, None), P("res"), P("res")) + (copied,) * 14
    return jax.shard_map(
        functools.partial(local, mesh.shape["res"]),
        mesh=mesh,
        in_specs=arguments,
        out_specs=(grouped, wide, grouped, wide) + (copied,) * 14,
        check_vma=False,
    )
```

```python
import functools
import jax
import jax.numpy as jnp
from jax import lax
from jax.experimental import pallas as pl
from jax.experimental.pallas import tpu as pltpu
from jax.sharding import PartitionSpec as P

EPSILON = 1e-05
CURVE = 0.7978845608028654
CUBIC = 0.044715
F32 = jnp.float32
BF16 = jnp.bfloat16
VMEM_LIMIT = 60 * 1024 * 1024
MESH = pl.DeviceIdType.MESH


def nn(a, b):
    return lax.dot_general(a, b, (((1,), (0,)), ((), ())), preferred_element_type=F32)


def nt(a, b):
    return lax.dot_general(a, b, (((1,), (1,)), ((), ())), preferred_element_type=F32)


def tn(a, b):
    return lax.dot_general(a, b, (((0,), (0,)), ((), ())), preferred_element_type=F32)


def narrow_gelu(v):
    v = v.astype(BF16)
    square = v * v
    t = jnp.tanh(v * (BF16(CURVE) + BF16(CURVE * CUBIC) * square))
    half = BF16(0.5) + BF16(0.5) * t
    slope = half + (half - half * half) * (v * (BF16(2.0 * CURVE) + BF16(6.0 * CURVE * CUBIC) * square))
    return v * half, slope


def gelu_parts(v):
    square = v * v
    t = jnp.tanh(v * (CURVE + (CURVE * CUBIC) * square))
    half = 0.5 + 0.5 * t
    slope = half + (half - half * half) * (v * (2.0 * CURVE + (6.0 * CURVE * CUBIC) * square))
    return v * half, slope


def tile_lanes(block, count):
    return jnp.concatenate([block] * count, axis=1) if count > 1 else block


def edge_operand(table_len, slabs, base, e_ref, nbr_ref):
    columns = []
    for j in range(slabs):
        row = nbr_ref[pl.ds(base + j, 1), :]
        ids = lax.broadcasted_iota(jnp.int16, (table_len, row.shape[1]), 0)
        hot = jnp.where(ids == jnp.broadcast_to(row, (16, row.shape[1])).astype(jnp.int16)[:1], BF16(1.0), BF16(0.0))
        columns.append(jnp.concatenate([hot, e_ref[j]], axis=0))
    return jnp.concatenate(columns, axis=1) if slabs > 1 else columns[0]


def message_forward_body(table_len, feat, slabs, e_ref, nbr_ref, mask_ref, own_ref, lhs_ref, self_ref, mid_ref,
                         h1_ref, gp1_ref, gp2_ref, s_ref, keep_ref, cnt_ref):
    step = pl.program_id(0)
    base = step * slabs
    rows = nbr_ref.shape[1]

    @pl.when(step == 0)
    def _():
        s_ref[...] = jnp.zeros_like(s_ref)
        cnt_ref[...] = jnp.zeros_like(cnt_ref)

    own = own_ref[...]
    own_chain = own // 2
    own_flag = own % 2
    pre = nn(lhs_ref[...], edge_operand(table_len, slabs, base, e_ref, nbr_ref))
    hidden, slope = narrow_gelu(pre[:feat] + tile_lanes(self_ref[...], slabs))
    total = s_ref[...]
    count = cnt_ref[...]
    keeps = []
    for j in range(slabs):
        cut = slice(j * rows, (j + 1) * rows)
        h1_ref[j] = hidden[:, cut]
        gp1_ref[j] = slope[:, cut]
        other = pre[feat : feat + 1, cut].astype(jnp.int32)
        joined = jnp.logical_or(own_chain == other // 2, own_flag * (other % 2) > 0)
        keep = jnp.where(joined, 1.0, 0.0) * mask_ref[pl.ds(base + j, 1), :].astype(F32)
        keep_ref[j] = keep
        keeps.append(keep)
        count = count + keep
    hidden, slope = narrow_gelu(nn(mid_ref[...], hidden))
    hidden = hidden.astype(F32)
    for j in range(slabs):
        cut = slice(j * rows, (j + 1) * rows)
        gp2_ref[j] = slope[:, cut]
        total = total + hidden[:, cut] * keeps[j]
    s_ref[...] = total
    cnt_ref[...] = count


def message_forward(e, nbr, mask, own_tag, lhs, self_t, mid_t, slabs):
    fan, edge_w, rows = e.shape
    feat = self_t.shape[0]
    table_len = lhs.shape[1] - edge_w
    whole = lambda a: pl.BlockSpec(a.shape, lambda i: (0,) * a.ndim)
    slab = lambda f: pl.BlockSpec((slabs, f, rows), lambda i: (i, 0, 0))
    big = pltpu.HBM((fan, feat, rows), BF16)
    e, nbr, mask = far_off(e, nbr, mask)
    return pl.pallas_call(
        functools.partial(message_forward_body, table_len, feat, slabs),
        grid=(fan // slabs,),
        in_specs=[slab(edge_w), whole(nbr), whole(mask), whole(own_tag), whole(lhs), whole(self_t), whole(mid_t)],
        out_specs=[slab(feat), slab(feat), slab(feat), pl.BlockSpec((feat, rows), lambda i: (0, 0)), slab(1),
                   pl.BlockSpec((1, rows), lambda i: (0, 0))],
        out_shape=[big, big, big, jax.ShapeDtypeStruct((feat, rows), F32), pltpu.HBM((fan, 1, rows), F32),
                   jax.ShapeDtypeStruct((1, rows), F32)],
        compiler_params=pltpu.CompilerParams(vmem_limit_bytes=30 * 1024 * 1024),
        name="message_forward",
    )(e, nbr, mask, own_tag, lhs, self_t, mid_t)


def edge_body(table_len, slabs, e_ref, cot_ref, nbr_ref, lhs_ref, self_ref, mid_t_ref, out_t_ref, mid_ref, out_ref, edge_ref,
              gain_ref, offset_ref,
              new_ref, part_ref, gout_ref, gmid_ref, gin_ref, dself_ref, ggain_ref, goff_ref):
    step = pl.program_id(0)
    base = step * slabs
    rows = nbr_ref.shape[1]

    @pl.when(step == 0)
    def _():
        for ref in (gout_ref, gmid_ref, gin_ref, dself_ref, ggain_ref, goff_ref):
            ref[...] = jnp.zeros_like(ref)

    x = edge_operand(table_len, slabs, base, e_ref, nbr_ref)
    self_t = tile_lanes(self_ref[...], slabs)
    hidden_three, slope_three = narrow_gelu(nn(lhs_ref[...], x) + self_t)
    hidden_four, slope_four = narrow_gelu(nn(mid_t_ref[...], hidden_three))
    branch = nn(out_t_ref[...], hidden_four)
    gain = gain_ref[...]
    offset = offset_ref[...]
    scale = 1.0 / e_ref.shape[1]
    resid = []
    ggain = ggain_ref[...]
    goff = goff_ref[...]
    for j in range(slabs):
        z = e_ref[j].astype(F32) + branch[:, j * rows : (j + 1) * rows]
        z = z - jnp.sum(z, axis=0, keepdims=True) * scale
        r = lax.rsqrt(jnp.sum(z * z, axis=0, keepdims=True) * scale + EPSILON)
        h = z * r
        new_ref[j] = (h * gain + offset).astype(BF16)
        dy = cot_ref[j].astype(F32)
        ggain = ggain + dy * h
        goff = goff + dy
        dh = dy * gain
        one = jnp.sum(dh, axis=0, keepdims=True) * scale
        two = jnp.sum(dh * h, axis=0, keepdims=True) * scale
        resid.append(r * (dh - one - h * two))
    ggain_ref[...] = ggain
    goff_ref[...] = goff
    resid = jnp.concatenate(resid, axis=1) if slabs > 1 else resid[0]
    delta = resid.astype(BF16)
    gout_ref[...] += nt(hidden_four, delta)
    delta_four = (nn(out_ref[...], delta) * slope_four.astype(F32)).astype(BF16)
    gmid_ref[...] += nt(hidden_three, delta_four)
    delta_three = nn(mid_ref[...], delta_four) * slope_three.astype(F32)
    low = delta_three.astype(BF16)
    gin_ref[...] += nt(x, low)
    part = resid + nn(edge_ref[...], low)
    dself = dself_ref[...]
    for j in range(slabs):
        cut = slice(j * rows, (j + 1) * rows)
        part_ref[j] = part[:, cut]
        dself = dself + low[:, cut].astype(F32)
    dself_ref[...] = dself


def edge_pass(e, cot, nbr, lhs, self_t, mid_t, out_t, mid, out, edge, gain, offset, slabs):
    fan, edge_w, rows = e.shape
    table_len = lhs.shape[1] - edge_w
    whole = lambda a: pl.BlockSpec(a.shape, lambda i: (0,) * a.ndim)
    slab = pl.BlockSpec((slabs, edge_w, rows), lambda i: (i, 0, 0))
    keep = lambda *s: (pl.BlockSpec(s, lambda i: (0,) * len(s)), jax.ShapeDtypeStruct(s, F32))
    sums = [keep(edge_w, edge_w), keep(edge_w, edge_w), keep(table_len + edge_w, edge_w), keep(edge_w, rows), keep(edge_w, rows),
            keep(edge_w, rows)]
    e, cot, nbr, mid, out = far_off(e, cot, nbr, mid, out)
    consts = (nbr, lhs, self_t, mid_t, out_t, mid, out, edge, gain, offset)
    return pl.pallas_call(
        functools.partial(edge_body, table_len, slabs),
        grid=(fan // slabs,),
        in_specs=[slab, slab] + [whole(a) for a in consts],
        out_specs=[slab, slab] + [s for s, _ in sums],
        out_shape=[pltpu.HBM(e.shape, BF16), pltpu.HBM(e.shape, F32)] + [s for _, s in sums],
        compiler_params=pltpu.CompilerParams(vmem_limit_bytes=42 * 1024 * 1024),
        name="edge_pass",
    )(e, cot, *consts)


LANES = 512


def spot():
    group, place = lax.axis_index("tm"), lax.axis_index("res")
    return group, place, lax.rem(place, 2), place // 2, lax.rem(group, 2), group // 2


def grain(places):
    return 16 * max(1, places // 4)


def piece(places, depth, index):
    across = min(places, 4)
    rows, wide = piece_shape(places, depth)
    top = pl.multiple_of((index // across) * rows, rows)
    left = pl.multiple_of(lax.rem(index, across) * wide, wide)
    return pl.ds(top, rows), pl.ds(left, wide)


def piece_shape(places, depth):
    across = min(places, 4)
    return depth // (places // across), LANES // across


def remote(source, target, send, recv, group, place):
    return pltpu.make_async_remote_copy(
        src_ref=source, dst_ref=target, send_sem=send, recv_sem=recv, device_id={"tm": group, "res": place}, device_id_type=MESH
    )


class Chunk:
    def __init__(self, places, source, result, acc, from_core, from_first, from_second, from_line, stage, out, sends, recvs, local):
        self.places, self.source, self.result, self.acc = places, source, result, acc
        self.from_core, self.from_first, self.from_second = from_core, from_first, from_second
        self.from_line, self.stage, self.out = from_line, stage, out
        self.sends, self.recvs, self.local = sends, recvs, local
        self.depth = acc.shape[1]

    def run(self, stage):
        (self.spread, self.halve, self.quarter, self.scatter, self.settle, self.gather, self.widen, self.share, self.store,
         self.close)[stage]()

    def link(self, slot, source, target, group, place):
        return functools.partial(remote, source, target, self.sends.at[slot], self.recvs.at[slot], group, place)

    def core_copy(self):
        group, place, core, lane, x, y = spot()
        theirs = pl.multiple_of((1 - core) * 8, 8)
        return self.link(0, self.source.at[pl.ds(theirs, 8)], self.from_core, group, place + 1 - 2 * core)

    def load_copy(self):
        core = spot()[2]
        return pltpu.make_async_copy(self.source.at[pl.ds(pl.multiple_of(core * 8, 8), 8)], self.acc, self.local.at[0])

    def half_copies(self):
        group, place, core, lane, x, y = spot()
        return [
            self.link(1, self.acc.at[pl.ds((1 - x) * 2, 2)], self.from_first.at[pl.ds(0, 2)], group + 1 - 2 * x, place),
            self.link(2, self.acc.at[pl.ds(4 + (1 - y) * 2, 2)], self.from_first.at[pl.ds(2, 2)], group + 2 - 4 * y, place),
        ]

    def quarter_copies(self):
        group, place, core, lane, x, y = spot()
        return [
            self.link(3, self.acc.at[x * 2 + 1 - y], self.from_second.at[0], group + 2 - 4 * y, place),
            self.link(4, self.acc.at[4 + y * 2 + 1 - x], self.from_second.at[1], group + 1 - 2 * x, place),
        ]

    def line_copies(self):
        group, place, core, lane, x, y = spot()
        copies = []
        for s in range(1, self.places):
            ahead, behind = lax.rem(lane + s, self.places), lax.rem(lane + self.places - s, self.places)
            rows, wide = piece(self.places, self.depth, ahead)
            view = self.stage.at[:, rows, wide]
            copies.append((self.link(4 + s, view, self.from_line.at[lane], group, ahead * 2 + core),
                           self.link(4 + s, view, self.from_line.at[behind], group, behind * 2 + core)))
        return copies

    def own(self):
        group, place, core, lane, x, y = spot()
        return core * 8 + x * 2 + y, core * 8 + 4 + y * 2 + x

    def spread_copies(self):
        group, place, core, lane, x, y = spot()
        copies = []
        slot = 4 + self.places
        for own in self.own():
            for s in range(1, self.places):
                ahead, behind = lax.rem(lane + s, self.places), lax.rem(lane + self.places - s, self.places)
                rows, wide = piece(self.places, self.depth, lane)
                back_rows, back_wide = piece(self.places, self.depth, behind)
                view, back = self.out.at[own, rows, wide], self.out.at[own, back_rows, back_wide]
                copies.append((self.link(slot, view, view, group, ahead * 2 + core), self.link(slot, back, back, group, behind * 2 + core)))
                slot += 1
        return copies

    def both(self, slot, view, back, group, place):
        return self.link(slot, view, view, group, place), self.link(slot, back, back, group, place)

    def gather_copies(self):
        group, place, core, lane, x, y = spot()
        slot = 2 + 3 * self.places
        first, second = self.own()
        return [
            self.both(slot, self.out.at[first], self.out.at[core * 8 + x * 2 + 1 - y], group + 2 - 4 * y, place),
            self.both(slot + 1, self.out.at[second], self.out.at[core * 8 + 4 + y * 2 + 1 - x], group + 1 - 2 * x, place),
        ]

    def widen_copies(self):
        group, place, core, lane, x, y = spot()
        slot = 4 + 3 * self.places
        two = lambda start: self.out.at[pl.ds(start, 2)]
        return [
            self.both(slot, two(core * 8 + x * 2), two(core * 8 + 2 - x * 2), group + 1 - 2 * x, place),
            self.both(slot + 1, two(core * 8 + 4 + y * 2), two(core * 8 + 6 - y * 2), group + 2 - 4 * y, place),
        ]

    def share_copy(self):
        group, place, core, lane, x, y = spot()
        eight = lambda which: self.out.at[pl.ds(pl.multiple_of(which * 8, 8), 8)]
        return self.both(6 + 3 * self.places, eight(core), eight(1 - core), group, place + 1 - 2 * core)

    def store_copy(self, which, slot):
        eight = pl.ds(pl.multiple_of(which * 8, 8), 8)
        return pltpu.make_async_copy(self.out.at[eight], self.result.at[eight], self.local.at[slot])

    def spread(self):
        self.core_copy()().start()
        self.load_copy().start()

    def halve(self):
        group, place, core, lane, x, y = spot()
        self.load_copy().wait()
        self.core_copy()().wait()
        acc, extra = self.acc, self.from_core
        give = [(1 - x) * 2, 4 + (1 - y) * 2]
        keep = [x * 2, 4 + y * 2]
        for start in give:
            for i in range(2):
                acc[start + i] = acc[start + i] + extra[start + i]
        for copy in self.half_copies():
            copy().start()
        for start in keep:
            for i in range(2):
                acc[start + i] = acc[start + i] + extra[start + i]

    def quarter(self):
        group, place, core, lane, x, y = spot()
        for copy in self.half_copies():
            copy().wait()
        acc, extra = self.acc, self.from_first
        acc[x * 2 + 1 - y] = acc[x * 2 + 1 - y] + extra[1 - y]
        acc[4 + y * 2 + 1 - x] = acc[4 + y * 2 + 1 - x] + extra[3 - x]
        for copy in self.quarter_copies():
            copy().start()
        self.stage[0] = acc[x * 2 + y] + extra[y]
        self.stage[1] = acc[4 + y * 2 + x] + extra[2 + x]

    def scatter(self):
        for copy in self.quarter_copies():
            copy().wait()
        for s in range(2):
            self.stage[s] = self.stage[s] + self.from_second[s]
        for send, arrive in self.line_copies():
            send().start()

    def settle(self):
        group, place, core, lane, x, y = spot()
        rows, wide = piece(self.places, self.depth, lane)
        total = self.stage[:, rows, wide].astype(F32)
        pairs = self.line_copies()
        for s in range(1, self.places):
            pairs[s - 1][1]().wait_recv()
            total = total + self.from_line[lax.rem(lane + self.places - s, self.places)].astype(F32)
        first, second = self.own()
        total = total.astype(BF16)
        self.out[first, rows, wide] = total[0]
        self.out[second, rows, wide] = total[1]
        for send, arrive in self.spread_copies():
            send().start()
        for send, arrive in pairs:
            send().wait_send()

    def finish(self, pairs):
        for send, arrive in pairs:
            arrive().wait_recv()
        for send, arrive in pairs:
            send().wait_send()

    def gather(self):
        self.finish(self.spread_copies())
        for send, arrive in self.gather_copies():
            send().start()

    def widen(self):
        self.finish(self.gather_copies())
        for send, arrive in self.widen_copies():
            send().start()

    def share(self):
        core = spot()[2]
        self.finish(self.widen_copies())
        self.share_copy()[0]().start()
        self.store_copy(core, 1).start()

    def store(self):
        core = spot()[2]
        self.share_copy()[1]().wait_recv()
        self.store_copy(1 - core, 2).start()

    def close(self):
        core = spot()[2]
        self.share_copy()[0]().wait_send()
        self.store_copy(core, 1).wait()
        self.store_copy(1 - core, 2).wait()


CHUNK_REFS = 10
ROOMY = 512


def chunk_scratch(places, depth):
    rows, wide = piece_shape(places, depth)
    shapes = [(8, depth, LANES), (8, depth, LANES), (4, depth, LANES), (2, depth, LANES), (places, 2, rows, wide), (2, depth, LANES),
              (16, depth, LANES)]
    links = 7 + 3 * places
    return [pltpu.VMEM(s, BF16) for s in shapes] + [pltpu.SemaphoreType.DMA((links,))] * 2 + [pltpu.SemaphoreType.DMA((3,))]


def greet_all(n):
    group, place, core, lane, x, y = spot()
    barrier = pltpu.get_barrier_semaphore()
    partners = [(group + 1 - 2 * x, place), (group + 2 - 4 * y, place)]
    partners += [(group, lax.rem(place + s, n)) for s in range(1, n)]
    for near, far in partners:
        pl.semaphore_signal(barrier, inc=1, device_id={"tm": near, "res": far}, device_id_type=MESH)


def chunk_plan(places, early_rows, late_first, late_second):
    unit = grain(places)
    depth = lambda rows: -(-rows // (16 * unit)) * unit
    total = depth(early_rows)
    steps = total // unit
    return [(steps + k) // 4 * unit for k in range(4)], [depth(late_first), depth(late_second)]


def pack(bufs, row, value):
    start = 0
    value = value.astype(BF16)
    for buf in bufs:
        size = buf.shape[0] * buf.shape[1]
        depth = buf.shape[1]
        low, high = max(row, start), min(row + value.shape[0], start + size)
        while low < high:
            slot, inner = divmod(low - start, depth)
            step = min(high - low, depth - inner)
            buf[slot, inner : inner + step, : value.shape[1]] = value[low - row : low - row + step]
            low += step
        start += size


def fill(bufs, row, values):
    for value in values:
        pack(bufs, row, value)
        row += value.shape[0]
    spare = sum(b.shape[0] * b.shape[1] for b in bufs) - row
    if spare:
        pack(bufs, row, jnp.zeros((spare, bufs[0].shape[2]), F32))


def unpack(bufs, row, count, width):
    pieces = []
    start = 0
    for buf in bufs:
        depth = buf.shape[1]
        size = buf.shape[0] * depth
        low, high = max(row, start), min(row + count, start + size)
        while low < high:
            slot, inner = divmod(low - start, depth)
            step = min(high - low, depth - inner)
            pieces.append((buf[slot, inner : inner + step, : width], low - row))
            low += step
        start += size
    return pieces


def ring_place(n):
    me = lax.axis_index("res")
    return me, [lax.rem(me + s, n) for s in range(n)]


def greet_start(peers):
    barrier = pltpu.get_barrier_semaphore()
    for peer in peers[1:]:
        pl.semaphore_signal(barrier, inc=1, device_id={"res": peer}, device_id_type=MESH)


def greet_end(peers):
    pl.semaphore_wait(pltpu.get_barrier_semaphore(), len(peers) - 1)


def copy_to(peer, source, target, send, recv):
    return pltpu.make_async_remote_copy(
        src_ref=source, dst_ref=target, send_sem=send, recv_sem=recv, device_id={"res": peer}, device_id_type=MESH
    )


def swap(n, me, peers, source, target, send, recv, placed=False):
    view = lambda s: source.at[peers[s] if placed else s]
    sent = [copy_to(peers[s], view(s), target.at[me], send.at[s], recv.at[me]) for s in range(1, n)]
    back = [copy_to(peers[s], view(s), target.at[peers[s]], send.at[s], recv.at[peers[s]]) for s in range(1, n)]
    return sent, back


def row_norm(values):
    values = values - jnp.mean(values, axis=1, keepdims=True)
    r = lax.rsqrt(jnp.mean(values * values, axis=1, keepdims=True) + EPSILON)
    return values * r, r


def row_norm_back(dh, h, r):
    return r * (dh - jnp.mean(dh, axis=1, keepdims=True) - h * jnp.mean(dh * h, axis=1, keepdims=True))


def table_rows_body(n, fetch_ref, x_ref, chain_ref, flag_ref, win_hbm, mid_hbm, umid_hbm, uout_hbm, uin_hbm, gain_ref, off_ref,
                    lhs_ref, self_ref, midt_ref, umidt_ref, uoutt_ref, uedge_ref, sel_ref, tag_ref, gaint_ref, offt_ref, far_ref,
                    idx_out, idx_in, row_out, far, wants, asked, win_ref, mid_ref, umid_ref, uout_ref, uin_ref, send_a, recv_a, send_b, recv_b,
                    load):
    me, peers = ring_place(n)
    greet_start(peers)
    pairs = ((win_hbm, win_ref), (mid_hbm, mid_ref), (umid_hbm, umid_ref), (uout_hbm, uout_ref), (uin_hbm, uin_ref))
    loads = [pltpu.make_async_copy(pairs[k][0], pairs[k][1], load.at[k]) for k in range(5)]
    for copy in loads:
        copy.start()
    rows, feat = x_ref.shape
    cap = fetch_ref.shape[1]
    edge_w = win_ref.shape[0] - 2 * feat
    tag = chain_ref[...].reshape(1, rows) * 2 + flag_ref[...].reshape(1, rows)
    tag_ref[...] = tag
    for s in range(n):
        idx_out[s] = jnp.full((8, 128), -1, jnp.int32)
        idx_out[s, 0:1, 0:cap] = fetch_ref[pl.ds(peers[s], 1), :]
        idx_out[s, 1:2, 0:rows] = tag
    greet_end(peers)
    sent, back = swap(n, me, peers, idx_out, idx_in, send_a, recv_a)
    for copy in sent:
        copy.start()
    idx_in[me] = idx_out[0]
    x = x_ref[...]
    for p in range(n):
        wants[0:1, p * cap : (p + 1) * cap] = fetch_ref[p : p + 1, :]
    loads[0].wait()
    self_ref[...] = jnp.transpose(nn(x, win_ref[:feat, :]))

    copies, backs = swap(n, me, peers, row_out, far, send_b, recv_b, True)
    for copy in back:
        copy.wait_recv()
    for p in range(n):
        asked[0:1, p * cap : (p + 1) * cap] = idx_in[p, 0:1, 0:cap]
    spots = lax.broadcasted_iota(jnp.int32, (rows, n * cap), 0)
    hot = jnp.where(spots + me * rows == asked[...], 1.0, 0.0).astype(BF16)
    row_out[...] = tn(hot, x).astype(BF16).reshape(n, cap, feat)
    for copy in copies:
        copy.start()
    sel_ref[...] = hot
    far[me] = row_out[me]
    for copy in loads[1:]:
        copy.wait()
    midt_ref[...] = jnp.transpose(mid_ref[...])
    umidt_ref[...] = jnp.transpose(umid_ref[...])
    uoutt_ref[...] = jnp.transpose(uout_ref[...])
    uedge_ref[...] = jnp.transpose(uin_ref[:, 2 * feat :])
    for source, target in ((gain_ref, gaint_ref), (off_ref, offt_ref)):
        target[...] = jnp.transpose(jnp.broadcast_to(source[...].astype(F32).reshape(1, edge_w), (rows, edge_w)))
    neigh = win_ref[feat : 2 * feat, :]
    extra = lhs_ref.shape[0] - feat
    table_len = rows + n * cap
    lhs_ref[feat:, table_len:] = jnp.zeros((extra, edge_w), BF16)
    lhs_ref[:feat, table_len:] = jnp.transpose(win_ref[2 * feat :, :])
    lhs_ref[:feat, :rows] = jnp.transpose(nn(x, neigh)).astype(BF16)
    lhs_ref[feat:, :rows] = jnp.broadcast_to(tag.astype(F32), (extra, rows)).astype(BF16)
    tags = jnp.concatenate([idx_in[p, 1:2, 0:rows] for p in range(n)] + [jnp.zeros((-n % 16, rows), jnp.int32)] * (n % 16 > 0), axis=0)
    want = wants[...]
    picked = nn(tags.astype(F32).astype(BF16), jnp.where(spots == lax.rem(want, rows), 1.0, 0.0).astype(BF16))
    owner = lax.broadcasted_iota(jnp.int32, picked.shape, 0) == want // rows
    far_tag = jnp.sum(jnp.where(owner, picked, 0.0), axis=0, keepdims=True)
    lhs_ref[feat:, rows:table_len] = jnp.broadcast_to(far_tag, (extra, n * cap)).astype(BF16)
    for copy in backs:
        copy.wait_recv()
    got = far[...].reshape(n * cap, feat)
    lhs_ref[:feat, rows:table_len] = jnp.transpose(nn(got, neigh)).astype(BF16)
    far_ref[...] = got
    for copy in sent + copies:
        copy.wait_send()


def far_off(*arrays):
    return [pltpu.with_memory_space_constraint(a, pltpu.HBM) for a in arrays]


def vmem_call(body, args, outs, scratch, collective, name, outside=(), raw=()):
    whole = pl.BlockSpec(memory_space=pltpu.VMEM)
    return pl.pallas_call(
        body,
        out_shape=[pltpu.HBM(s, d) if i in outside else jax.ShapeDtypeStruct(s, d) for i, (s, d) in enumerate(outs)],
        in_specs=[pl.BlockSpec(memory_space=pl.ANY) if i in raw else whole for i in range(len(args))],
        out_specs=[whole] * len(outs),
        scratch_shapes=scratch,
        compiler_params=pltpu.CompilerParams(vmem_limit_bytes=30 * 1024 * 1024, collective_id=collective, has_side_effects=True),
        name=name,
    )(*args)


def table_rows(n, fetch, x, chain, flag, win, mid, umid, uout, uin, gain, off):
    rows, feat = x.shape
    cap = fetch.shape[1]
    edge_w = win.shape[0] - 2 * feat
    table_len = rows + n * cap
    outs = [((feat + 16, table_len + edge_w), BF16), ((feat, rows), F32), (mid.shape, BF16), (umid.shape, BF16), (uout.shape, BF16),
            ((edge_w, edge_w), BF16), ((rows, n * cap), BF16), ((1, rows), jnp.int32), ((edge_w, rows), F32), ((edge_w, rows), F32),
            ((n * cap, feat), BF16)]
    sems = [pltpu.SemaphoreType.DMA((n,))] * 4 + [pltpu.SemaphoreType.DMA((5,))]
    scratch = [pltpu.VMEM((n, 8, 128), jnp.int32)] * 2 + [pltpu.VMEM((n, cap, feat), BF16)] * 2 + [pltpu.VMEM((1, n * cap), jnp.int32)] * 2
    scratch += [pltpu.VMEM(w.shape, BF16) for w in (win, mid, umid, uout, uin)]
    return vmem_call(functools.partial(table_rows_body, n), far_off(fetch, x, chain, flag, win, mid, umid, uout, uin, gain, off), outs,
                     scratch + sems, 0, "table_rows", (10,), range(4, 9))


def node_forward_body(n, s_ref, cnt_ref, x_ref, mout_ref, gain_ref, off_ref, exp_ref, con_ref, gain2_ref, off2_ref, sel_ref, uin_ref,
                      node_ref, lhs_ref, self_ref, h1_ref, r1_ref, h2_ref, r2_ref, acted_ref, slope_ref,
                      row_out, far, send_a, recv_a):
    me, peers = ring_place(n)
    greet_start(peers)
    rows, feat = x_ref.shape
    cap = sel_ref.shape[1] // n
    edge_w = uin_ref.shape[0]
    line = lambda ref: ref[...].astype(F32).reshape(1, feat)
    mean = jnp.transpose(s_ref[...] / jnp.maximum(cnt_ref[...], 1.0))
    upper = mean.astype(BF16)
    lower = (mean - upper.astype(F32)).astype(BF16)
    aggregate = nn(upper, mout_ref[...]) + nn(lower, mout_ref[...])
    h, r = row_norm(x_ref[...].astype(F32) + aggregate)
    h1_ref[...] = h
    r1_ref[...] = r
    first = h * line(gain_ref) + line(off_ref)
    hidden, slope = gelu_parts(nn(first.astype(BF16), exp_ref[...]))
    acted = hidden.astype(BF16)
    acted_ref[...] = acted
    slope_ref[...] = slope
    h, r = row_norm(first + nn(acted, con_ref[...]))
    h2_ref[...] = h
    r2_ref[...] = r
    low = (h * line(gain2_ref) + line(off2_ref)).astype(BF16)
    node_ref[...] = low
    neigh = nt(low, uin_ref[:, feat : 2 * feat])
    packed = neigh.astype(BF16)
    greet_end(peers)
    copies, backs = swap(n, me, peers, row_out, far, send_a, recv_a, True)
    row_out[...] = tn(sel_ref[...], packed).astype(BF16).reshape(n, cap, edge_w)
    for copy in copies:
        copy.start()
    far[me] = row_out[me]
    self_ref[...] = nt(uin_ref[:, :feat], low)
    table_len = rows + n * cap
    lhs_ref[:, :rows] = jnp.transpose(neigh).astype(BF16)
    lhs_ref[:, table_len:] = uin_ref[:, 2 * feat :]
    for copy in backs:
        copy.wait_recv()
    lhs_ref[:, rows:table_len] = jnp.transpose(far[...].reshape(n * cap, edge_w))
    for copy in copies:
        copy.wait_send()


def node_forward(n, s, cnt, x, mout, gain, off, expand, contract, gain2, off2, sel, uin):
    rows, feat = x.shape
    cap = sel.shape[1] // n
    edge_w = uin.shape[0]
    table_len = rows + n * cap
    hidden = expand.shape[1]
    outs = [(x.shape, BF16), ((edge_w, table_len + edge_w), BF16), ((edge_w, rows), F32), (x.shape, F32), ((rows, 1), F32),
            (x.shape, F32), ((rows, 1), F32), ((rows, hidden), BF16), ((rows, hidden), F32)]
    scratch = [pltpu.VMEM((n, cap, edge_w), BF16)] * 2 + [pltpu.SemaphoreType.DMA((n,))] * 2
    return vmem_call(functools.partial(node_forward_body, n),
                     [s, cnt] + far_off(x, mout, gain, off) + [expand, contract] + far_off(gain2, off2) + [sel, uin], outs, scratch, 1,
                     "node_forward")


def swap_back_start(n, me, peers, gin, sel_ref, row_out, far, send, recv, rows):
    cap = sel_ref.shape[1] // n
    copies, backs = swap(n, me, peers, row_out, far, send, recv, True)
    row_out[...] = gin[pl.ds(rows, n * cap), :].astype(BF16).reshape(n, cap, gin.shape[1])
    for copy in copies:
        copy.start()
    far[me] = row_out[me]
    return copies, backs


def swap_back_finish(n, copies, gin, sel_ref, far, rows):
    for copy in copies[1]:
        copy.wait_recv()
    total = gin[:rows, :] + nn(sel_ref[...], far[...].reshape(sel_ref.shape[1], gin.shape[1]))
    for copy in copies[0]:
        copy.wait_send()
    return total.astype(BF16)


def node_backward_body(n, gin_ref, dself_ref, sel_ref, node_ref, cot_ref, uin_ref, h1_ref, r1_ref, h2_ref, r2_ref, acted_ref, slope_ref,
                       gain_ref, off_ref, gain2_ref, exp_ref, con_ref, s_ref, cnt_ref, mout_ref, ggain_ref, goff_ref,
                       gumid_ref, guout_ref, dfirst_ref, d2_ref, vec_ref, *rest):
    chunks, (row_out, far, send_a, recv_a) = rest[:-4], rest[-4:]
    me, peers = ring_place(n)
    rows, feat = node_ref.shape
    edge_w = uin_ref.shape[0]
    greet_start(peers)
    line = lambda ref: ref[...].astype(F32).reshape(1, feat)
    table_len = gin_ref.shape[0] - edge_w
    dself_t = dself_ref[...].astype(BF16)
    dself = jnp.transpose(dself_ref[...]).astype(BF16)
    greet_end(peers)
    copies = swap_back_start(n, me, peers, gin_ref, sel_ref, row_out, far, send_a, recv_a, rows)
    node = node_ref[...]
    at = early_rows(feat, acted_ref.shape[1], edge_w)
    pack(chunks, at["update_self"], nn(dself_t, node))
    gap = jnp.zeros((edge_w, 256 - edge_w), F32)
    pack(chunks, at["update_edge"], jnp.concatenate([jnp.transpose(gin_ref[table_len:, :]), gap, gumid_ref[...], gap], axis=1))
    pack(chunks, at["update_out"], jnp.concatenate([guout_ref[...], jnp.zeros((edge_w, feat - edge_w), F32)], axis=1))
    side = jnp.zeros((1, feat - edge_w), F32)
    edge_sums = [jnp.concatenate([jnp.sum(jnp.transpose(ref[...]), axis=0, keepdims=True), side], axis=1) for ref in (ggain_ref, goff_ref)]
    used = at["end"]
    spare = sum(c.shape[0] * c.shape[1] for c in chunks) - used
    if spare:
        pack(chunks, used, jnp.zeros((spare, feat), F32))
    dy = cot_ref[...].astype(F32) + nn(dself, uin_ref[:, :feat])
    own = swap_back_finish(n, copies, gin_ref, sel_ref, far, rows)
    dy = dy + nn(own, uin_ref[:, feat : 2 * feat])
    pack(chunks, at["update_neigh"], tn(own, node))
    h2 = h2_ref[...]
    ffn_sums = [jnp.sum(dy * h2, axis=0, keepdims=True), jnp.sum(dy, axis=0, keepdims=True)]
    second = row_norm_back(dy * line(gain2_ref), h2, r2_ref[...])
    dffn = second.astype(BF16)
    for b in range(acted_ref.shape[1] // feat):
        pack(chunks, at["contract"] + b * feat, tn(acted_ref[:, b * feat : (b + 1) * feat], dffn))
    dinner = (nt(dffn, con_ref[...]) * slope_ref[...]).astype(BF16)
    h1 = h1_ref[...]
    gain = line(gain_ref)
    first_low = (h1 * gain + line(off_ref)).astype(BF16)
    for b in range(acted_ref.shape[1] // feat):
        pack(chunks, at["expand"] + b * feat, tn(first_low, dinner[:, b * feat : (b + 1) * feat]))
    dy = second + nt(dinner, exp_ref[...])
    sums = [jnp.sum(dy * h1, axis=0, keepdims=True), jnp.sum(dy, axis=0, keepdims=True)] + ffn_sums
    dfirst = row_norm_back(dy * gain, h1, r1_ref[...])
    dfirst_ref[...] = dfirst
    back = (jnp.transpose(dfirst) / jnp.maximum(cnt_ref[...], 1.0)).astype(BF16)
    d2_ref[...] = nn(mout_ref[...], back)
    pack(chunks, at["message_out"], nt(s_ref[...].astype(BF16), back))
    vec_ref[...] = jnp.concatenate(sums + edge_sums + [jnp.zeros((10, feat), F32)], axis=0)


def early_rows(feat, hidden, edge_w):
    at, row = {}, 0
    for name, count in (("contract", hidden), ("expand", hidden), ("message_out", feat), ("update_self", edge_w),
                        ("update_neigh", edge_w), ("update_edge", edge_w), ("update_out", edge_w)):
        at[name] = row
        row += count
    at["end"] = row
    return at


def node_backward(n, gin, dself, sel, node, cot, uin, h1, r1, h2, r2, acted, slope, gain, off, gain2, expand, contract, s, cnt, mout,
                  ggain, goff, gumid, guout, depths):
    rows, feat = node.shape
    cap = sel.shape[1] // n
    edge_w = uin.shape[0]
    outs = [(node.shape, F32), ((feat, rows), F32), ((16, feat), F32)] + [((16, d, LANES), BF16) for d in depths]
    scratch = [pltpu.VMEM((n, cap, edge_w), BF16)] * 2 + [pltpu.SemaphoreType.DMA((n,))] * 2
    return vmem_call(functools.partial(node_backward_body, n),
                     [gin, dself, sel, node, cot, uin, h1, r1, h2, r2, acted, slope] + far_off(gain, off, gain2)
                     + [expand, contract, s, cnt, mout, ggain, goff, gumid, guout], outs, scratch, 2, "node_backward",
                     (0, 1, 2))


EARLY_ORDER = (
    ((0, 0),),
    ((3, 0), (1, 0), (0, 1)),
    (),
    ((1, 1),),
    (),
    ((0, 2),),
    ((2, 0), (1, 2), (3, 1)),
    ((0, 3),),
    ((2, 1), (1, 3)),
    (),
    ((0, 4), (3, 2)),
    (),
)
LATE_ORDER = (
    (2, 2), (1, 4), (0, 5), (4, 1), (5, 0), (2, 3), (5, 1), (3, 3), (0, 6), (1, 5), (2, 4), (4, 2), (5, 2), (3, 4), (1, 6),
    (2, 5), (5, 3), (3, 5), (4, 3), (2, 6), (0, 7), (5, 4), (3, 6), (4, 4), (5, 5), (2, 7), (4, 5), (5, 6), (-1, 0), (3, 7),
    (1, 7), (4, 6), (2, 8), (0, 8), (0, 9), (1, 8), (5, 7), (3, 8), (4, 7), (5, 8), (1, 9), (3, 9), (2, 9), (4, 8), (5, 9),
    (4, 9),
)


def message_backward_body(n, table_len, slabs, early, late, *refs):
    (e_ref, h1_ref, gp1_ref, gp2_ref, part_ref, keep_ref, nbr_ref, d2_ref, mid_ref, win_ref, x_ref, far_ref, dfirst_ref, vec_ref, sel_ref) = refs[:15]
    refs = refs[15:]
    sources, refs = refs[:early], refs[early:]
    egrad_ref, grad_ref, results, refs = refs[0], refs[1], refs[2 : 2 + early + late], refs[2 + early + late :]
    (gmid, gin, dself_sum, row_out, far, send_a, recv_a), refs = refs[:7], refs[7:]
    late_sources, refs = refs[:late], refs[late:]
    places = n // 2
    chunks = [Chunk(places, (list(sources) + list(late_sources))[i], results[i], *refs[CHUNK_REFS * i : CHUNK_REFS * (i + 1)])
              for i in range(early + late)]
    step = pl.program_id(0)
    base = step * slabs
    steps = pl.num_programs(0)
    rows = nbr_ref.shape[1]
    feat = d2_ref.shape[0]

    @pl.when(step == 0)
    def _():
        greet_all(n)
        for ref in (gmid, gin, dself_sum):
            ref[...] = jnp.zeros_like(ref)

    count = nbr_ref.shape[0] // slabs
    def slot(half):
        for at in range(count):
            which = EARLY_ORDER[2 * at + half]
            if which:

                @pl.when(step == at)
                def _(which=which):
                    for i, stage in which:
                        chunks[i].run(stage)

    x = edge_operand(table_len, slabs, base, e_ref, nbr_ref)
    back = d2_ref[...]
    wide = lambda ref: jnp.concatenate([ref[j] for j in range(slabs)], axis=1)
    two = jnp.concatenate([(back * keep_ref[j] * gp2_ref[j].astype(F32)).astype(BF16) for j in range(slabs)], axis=1)
    gmid[...] += nt(wide(h1_ref), two)

    @pl.when(step == 0)
    def _():
        pl.semaphore_wait(pltpu.get_barrier_semaphore(), n + 1)

    slot(0)
    one = (nn(mid_ref[...], two) * wide(gp1_ref).astype(F32)).astype(BF16)
    gin[...] += nt(x, one)
    part = nn(win_ref[2 * feat :, :], one)
    total = dself_sum[...]
    for j in range(slabs):
        cut = slice(j * rows, (j + 1) * rows)
        egrad_ref[j] = (part_ref[j] + part[:, cut]).astype(BF16)
        total = total + one[:, cut].astype(F32)
    dself_sum[...] = total
    slot(1)

    @pl.when(step == steps - 1)
    def _():
        nodes = x_ref[...]
        dself = jnp.transpose(dself_sum[...]).astype(BF16)
        near = gin[:rows, :].astype(BF16)
        beyond = gin[rows:table_len, :].astype(BF16)
        fill(late_sources[:1], 0, [gmid[...], gin[table_len:, :], vec_ref[...]])
        chunks[early].run(0)
        fill(late_sources[1:], 0, [tn(nodes, dself), tn(nodes, near) + tn(far_ref[...], beyond)])
        me, peers = ring_place(n)
        copies = swap_back_start(n, me, peers, gin, sel_ref, row_out, far, send_a, recv_a, rows)
        for i, stage in LATE_ORDER:
            if i < 0:
                own = swap_back_finish(n, copies, gin, sel_ref, far, rows)
                grad_ref[...] = dfirst_ref[...] + nt(dself, win_ref[:feat, :]) + nt(own, win_ref[feat : 2 * feat, :])
            else:
                chunks[i].run(stage)


def message_backward(n, e, h1, gp1, gp2, part, keep, nbr, d2, mid, win, x, far_x, dfirst, vectors, sel, sources, late_depths, table_len, slabs):
    fan, edge_w, rows = e.shape
    feat = d2.shape[0]
    cap = sel.shape[1] // n
    places = n // 2
    whole = lambda a: pl.BlockSpec(a.shape, lambda i: (0,) * a.ndim)
    slab = lambda f: pl.BlockSpec((slabs, f, rows), lambda i: (i, 0, 0))
    anywhere = pl.BlockSpec(memory_space=pl.ANY)
    consts = (nbr, d2, mid, win, x, far_x, dfirst, vectors, sel)
    roomy = table_len <= ROOMY
    place = pltpu.VMEM if roomy else pltpu.HBM
    sources = [pltpu.with_memory_space_constraint(c, place) for c in sources]
    depths = [s.shape[1] for s in sources] + list(late_depths)
    scratch = [pltpu.VMEM((feat, feat), F32), pltpu.VMEM((table_len + edge_w, feat), F32), pltpu.VMEM((feat, rows), F32)]
    scratch += [pltpu.VMEM((n, cap, feat), BF16)] * 2 + [pltpu.SemaphoreType.DMA((n,))] * 2
    scratch += [pltpu.VMEM((16, d, LANES), BF16) for d in late_depths]
    for d in depths:
        scratch += chunk_scratch(places, d)
    return pl.pallas_call(
        functools.partial(message_backward_body, n, table_len, slabs, len(sources), len(late_depths)),
        grid=(fan // slabs,),
        in_specs=[slab(edge_w), slab(feat), slab(feat), slab(feat), slab(edge_w), slab(1)] + [whole(a) for a in consts]
        + [anywhere] * len(sources),
        out_specs=[slab(edge_w), whole(x)] + [anywhere] * len(depths),
        out_shape=[place(e.shape, BF16), place(x.shape, F32)]
        + [place((16, d, LANES), BF16) for d in depths],
        scratch_shapes=scratch,
        compiler_params=pltpu.CompilerParams(vmem_limit_bytes=(42 if roomy else 58) * 1024 * 1024, collective_id=3, has_side_effects=True),
        name="message_backward",
    )(e, h1, gp1, gp2, part, keep, *consts, *sources)


def unpack_body(early, late, feat, hidden, edge_w, *refs):
    count = early + late
    sources, refs = refs[:count], refs[count:]
    (egrad, grad, node), refs = refs[:3], refs[3:]
    (gwin, gmid, gmout, gexp, gcon, guin, egrad_out, grad_out, node_out, gumid, guout), refs = refs[:11], refs[11:]
    vectors_out, refs = refs[:6], refs[6:]
    held = sources
    (swin, smid, smout, sexp, scon, suin, segrad), send = refs[:7], refs[7]
    at = early_rows(feat, hidden, edge_w)
    sent = []

    def push(source, target):
        copy = pltpu.make_async_copy(source, target, send.at[len(sent)])
        copy.start()
        sent.append(copy)

    push(grad, grad_out)
    push(node, node_out)

    def section(bufs, row, size, width, target, top=0, left=0, lane=0):
        for value, offset in unpack(bufs, row, size, LANES):
            target[top + offset : top + offset + value.shape[0], left : left + width] = value[:, lane : lane + width].astype(F32)

    front, back = held[:early], held[early:]
    for b in range(hidden // feat):
        section(front, at["contract"] + b * feat, feat, feat, scon, top=b * feat)
        push(scon.at[pl.ds(b * feat, feat)], gcon.at[pl.ds(b * feat, feat)])
    for b in range(hidden // feat):
        section(front, at["expand"] + b * feat, feat, feat, sexp, left=b * feat)
        push(sexp.at[:, pl.ds(b * feat, feat)], gexp.at[:, pl.ds(b * feat, feat)])
    section(front, at["message_out"], feat, feat, smout)
    push(smout, gmout)
    section(front, at["update_self"], edge_w, feat, suin)
    section(front, at["update_neigh"], edge_w, feat, suin, left=feat)
    section(front, at["update_edge"], edge_w, edge_w, suin, left=2 * feat)
    push(suin, guin)
    section(front, at["update_edge"], edge_w, edge_w, gumid, lane=256)
    section(front, at["update_out"], edge_w, edge_w, guout)
    vectors = unpack(back[:1], feat + edge_w, 16, LANES)[0][0].astype(F32)
    for k in range(6):
        size = vectors_out[k].shape[0]
        vectors_out[k][...] = vectors[k : k + 1, :size].reshape(size)
    section(back[:1], 0, feat, feat, smid)
    push(smid, gmid)
    section(back[:1], feat, edge_w, feat, swin, top=2 * feat)
    section(back[1:], 0, 2 * feat, feat, swin)
    push(swin, gwin)
    slab = egrad.shape[0] // 4
    for b in range(4):
        for k in range(b * slab, (b + 1) * slab):
            segrad[k] = egrad[k].astype(F32)
        push(segrad.at[pl.ds(b * slab, slab)], egrad_out.at[pl.ds(b * slab, slab)])
    for copy in sent:
        copy.wait()


def unpack_all(chunks, egrad, grad, node, early, feat, hidden, edge_w, roomy):
    whole, anywhere = pl.BlockSpec(memory_space=pltpu.VMEM), pl.BlockSpec(memory_space=pl.ANY)
    big = [(2 * feat + edge_w, feat), (feat, feat), (feat, feat), (feat, hidden), (hidden, feat), (edge_w, 2 * feat + edge_w), egrad.shape]
    small = [(edge_w, edge_w), (edge_w, edge_w), (feat,), (feat,), (feat,), (feat,), (edge_w,), (edge_w,)]
    shapes = [jax.ShapeDtypeStruct(s, F32) for s in big] + [jax.ShapeDtypeStruct(grad.shape, F32), jax.ShapeDtypeStruct(node.shape, BF16)]
    return pl.pallas_call(
        functools.partial(unpack_body, early, len(chunks) - early, feat, hidden, edge_w),
        in_specs=[whole] * (len(chunks) + 3),
        out_specs=[anywhere] * 9 + [whole] * 8,
        out_shape=shapes + [jax.ShapeDtypeStruct(s, F32) for s in small],
        scratch_shapes=[pltpu.VMEM(s, F32) for s in big]
        + [pltpu.SemaphoreType.DMA((24,))],
        compiler_params=pltpu.CompilerParams(vmem_limit_bytes=(30 if roomy else 46) * 1024 * 1024),
        name="unpack_all",
    )(*chunks, egrad, grad, node)


def local(n, node_feats, edge_feats, node_cotan, edge_cotan, neighbour, edge_mask, fetch_rows, chain_ids, complex_flag, message_in,
          message_mid, message_out, gain_node, offset_node, expand_weight, contract_weight, gain_ffn, offset_ffn, update_in, update_mid,
          update_out, gain_edge, offset_edge):
    x = node_feats[0]
    rows, feat = x.shape
    fan = neighbour.shape[1]
    edge_w = edge_feats.shape[3]
    e = jnp.transpose(edge_feats[0], (1, 2, 0))
    cot = jnp.transpose(edge_cotan[0], (1, 2, 0))
    nbr = jnp.transpose(neighbour)
    mask = jnp.transpose(edge_mask)
    uin = jnp.transpose(update_in)
    lhs, self_t, mid_t, umid_t, uout_t, uedge, sel, tag, gain_t, offset_t, far_x = table_rows(
        n, fetch_rows[0], x, chain_ids, complex_flag, message_in, message_mid, update_mid, update_out, uin, gain_edge, offset_edge
    )
    table_len = lhs.shape[1] - edge_w
    fit = lambda *options: next(c for c in options + (6, 4, 2, 1) if fan % c == 0)
    slabs = fit(10)
    h1, gp1, gp2, s, keep, cnt = message_forward(e, nbr, mask, tag, lhs, self_t, mid_t, slabs)
    node, lhs3, self3, n1, r1, n2, r2, acted, slope = node_forward(
        n, s, cnt, x, message_out, gain_node, offset_node, expand_weight, contract_weight, gain_ffn, offset_ffn,
        sel, uin
    )
    edge_new, part, guout, gumid, gin3, dself3, ggain, goff = edge_pass(
        e, cot, nbr, lhs3, self3, umid_t, uout_t, update_mid, update_out, uedge, gain_t, offset_t, fit(20, 10)
    )
    hidden = expand_weight.shape[1]
    early_depths, late_depths = chunk_plan(n // 2, early_rows(feat, hidden, edge_w)["end"], feat + edge_w + 16, 2 * feat)
    dfirst, d2, sums, *sources = node_backward(
        n, gin3, dself3, sel, node, node_cotan[0], uin, n1, r1, n2, r2, acted, slope, gain_node, offset_node, gain_ffn,
        expand_weight, contract_weight, s, cnt, message_out, ggain, goff, gumid, guout, early_depths
    )
    egrad, ngrad, *sums = message_backward(
        n, e, h1, gp1, gp2, part, keep, nbr, d2, message_mid, message_in, x, far_x, dfirst, sums, sel, sources, late_depths, table_len, slabs
    )
    gwin, gmid, gmout, gexp, gcon, guin, egrad, ngrad, node, gumid, guout, gnode, onode, gffn, offn, gedge, oedge = unpack_all(
        sums, egrad, ngrad, node, len(sources), feat, hidden, edge_w, table_len <= ROOMY
    )
    native = lambda a: jnp.transpose(a, (2, 0, 1))[None]
    return (node[None], native(edge_new), ngrad[None], native(egrad), gwin, gmid, gmout, gnode, onode, gexp, gcon, gffn, offn,
            jnp.transpose(guin), gumid, guout, gedge, oedge)


def solution(mesh):
    grouped, placed, copied = P("tm", "res", None), P("res", None), P()
    wide = P("tm", "res", None, None)
    arguments = (grouped, wide, grouped, wide, placed, placed, P("res", None, None), P("res"), P("res")) + (copied,) * 14
    return jax.shard_map(
        functools.partial(local, mesh.shape["res"]),
        mesh=mesh,
        in_specs=arguments,
        out_specs=(grouped, wide, grouped, wide) + (copied,) * 14,
        check_vma=False,
    )
```

```python
import functools
import jax
import jax.numpy as jnp
from jax import lax
from jax.experimental import pallas as pl
from jax.experimental.pallas import tpu as pltpu
from jax.sharding import PartitionSpec as P

EPSILON = 1e-05
CURVE = 0.7978845608028654
CUBIC = 0.044715
F32 = jnp.float32
BF16 = jnp.bfloat16
VMEM_LIMIT = 60 * 1024 * 1024
MESH = pl.DeviceIdType.MESH


def nn(a, b):
    return lax.dot_general(a, b, (((1,), (0,)), ((), ())), preferred_element_type=F32)


def nt(a, b):
    return lax.dot_general(a, b, (((1,), (1,)), ((), ())), preferred_element_type=F32)


def tn(a, b):
    return lax.dot_general(a, b, (((0,), (0,)), ((), ())), preferred_element_type=F32)


def narrow_gelu(v):
    v = v.astype(BF16)
    square = v * v
    t = jnp.tanh(v * (BF16(CURVE) + BF16(CURVE * CUBIC) * square))
    half = BF16(0.5) + BF16(0.5) * t
    slope = half + (half - half * half) * (v * (BF16(2.0 * CURVE) + BF16(6.0 * CURVE * CUBIC) * square))
    return v * half, slope


def gelu_parts(v):
    square = v * v
    t = jnp.tanh(v * (CURVE + (CURVE * CUBIC) * square))
    half = 0.5 + 0.5 * t
    slope = half + (half - half * half) * (v * (2.0 * CURVE + (6.0 * CURVE * CUBIC) * square))
    return v * half, slope


def tile_lanes(block, count):
    return jnp.concatenate([block] * count, axis=1) if count > 1 else block


def edge_operand(table_len, slabs, base, e_ref, nbr_ref):
    columns = []
    for j in range(slabs):
        row = nbr_ref[pl.ds(base + j, 1), :]
        ids = lax.broadcasted_iota(jnp.int16, (table_len, row.shape[1]), 0)
        hot = jnp.where(ids == jnp.broadcast_to(row, (16, row.shape[1])).astype(jnp.int16)[:1], BF16(1.0), BF16(0.0))
        columns.append(jnp.concatenate([hot, e_ref[j]], axis=0))
    return jnp.concatenate(columns, axis=1) if slabs > 1 else columns[0]


def message_forward_body(table_len, feat, slabs, e_ref, nbr_ref, mask_ref, own_ref, lhs_ref, self_ref, mid_ref,
                         h1_ref, gp1_ref, gp2_ref, s_ref, keep_ref, cnt_ref):
    step = pl.program_id(0)
    base = step * slabs
    rows = nbr_ref.shape[1]

    @pl.when(step == 0)
    def _():
        s_ref[...] = jnp.zeros_like(s_ref)
        cnt_ref[...] = jnp.zeros_like(cnt_ref)

    own = own_ref[...]
    own_chain = own // 2
    own_flag = own % 2
    pre = nn(lhs_ref[...], edge_operand(table_len, slabs, base, e_ref, nbr_ref))
    hidden, slope = narrow_gelu(pre[:feat] + tile_lanes(self_ref[...], slabs))
    total = s_ref[...]
    count = cnt_ref[...]
    keeps = []
    for j in range(slabs):
        cut = slice(j * rows, (j + 1) * rows)
        h1_ref[j] = hidden[:, cut]
        gp1_ref[j] = slope[:, cut]
        other = pre[feat : feat + 1, cut].astype(jnp.int32)
        joined = jnp.logical_or(own_chain == other // 2, own_flag * (other % 2) > 0)
        keep = jnp.where(joined, 1.0, 0.0) * mask_ref[pl.ds(base + j, 1), :].astype(F32)
        keep_ref[j] = keep
        keeps.append(keep)
        count = count + keep
    hidden, slope = narrow_gelu(nn(mid_ref[...], hidden))
    hidden = hidden.astype(F32)
    for j in range(slabs):
        cut = slice(j * rows, (j + 1) * rows)
        gp2_ref[j] = slope[:, cut]
        total = total + hidden[:, cut] * keeps[j]
    s_ref[...] = total
    cnt_ref[...] = count


def message_forward(e, nbr, mask, own_tag, lhs, self_t, mid_t, slabs):
    fan, edge_w, rows = e.shape
    feat = self_t.shape[0]
    table_len = lhs.shape[1] - edge_w
    whole = lambda a: pl.BlockSpec(a.shape, lambda i: (0,) * a.ndim)
    slab = lambda f: pl.BlockSpec((slabs, f, rows), lambda i: (i, 0, 0))
    big = pltpu.HBM((fan, feat, rows), BF16)
    e, nbr, mask = far_off(e, nbr, mask)
    return pl.pallas_call(
        functools.partial(message_forward_body, table_len, feat, slabs),
        grid=(fan // slabs,),
        in_specs=[slab(edge_w), whole(nbr), whole(mask), whole(own_tag), whole(lhs), whole(self_t), whole(mid_t)],
        out_specs=[slab(feat), slab(feat), slab(feat), pl.BlockSpec((feat, rows), lambda i: (0, 0)), slab(1),
                   pl.BlockSpec((1, rows), lambda i: (0, 0))],
        out_shape=[big, big, big, jax.ShapeDtypeStruct((feat, rows), F32), pltpu.HBM((fan, 1, rows), F32),
                   jax.ShapeDtypeStruct((1, rows), F32)],
        compiler_params=pltpu.CompilerParams(vmem_limit_bytes=30 * 1024 * 1024),
        name="message_forward",
    )(e, nbr, mask, own_tag, lhs, self_t, mid_t)


def edge_body(table_len, slabs, e_ref, cot_ref, nbr_ref, lhs_ref, self_ref, mid_t_ref, out_t_ref, mid_ref, out_ref, edge_ref,
              gain_ref, offset_ref,
              new_ref, part_ref, gout_ref, gmid_ref, gin_ref, dself_ref, ggain_ref, goff_ref):
    step = pl.program_id(0)
    base = step * slabs
    rows = nbr_ref.shape[1]

    @pl.when(step == 0)
    def _():
        for ref in (gout_ref, gmid_ref, gin_ref, dself_ref, ggain_ref, goff_ref):
            ref[...] = jnp.zeros_like(ref)

    x = edge_operand(table_len, slabs, base, e_ref, nbr_ref)
    self_t = tile_lanes(self_ref[...], slabs)
    hidden_three, slope_three = narrow_gelu(nn(lhs_ref[...], x) + self_t)
    hidden_four, slope_four = narrow_gelu(nn(mid_t_ref[...], hidden_three))
    branch = nn(out_t_ref[...], hidden_four)
    gain = gain_ref[...]
    offset = offset_ref[...]
    scale = 1.0 / e_ref.shape[1]
    resid = []
    ggain = ggain_ref[...]
    goff = goff_ref[...]
    for j in range(slabs):
        z = e_ref[j].astype(F32) + branch[:, j * rows : (j + 1) * rows]
        z = z - jnp.sum(z, axis=0, keepdims=True) * scale
        r = lax.rsqrt(jnp.sum(z * z, axis=0, keepdims=True) * scale + EPSILON)
        h = z * r
        new_ref[j] = (h * gain + offset).astype(BF16)
        dy = cot_ref[j].astype(F32)
        ggain = ggain + dy * h
        goff = goff + dy
        dh = dy * gain
        one = jnp.sum(dh, axis=0, keepdims=True) * scale
        two = jnp.sum(dh * h, axis=0, keepdims=True) * scale
        resid.append(r * (dh - one - h * two))
    ggain_ref[...] = ggain
    goff_ref[...] = goff
    resid = jnp.concatenate(resid, axis=1) if slabs > 1 else resid[0]
    delta = resid.astype(BF16)
    gout_ref[...] += nt(hidden_four, delta)
    delta_four = (nn(out_ref[...], delta) * slope_four.astype(F32)).astype(BF16)
    gmid_ref[...] += nt(hidden_three, delta_four)
    delta_three = nn(mid_ref[...], delta_four) * slope_three.astype(F32)
    low = delta_three.astype(BF16)
    gin_ref[...] += nt(x, low)
    part = resid + nn(edge_ref[...], low)
    dself = dself_ref[...]
    for j in range(slabs):
        cut = slice(j * rows, (j + 1) * rows)
        part_ref[j] = part[:, cut].astype(BF16)
        dself = dself + low[:, cut].astype(F32)
    dself_ref[...] = dself


def edge_pass(e, cot, nbr, lhs, self_t, mid_t, out_t, mid, out, edge, gain, offset, slabs):
    fan, edge_w, rows = e.shape
    table_len = lhs.shape[1] - edge_w
    whole = lambda a: pl.BlockSpec(a.shape, lambda i: (0,) * a.ndim)
    slab = pl.BlockSpec((slabs, edge_w, rows), lambda i: (i, 0, 0))
    keep = lambda *s: (pl.BlockSpec(s, lambda i: (0,) * len(s)), jax.ShapeDtypeStruct(s, F32))
    sums = [keep(edge_w, edge_w), keep(edge_w, edge_w), keep(table_len + edge_w, edge_w), keep(edge_w, rows), keep(edge_w, rows),
            keep(edge_w, rows)]
    e, cot, nbr, mid, out = far_off(e, cot, nbr, mid, out)
    consts = (nbr, lhs, self_t, mid_t, out_t, mid, out, edge, gain, offset)
    return pl.pallas_call(
        functools.partial(edge_body, table_len, slabs),
        grid=(fan // slabs,),
        in_specs=[slab, slab] + [whole(a) for a in consts],
        out_specs=[slab, slab] + [s for s, _ in sums],
        out_shape=[pltpu.HBM(e.shape, BF16), pltpu.HBM(e.shape, BF16)] + [s for _, s in sums],
        compiler_params=pltpu.CompilerParams(vmem_limit_bytes=42 * 1024 * 1024),
        name="edge_pass",
    )(e, cot, *consts)


LANES = 512


def spot():
    group, place = lax.axis_index("tm"), lax.axis_index("res")
    return group, place, lax.rem(place, 2), place // 2, lax.rem(group, 2), group // 2


def grain(places):
    return 16 * max(1, places // 4)


def piece(places, depth, index):
    across = min(places, 4)
    rows, wide = piece_shape(places, depth)
    top = pl.multiple_of((index // across) * rows, rows)
    left = pl.multiple_of(lax.rem(index, across) * wide, wide)
    return pl.ds(top, rows), pl.ds(left, wide)


def piece_shape(places, depth):
    across = min(places, 4)
    return depth // (places // across), LANES // across


def remote(source, target, send, recv, group, place):
    return pltpu.make_async_remote_copy(
        src_ref=source, dst_ref=target, send_sem=send, recv_sem=recv, device_id={"tm": group, "res": place}, device_id_type=MESH
    )


class Chunk:
    def __init__(self, places, source, result, acc, from_core, from_first, from_second, from_line, stage, out, sends, recvs, local):
        self.places, self.source, self.result, self.acc = places, source, result, acc
        self.from_core, self.from_first, self.from_second = from_core, from_first, from_second
        self.from_line, self.stage, self.out = from_line, stage, out
        self.sends, self.recvs, self.local = sends, recvs, local
        self.depth = acc.shape[1]

    def run(self, stage):
        (self.spread, self.halve, self.quarter, self.scatter, self.settle, self.gather, self.widen, self.share, self.store,
         self.close)[stage]()

    def link(self, slot, source, target, group, place):
        return functools.partial(remote, source, target, self.sends.at[slot], self.recvs.at[slot], group, place)

    def core_copy(self):
        group, place, core, lane, x, y = spot()
        theirs = pl.multiple_of((1 - core) * 8, 8)
        return self.link(0, self.source.at[pl.ds(theirs, 8)], self.from_core, group, place + 1 - 2 * core)

    def load_copy(self):
        core = spot()[2]
        return pltpu.make_async_copy(self.source.at[pl.ds(pl.multiple_of(core * 8, 8), 8)], self.acc, self.local.at[0])

    def half_copies(self):
        group, place, core, lane, x, y = spot()
        return [
            self.link(1, self.acc.at[pl.ds((1 - x) * 2, 2)], self.from_first.at[pl.ds(0, 2)], group + 1 - 2 * x, place),
            self.link(2, self.acc.at[pl.ds(4 + (1 - y) * 2, 2)], self.from_first.at[pl.ds(2, 2)], group + 2 - 4 * y, place),
        ]

    def quarter_copies(self):
        group, place, core, lane, x, y = spot()
        return [
            self.link(3, self.acc.at[x * 2 + 1 - y], self.from_second.at[0], group + 2 - 4 * y, place),
            self.link(4, self.acc.at[4 + y * 2 + 1 - x], self.from_second.at[1], group + 1 - 2 * x, place),
        ]

    def line_copies(self):
        group, place, core, lane, x, y = spot()
        copies = []
        for s in range(1, self.places):
            ahead, behind = lax.rem(lane + s, self.places), lax.rem(lane + self.places - s, self.places)
            rows, wide = piece(self.places, self.depth, ahead)
            view = self.stage.at[:, rows, wide]
            copies.append((self.link(4 + s, view, self.from_line.at[lane], group, ahead * 2 + core),
                           self.link(4 + s, view, self.from_line.at[behind], group, behind * 2 + core)))
        return copies

    def own(self):
        group, place, core, lane, x, y = spot()
        return core * 8 + x * 2 + y, core * 8 + 4 + y * 2 + x

    def spread_copies(self):
        group, place, core, lane, x, y = spot()
        copies = []
        slot = 4 + self.places
        for own in self.own():
            for s in range(1, self.places):
                ahead, behind = lax.rem(lane + s, self.places), lax.rem(lane + self.places - s, self.places)
                rows, wide = piece(self.places, self.depth, lane)
                back_rows, back_wide = piece(self.places, self.depth, behind)
                view, back = self.out.at[own, rows, wide], self.out.at[own, back_rows, back_wide]
                copies.append((self.link(slot, view, view, group, ahead * 2 + core), self.link(slot, back, back, group, behind * 2 + core)))
                slot += 1
        return copies

    def both(self, slot, view, back, group, place):
        return self.link(slot, view, view, group, place), self.link(slot, back, back, group, place)

    def gather_copies(self):
        group, place, core, lane, x, y = spot()
        slot = 2 + 3 * self.places
        first, second = self.own()
        return [
            self.both(slot, self.out.at[first], self.out.at[core * 8 + x * 2 + 1 - y], group + 2 - 4 * y, place),
            self.both(slot + 1, self.out.at[second], self.out.at[core * 8 + 4 + y * 2 + 1 - x], group + 1 - 2 * x, place),
        ]

    def widen_copies(self):
        group, place, core, lane, x, y = spot()
        slot = 4 + 3 * self.places
        two = lambda start: self.out.at[pl.ds(start, 2)]
        return [
            self.both(slot, two(core * 8 + x * 2), two(core * 8 + 2 - x * 2), group + 1 - 2 * x, place),
            self.both(slot + 1, two(core * 8 + 4 + y * 2), two(core * 8 + 6 - y * 2), group + 2 - 4 * y, place),
        ]

    def share_copy(self):
        group, place, core, lane, x, y = spot()
        eight = lambda which: self.out.at[pl.ds(pl.multiple_of(which * 8, 8), 8)]
        return self.both(6 + 3 * self.places, eight(core), eight(1 - core), group, place + 1 - 2 * core)

    def store_copy(self, which, slot):
        eight = pl.ds(pl.multiple_of(which * 8, 8), 8)
        return pltpu.make_async_copy(self.out.at[eight], self.result.at[eight], self.local.at[slot])

    def spread(self):
        self.core_copy()().start()
        self.load_copy().start()

    def halve(self):
        group, place, core, lane, x, y = spot()
        self.load_copy().wait()
        self.core_copy()().wait()
        acc, extra = self.acc, self.from_core
        give = [(1 - x) * 2, 4 + (1 - y) * 2]
        keep = [x * 2, 4 + y * 2]
        for start in give:
            for i in range(2):
                acc[start + i] = acc[start + i] + extra[start + i]
        for copy in self.half_copies():
            copy().start()
        for start in keep:
            for i in range(2):
                acc[start + i] = acc[start + i] + extra[start + i]

    def quarter(self):
        group, place, core, lane, x, y = spot()
        for copy in self.half_copies():
            copy().wait()
        acc, extra = self.acc, self.from_first
        acc[x * 2 + 1 - y] = acc[x * 2 + 1 - y] + extra[1 - y]
        acc[4 + y * 2 + 1 - x] = acc[4 + y * 2 + 1 - x] + extra[3 - x]
        for copy in self.quarter_copies():
            copy().start()
        self.stage[0] = acc[x * 2 + y] + extra[y]
        self.stage[1] = acc[4 + y * 2 + x] + extra[2 + x]

    def scatter(self):
        for copy in self.quarter_copies():
            copy().wait()
        for s in range(2):
            self.stage[s] = self.stage[s] + self.from_second[s]
        for send, arrive in self.line_copies():
            send().start()

    def settle(self):
        group, place, core, lane, x, y = spot()
        rows, wide = piece(self.places, self.depth, lane)
        total = self.stage[:, rows, wide].astype(F32)
        pairs = self.line_copies()
        for s in range(1, self.places):
            pairs[s - 1][1]().wait_recv()
            total = total + self.from_line[lax.rem(lane + self.places - s, self.places)].astype(F32)
        first, second = self.own()
        total = total.astype(BF16)
        self.out[first, rows, wide] = total[0]
        self.out[second, rows, wide] = total[1]
        for send, arrive in self.spread_copies():
            send().start()
        for send, arrive in pairs:
            send().wait_send()

    def finish(self, pairs):
        for send, arrive in pairs:
            arrive().wait_recv()
        for send, arrive in pairs:
            send().wait_send()

    def gather(self):
        self.finish(self.spread_copies())
        for send, arrive in self.gather_copies():
            send().start()

    def widen(self):
        self.finish(self.gather_copies())
        for send, arrive in self.widen_copies():
            send().start()

    def share(self):
        core = spot()[2]
        self.finish(self.widen_copies())
        self.share_copy()[0]().start()
        self.store_copy(core, 1).start()

    def store(self):
        core = spot()[2]
        self.share_copy()[1]().wait_recv()
        self.store_copy(1 - core, 2).start()

    def close(self):
        core = spot()[2]
        self.share_copy()[0]().wait_send()
        self.store_copy(core, 1).wait()
        self.store_copy(1 - core, 2).wait()


CHUNK_REFS = 10
ROOMY = 512


def chunk_scratch(places, depth):
    rows, wide = piece_shape(places, depth)
    shapes = [(8, depth, LANES), (8, depth, LANES), (4, depth, LANES), (2, depth, LANES), (places, 2, rows, wide), (2, depth, LANES),
              (16, depth, LANES)]
    links = 7 + 3 * places
    return [pltpu.VMEM(s, BF16) for s in shapes] + [pltpu.SemaphoreType.DMA((links,))] * 2 + [pltpu.SemaphoreType.DMA((3,))]


def greet_all(n):
    group, place, core, lane, x, y = spot()
    barrier = pltpu.get_barrier_semaphore()
    partners = [(group + 1 - 2 * x, place), (group + 2 - 4 * y, place)]
    partners += [(group, lax.rem(place + s, n)) for s in range(1, n)]
    for near, far in partners:
        pl.semaphore_signal(barrier, inc=1, device_id={"tm": near, "res": far}, device_id_type=MESH)


def chunk_plan(places, early_rows, late_first, late_second):
    unit = grain(places)
    depth = lambda rows: -(-rows // (16 * unit)) * unit
    total = depth(early_rows)
    steps = total // unit
    return [(steps + k) // 4 * unit for k in range(4)], [depth(late_first), depth(late_second)]


def pack(bufs, row, value):
    start = 0
    value = value.astype(BF16)
    for buf in bufs:
        size = buf.shape[0] * buf.shape[1]
        depth = buf.shape[1]
        low, high = max(row, start), min(row + value.shape[0], start + size)
        while low < high:
            slot, inner = divmod(low - start, depth)
            step = min(high - low, depth - inner)
            buf[slot, inner : inner + step, : value.shape[1]] = value[low - row : low - row + step]
            low += step
        start += size


def fill(bufs, row, values):
    for value in values:
        pack(bufs, row, value)
        row += value.shape[0]
    spare = sum(b.shape[0] * b.shape[1] for b in bufs) - row
    if spare:
        pack(bufs, row, jnp.zeros((spare, bufs[0].shape[2]), F32))


def unpack(bufs, row, count, width):
    pieces = []
    start = 0
    for buf in bufs:
        depth = buf.shape[1]
        size = buf.shape[0] * depth
        low, high = max(row, start), min(row + count, start + size)
        while low < high:
            slot, inner = divmod(low - start, depth)
            step = min(high - low, depth - inner)
            pieces.append((buf[slot, inner : inner + step, : width], low - row))
            low += step
        start += size
    return pieces


def ring_place(n):
    me = lax.axis_index("res")
    return me, [lax.rem(me + s, n) for s in range(n)]


def greet_start(peers):
    barrier = pltpu.get_barrier_semaphore()
    for peer in peers[1:]:
        pl.semaphore_signal(barrier, inc=1, device_id={"res": peer}, device_id_type=MESH)


def greet_end(peers):
    pl.semaphore_wait(pltpu.get_barrier_semaphore(), len(peers) - 1)


def copy_to(peer, source, target, send, recv):
    return pltpu.make_async_remote_copy(
        src_ref=source, dst_ref=target, send_sem=send, recv_sem=recv, device_id={"res": peer}, device_id_type=MESH
    )


def swap(n, me, peers, source, target, send, recv, placed=False):
    view = lambda s: source.at[peers[s] if placed else s]
    sent = [copy_to(peers[s], view(s), target.at[me], send.at[s], recv.at[me]) for s in range(1, n)]
    back = [copy_to(peers[s], view(s), target.at[peers[s]], send.at[s], recv.at[peers[s]]) for s in range(1, n)]
    return sent, back


def row_norm(values):
    values = values - jnp.mean(values, axis=1, keepdims=True)
    r = lax.rsqrt(jnp.mean(values * values, axis=1, keepdims=True) + EPSILON)
    return values * r, r


def row_norm_back(dh, h, r):
    return r * (dh - jnp.mean(dh, axis=1, keepdims=True) - h * jnp.mean(dh * h, axis=1, keepdims=True))


def table_rows_body(n, fetch_ref, x_ref, chain_ref, flag_ref, win_hbm, mid_hbm, umid_hbm, uout_hbm, uin_hbm, gain_ref, off_ref,
                    lhs_ref, self_ref, midt_ref, umidt_ref, uoutt_ref, uedge_ref, sel_ref, tag_ref, gaint_ref, offt_ref, far_ref,
                    idx_out, idx_in, row_out, far, wants, asked, win_ref, mid_ref, umid_ref, uout_ref, uin_ref, send_a, recv_a, send_b, recv_b,
                    load):
    me, peers = ring_place(n)
    greet_start(peers)
    pairs = ((win_hbm, win_ref), (mid_hbm, mid_ref), (umid_hbm, umid_ref), (uout_hbm, uout_ref), (uin_hbm, uin_ref))
    loads = [pltpu.make_async_copy(pairs[k][0], pairs[k][1], load.at[k]) for k in range(5)]
    for copy in loads:
        copy.start()
    rows, feat = x_ref.shape
    cap = fetch_ref.shape[1]
    edge_w = win_ref.shape[0] - 2 * feat
    tag = chain_ref[...].reshape(1, rows) * 2 + flag_ref[...].reshape(1, rows)
    tag_ref[...] = tag
    for s in range(n):
        idx_out[s] = jnp.full((8, 128), -1, jnp.int32)
        idx_out[s, 0:1, 0:cap] = fetch_ref[pl.ds(peers[s], 1), :]
        idx_out[s, 1:2, 0:rows] = tag
    greet_end(peers)
    sent, back = swap(n, me, peers, idx_out, idx_in, send_a, recv_a)
    for copy in sent:
        copy.start()
    idx_in[me] = idx_out[0]
    x = x_ref[...]
    for p in range(n):
        wants[0:1, p * cap : (p + 1) * cap] = fetch_ref[p : p + 1, :]
    loads[0].wait()
    self_ref[...] = jnp.transpose(nn(x, win_ref[:feat, :]))

    copies, backs = swap(n, me, peers, row_out, far, send_b, recv_b, True)
    for copy in back:
        copy.wait_recv()
    for p in range(n):
        asked[0:1, p * cap : (p + 1) * cap] = idx_in[p, 0:1, 0:cap]
    spots = lax.broadcasted_iota(jnp.int32, (rows, n * cap), 0)
    hot = jnp.where(spots + me * rows == asked[...], 1.0, 0.0).astype(BF16)
    row_out[...] = tn(hot, x).astype(BF16).reshape(n, cap, feat)
    for copy in copies:
        copy.start()
    sel_ref[...] = hot
    far[me] = row_out[me]
    for copy in loads[1:]:
        copy.wait()
    midt_ref[...] = jnp.transpose(mid_ref[...])
    umidt_ref[...] = jnp.transpose(umid_ref[...])
    uoutt_ref[...] = jnp.transpose(uout_ref[...])
    uedge_ref[...] = jnp.transpose(uin_ref[:, 2 * feat :])
    for source, target in ((gain_ref, gaint_ref), (off_ref, offt_ref)):
        target[...] = jnp.transpose(jnp.broadcast_to(source[...].astype(F32).reshape(1, edge_w), (rows, edge_w)))
    neigh = win_ref[feat : 2 * feat, :]
    extra = lhs_ref.shape[0] - feat
    table_len = rows + n * cap
    lhs_ref[feat:, table_len:] = jnp.zeros((extra, edge_w), BF16)
    lhs_ref[:feat, table_len:] = jnp.transpose(win_ref[2 * feat :, :])
    lhs_ref[:feat, :rows] = jnp.transpose(nn(x, neigh)).astype(BF16)
    lhs_ref[feat:, :rows] = jnp.broadcast_to(tag.astype(F32), (extra, rows)).astype(BF16)
    tags = jnp.concatenate([idx_in[p, 1:2, 0:rows] for p in range(n)] + [jnp.zeros((-n % 16, rows), jnp.int32)] * (n % 16 > 0), axis=0)
    want = wants[...]
    picked = nn(tags.astype(F32).astype(BF16), jnp.where(spots == lax.rem(want, rows), 1.0, 0.0).astype(BF16))
    owner = lax.broadcasted_iota(jnp.int32, picked.shape, 0) == want // rows
    far_tag = jnp.sum(jnp.where(owner, picked, 0.0), axis=0, keepdims=True)
    lhs_ref[feat:, rows:table_len] = jnp.broadcast_to(far_tag, (extra, n * cap)).astype(BF16)
    for copy in backs:
        copy.wait_recv()
    got = far[...].reshape(n * cap, feat)
    lhs_ref[:feat, rows:table_len] = jnp.transpose(nn(got, neigh)).astype(BF16)
    far_ref[...] = got
    for copy in sent + copies:
        copy.wait_send()


def far_off(*arrays):
    return [pltpu.with_memory_space_constraint(a, pltpu.HBM) for a in arrays]


def vmem_call(body, args, outs, scratch, collective, name, outside=(), raw=()):
    whole = pl.BlockSpec(memory_space=pltpu.VMEM)
    return pl.pallas_call(
        body,
        out_shape=[pltpu.HBM(s, d) if i in outside else jax.ShapeDtypeStruct(s, d) for i, (s, d) in enumerate(outs)],
        in_specs=[pl.BlockSpec(memory_space=pl.ANY) if i in raw else whole for i in range(len(args))],
        out_specs=[whole] * len(outs),
        scratch_shapes=scratch,
        compiler_params=pltpu.CompilerParams(vmem_limit_bytes=30 * 1024 * 1024, collective_id=collective, has_side_effects=True),
        name=name,
    )(*args)


def table_rows(n, fetch, x, chain, flag, win, mid, umid, uout, uin, gain, off):
    rows, feat = x.shape
    cap = fetch.shape[1]
    edge_w = win.shape[0] - 2 * feat
    table_len = rows + n * cap
    outs = [((feat + 16, table_len + edge_w), BF16), ((feat, rows), F32), (mid.shape, BF16), (umid.shape, BF16), (uout.shape, BF16),
            ((edge_w, edge_w), BF16), ((rows, n * cap), BF16), ((1, rows), jnp.int32), ((edge_w, rows), F32), ((edge_w, rows), F32),
            ((n * cap, feat), BF16)]
    sems = [pltpu.SemaphoreType.DMA((n,))] * 4 + [pltpu.SemaphoreType.DMA((5,))]
    scratch = [pltpu.VMEM((n, 8, 128), jnp.int32)] * 2 + [pltpu.VMEM((n, cap, feat), BF16)] * 2 + [pltpu.VMEM((1, n * cap), jnp.int32)] * 2
    scratch += [pltpu.VMEM(w.shape, BF16) for w in (win, mid, umid, uout, uin)]
    return vmem_call(functools.partial(table_rows_body, n), far_off(fetch, x, chain, flag, win, mid, umid, uout, uin, gain, off), outs,
                     scratch + sems, 0, "table_rows", (10,), range(4, 9))


def node_forward_body(n, s_ref, cnt_ref, x_ref, mout_ref, gain_ref, off_ref, exp_ref, con_ref, gain2_ref, off2_ref, sel_ref, uin_ref,
                      node_ref, lhs_ref, self_ref, h1_ref, r1_ref, h2_ref, r2_ref, acted_ref, slope_ref,
                      row_out, far, send_a, recv_a):
    me, peers = ring_place(n)
    greet_start(peers)
    rows, feat = x_ref.shape
    cap = sel_ref.shape[1] // n
    edge_w = uin_ref.shape[0]
    line = lambda ref: ref[...].astype(F32).reshape(1, feat)
    mean = jnp.transpose(s_ref[...] / jnp.maximum(cnt_ref[...], 1.0))
    upper = mean.astype(BF16)
    lower = (mean - upper.astype(F32)).astype(BF16)
    aggregate = nn(upper, mout_ref[...]) + nn(lower, mout_ref[...])
    h, r = row_norm(x_ref[...].astype(F32) + aggregate)
    h1_ref[...] = h
    r1_ref[...] = r
    first = h * line(gain_ref) + line(off_ref)
    hidden, slope = gelu_parts(nn(first.astype(BF16), exp_ref[...]))
    acted = hidden.astype(BF16)
    acted_ref[...] = acted
    slope_ref[...] = slope
    h, r = row_norm(first + nn(acted, con_ref[...]))
    h2_ref[...] = h
    r2_ref[...] = r
    low = (h * line(gain2_ref) + line(off2_ref)).astype(BF16)
    node_ref[...] = low
    neigh = nt(low, uin_ref[:, feat : 2 * feat])
    packed = neigh.astype(BF16)
    greet_end(peers)
    copies, backs = swap(n, me, peers, row_out, far, send_a, recv_a, True)
    row_out[...] = tn(sel_ref[...], packed).astype(BF16).reshape(n, cap, edge_w)
    for copy in copies:
        copy.start()
    far[me] = row_out[me]
    self_ref[...] = nt(uin_ref[:, :feat], low)
    table_len = rows + n * cap
    lhs_ref[:, :rows] = jnp.transpose(neigh).astype(BF16)
    lhs_ref[:, table_len:] = uin_ref[:, 2 * feat :]
    for copy in backs:
        copy.wait_recv()
    lhs_ref[:, rows:table_len] = jnp.transpose(far[...].reshape(n * cap, edge_w))
    for copy in copies:
        copy.wait_send()


def node_forward(n, s, cnt, x, mout, gain, off, expand, contract, gain2, off2, sel, uin):
    rows, feat = x.shape
    cap = sel.shape[1] // n
    edge_w = uin.shape[0]
    table_len = rows + n * cap
    hidden = expand.shape[1]
    outs = [(x.shape, BF16), ((edge_w, table_len + edge_w), BF16), ((edge_w, rows), F32), (x.shape, F32), ((rows, 1), F32),
            (x.shape, F32), ((rows, 1), F32), ((rows, hidden), BF16), ((rows, hidden), F32)]
    scratch = [pltpu.VMEM((n, cap, edge_w), BF16)] * 2 + [pltpu.SemaphoreType.DMA((n,))] * 2
    return vmem_call(functools.partial(node_forward_body, n),
                     [s, cnt] + far_off(x, mout, gain, off) + [expand, contract] + far_off(gain2, off2) + [sel, uin], outs, scratch, 1,
                     "node_forward")


def swap_back_start(n, me, peers, gin, sel_ref, row_out, far, send, recv, rows):
    cap = sel_ref.shape[1] // n
    copies, backs = swap(n, me, peers, row_out, far, send, recv, True)
    row_out[...] = gin[pl.ds(rows, n * cap), :].astype(BF16).reshape(n, cap, gin.shape[1])
    for copy in copies:
        copy.start()
    far[me] = row_out[me]
    return copies, backs


def swap_back_finish(n, copies, gin, sel_ref, far, rows):
    for copy in copies[1]:
        copy.wait_recv()
    total = gin[:rows, :] + nn(sel_ref[...], far[...].reshape(sel_ref.shape[1], gin.shape[1]))
    for copy in copies[0]:
        copy.wait_send()
    return total.astype(BF16)


def node_backward_body(n, gin_ref, dself_ref, sel_ref, node_ref, cot_ref, uin_ref, h1_ref, r1_ref, h2_ref, r2_ref, acted_ref, slope_ref,
                       gain_ref, off_ref, gain2_ref, exp_ref, con_ref, s_ref, cnt_ref, mout_ref, ggain_ref, goff_ref,
                       gumid_ref, guout_ref, dfirst_ref, d2_ref, vec_ref, *rest):
    chunks, (row_out, far, send_a, recv_a) = rest[:-4], rest[-4:]
    me, peers = ring_place(n)
    rows, feat = node_ref.shape
    edge_w = uin_ref.shape[0]
    greet_start(peers)
    line = lambda ref: ref[...].astype(F32).reshape(1, feat)
    table_len = gin_ref.shape[0] - edge_w
    dself_t = dself_ref[...].astype(BF16)
    dself = jnp.transpose(dself_ref[...]).astype(BF16)
    greet_end(peers)
    copies = swap_back_start(n, me, peers, gin_ref, sel_ref, row_out, far, send_a, recv_a, rows)
    node = node_ref[...]
    at = early_rows(feat, acted_ref.shape[1], edge_w)
    pack(chunks, at["update_self"], nn(dself_t, node))
    gap = jnp.zeros((edge_w, 256 - edge_w), F32)
    pack(chunks, at["update_edge"], jnp.concatenate([jnp.transpose(gin_ref[table_len:, :]), gap, gumid_ref[...], gap], axis=1))
    pack(chunks, at["update_out"], jnp.concatenate([guout_ref[...], jnp.zeros((edge_w, feat - edge_w), F32)], axis=1))
    side = jnp.zeros((1, feat - edge_w), F32)
    edge_sums = [jnp.concatenate([jnp.sum(jnp.transpose(ref[...]), axis=0, keepdims=True), side], axis=1) for ref in (ggain_ref, goff_ref)]
    used = at["end"]
    spare = sum(c.shape[0] * c.shape[1] for c in chunks) - used
    if spare:
        pack(chunks, used, jnp.zeros((spare, feat), F32))
    dy = cot_ref[...].astype(F32) + nn(dself, uin_ref[:, :feat])
    own = swap_back_finish(n, copies, gin_ref, sel_ref, far, rows)
    dy = dy + nn(own, uin_ref[:, feat : 2 * feat])
    pack(chunks, at["update_neigh"], tn(own, node))
    h2 = h2_ref[...]
    ffn_sums = [jnp.sum(dy * h2, axis=0, keepdims=True), jnp.sum(dy, axis=0, keepdims=True)]
    second = row_norm_back(dy * line(gain2_ref), h2, r2_ref[...])
    dffn = second.astype(BF16)
    for b in range(acted_ref.shape[1] // feat):
        pack(chunks, at["contract"] + b * feat, tn(acted_ref[:, b * feat : (b + 1) * feat], dffn))
    dinner = (nt(dffn, con_ref[...]) * slope_ref[...]).astype(BF16)
    h1 = h1_ref[...]
    gain = line(gain_ref)
    first_low = (h1 * gain + line(off_ref)).astype(BF16)
    for b in range(acted_ref.shape[1] // feat):
        pack(chunks, at["expand"] + b * feat, tn(first_low, dinner[:, b * feat : (b + 1) * feat]))
    dy = second + nt(dinner, exp_ref[...])
    sums = [jnp.sum(dy * h1, axis=0, keepdims=True), jnp.sum(dy, axis=0, keepdims=True)] + ffn_sums
    dfirst = row_norm_back(dy * gain, h1, r1_ref[...])
    dfirst_ref[...] = dfirst
    back = (jnp.transpose(dfirst) / jnp.maximum(cnt_ref[...], 1.0)).astype(BF16)
    d2_ref[...] = nn(mout_ref[...], back)
    pack(chunks, at["message_out"], nt(s_ref[...].astype(BF16), back))
    vec_ref[...] = jnp.concatenate(sums + edge_sums + [jnp.zeros((10, feat), F32)], axis=0)


def early_rows(feat, hidden, edge_w):
    at, row = {}, 0
    for name, count in (("contract", hidden), ("expand", hidden), ("message_out", feat), ("update_self", edge_w),
                        ("update_neigh", edge_w), ("update_edge", edge_w), ("update_out", edge_w)):
        at[name] = row
        row += count
    at["end"] = row
    return at


def node_backward(n, gin, dself, sel, node, cot, uin, h1, r1, h2, r2, acted, slope, gain, off, gain2, expand, contract, s, cnt, mout,
                  ggain, goff, gumid, guout, depths):
    rows, feat = node.shape
    cap = sel.shape[1] // n
    edge_w = uin.shape[0]
    outs = [(node.shape, F32), ((feat, rows), F32), ((16, feat), F32)] + [((16, d, LANES), BF16) for d in depths]
    scratch = [pltpu.VMEM((n, cap, edge_w), BF16)] * 2 + [pltpu.SemaphoreType.DMA((n,))] * 2
    return vmem_call(functools.partial(node_backward_body, n),
                     [gin, dself, sel, node, cot, uin, h1, r1, h2, r2, acted, slope] + far_off(gain, off, gain2)
                     + [expand, contract, s, cnt, mout, ggain, goff, gumid, guout], outs, scratch, 2, "node_backward",
                     (0, 1, 2))


EARLY_ORDER = (
    ((0, 0),),
    ((3, 0), (1, 0), (0, 1)),
    (),
    ((1, 1),),
    (),
    ((0, 2),),
    ((2, 0), (1, 2), (3, 1)),
    ((0, 3),),
    ((2, 1), (1, 3)),
    (),
    ((0, 4), (3, 2)),
    (),
)
LATE_ORDER = (
    (2, 2), (1, 4), (0, 5), (4, 1), (5, 0), (2, 3), (5, 1), (3, 3), (0, 6), (1, 5), (2, 4), (4, 2), (5, 2), (3, 4), (1, 6),
    (2, 5), (5, 3), (3, 5), (4, 3), (2, 6), (0, 7), (5, 4), (3, 6), (4, 4), (5, 5), (2, 7), (4, 5), (5, 6), (-1, 0), (3, 7),
    (1, 7), (4, 6), (2, 8), (0, 8), (0, 9), (1, 8), (5, 7), (3, 8), (4, 7), (5, 8), (1, 9), (3, 9), (2, 9), (4, 8), (5, 9),
    (4, 9),
)


def message_backward_body(n, table_len, slabs, early, late, *refs):
    (e_ref, h1_ref, gp1_ref, gp2_ref, part_ref, keep_ref, nbr_ref, d2_ref, mid_ref, win_ref, x_ref, far_ref, dfirst_ref, vec_ref, sel_ref) = refs[:15]
    refs = refs[15:]
    sources, refs = refs[:early], refs[early:]
    egrad_ref, grad_ref, results, refs = refs[0], refs[1], refs[2 : 2 + early + late], refs[2 + early + late :]
    (gmid, gin, dself_sum, row_out, far, send_a, recv_a), refs = refs[:7], refs[7:]
    late_sources, refs = refs[:late], refs[late:]
    places = n // 2
    chunks = [Chunk(places, (list(sources) + list(late_sources))[i], results[i], *refs[CHUNK_REFS * i : CHUNK_REFS * (i + 1)])
              for i in range(early + late)]
    step = pl.program_id(0)
    base = step * slabs
    steps = pl.num_programs(0)
    rows = nbr_ref.shape[1]
    feat = d2_ref.shape[0]

    @pl.when(step == 0)
    def _():
        greet_all(n)
        for ref in (gmid, gin, dself_sum):
            ref[...] = jnp.zeros_like(ref)

    count = nbr_ref.shape[0] // slabs
    def slot(half):
        for at in range(count):
            which = EARLY_ORDER[2 * at + half]
            if which:

                @pl.when(step == at)
                def _(which=which):
                    for i, stage in which:
                        chunks[i].run(stage)

    x = edge_operand(table_len, slabs, base, e_ref, nbr_ref)
    back = d2_ref[...]
    wide = lambda ref: jnp.concatenate([ref[j] for j in range(slabs)], axis=1)
    two = jnp.concatenate([(back * keep_ref[j] * gp2_ref[j].astype(F32)).astype(BF16) for j in range(slabs)], axis=1)
    gmid[...] += nt(wide(h1_ref), two)

    @pl.when(step == 0)
    def _():
        pl.semaphore_wait(pltpu.get_barrier_semaphore(), n + 1)

    slot(0)
    one = (nn(mid_ref[...], two) * wide(gp1_ref).astype(F32)).astype(BF16)
    gin[...] += nt(x, one)
    part = nn(win_ref[2 * feat :, :], one)
    total = dself_sum[...]
    for j in range(slabs):
        cut = slice(j * rows, (j + 1) * rows)
        egrad_ref[j] = (part_ref[j].astype(F32) + part[:, cut]).astype(BF16)
        total = total + one[:, cut].astype(F32)
    dself_sum[...] = total
    slot(1)

    @pl.when(step == steps - 1)
    def _():
        nodes = x_ref[...]
        dself = jnp.transpose(dself_sum[...]).astype(BF16)
        near = gin[:rows, :].astype(BF16)
        beyond = gin[rows:table_len, :].astype(BF16)
        fill(late_sources[:1], 0, [gmid[...], gin[table_len:, :], vec_ref[...]])
        chunks[early].run(0)
        fill(late_sources[1:], 0, [tn(nodes, dself), tn(nodes, near) + tn(far_ref[...], beyond)])
        me, peers = ring_place(n)
        copies = swap_back_start(n, me, peers, gin, sel_ref, row_out, far, send_a, recv_a, rows)
        for i, stage in LATE_ORDER:
            if i < 0:
                own = swap_back_finish(n, copies, gin, sel_ref, far, rows)
                grad_ref[...] = dfirst_ref[...] + nt(dself, win_ref[:feat, :]) + nt(own, win_ref[feat : 2 * feat, :])
            else:
                chunks[i].run(stage)


def message_backward(n, e, h1, gp1, gp2, part, keep, nbr, d2, mid, win, x, far_x, dfirst, vectors, sel, sources, late_depths, table_len, slabs):
    fan, edge_w, rows = e.shape
    feat = d2.shape[0]
    cap = sel.shape[1] // n
    places = n // 2
    whole = lambda a: pl.BlockSpec(a.shape, lambda i: (0,) * a.ndim)
    slab = lambda f: pl.BlockSpec((slabs, f, rows), lambda i: (i, 0, 0))
    anywhere = pl.BlockSpec(memory_space=pl.ANY)
    consts = (nbr, d2, mid, win, x, far_x, dfirst, vectors, sel)
    roomy = table_len <= ROOMY
    place = pltpu.VMEM if roomy else pltpu.HBM
    sources = [pltpu.with_memory_space_constraint(c, place) for c in sources]
    depths = [s.shape[1] for s in sources] + list(late_depths)
    scratch = [pltpu.VMEM((feat, feat), F32), pltpu.VMEM((table_len + edge_w, feat), F32), pltpu.VMEM((feat, rows), F32)]
    scratch += [pltpu.VMEM((n, cap, feat), BF16)] * 2 + [pltpu.SemaphoreType.DMA((n,))] * 2
    scratch += [pltpu.VMEM((16, d, LANES), BF16) for d in late_depths]
    for d in depths:
        scratch += chunk_scratch(places, d)
    return pl.pallas_call(
        functools.partial(message_backward_body, n, table_len, slabs, len(sources), len(late_depths)),
        grid=(fan // slabs,),
        in_specs=[slab(edge_w), slab(feat), slab(feat), slab(feat), slab(edge_w), slab(1)] + [whole(a) for a in consts]
        + [anywhere] * len(sources),
        out_specs=[slab(edge_w), whole(x)] + [anywhere] * len(depths),
        out_shape=[place(e.shape, BF16), place(x.shape, F32)]
        + [place((16, d, LANES), BF16) for d in depths],
        scratch_shapes=scratch,
        compiler_params=pltpu.CompilerParams(vmem_limit_bytes=(42 if roomy else 58) * 1024 * 1024, collective_id=3, has_side_effects=True),
        name="message_backward",
    )(e, h1, gp1, gp2, part, keep, *consts, *sources)


def unpack_body(early, late, feat, hidden, edge_w, *refs):
    count = early + late
    sources, refs = refs[:count], refs[count:]
    (egrad, grad, node), refs = refs[:3], refs[3:]
    (gwin, gmid, gmout, gexp, gcon, guin, egrad_out, grad_out, node_out, gumid, guout), refs = refs[:11], refs[11:]
    vectors_out, refs = refs[:6], refs[6:]
    held = sources
    (swin, smid, smout, sexp, scon, suin, segrad), send = refs[:7], refs[7]
    at = early_rows(feat, hidden, edge_w)
    sent = []

    def push(source, target):
        copy = pltpu.make_async_copy(source, target, send.at[len(sent)])
        copy.start()
        sent.append(copy)

    push(grad, grad_out)
    push(node, node_out)

    def section(bufs, row, size, width, target, top=0, left=0, lane=0):
        for value, offset in unpack(bufs, row, size, LANES):
            target[top + offset : top + offset + value.shape[0], left : left + width] = value[:, lane : lane + width].astype(F32)

    front, back = held[:early], held[early:]
    for b in range(hidden // feat):
        section(front, at["contract"] + b * feat, feat, feat, scon, top=b * feat)
        push(scon.at[pl.ds(b * feat, feat)], gcon.at[pl.ds(b * feat, feat)])
    for b in range(hidden // feat):
        section(front, at["expand"] + b * feat, feat, feat, sexp, left=b * feat)
        push(sexp.at[:, pl.ds(b * feat, feat)], gexp.at[:, pl.ds(b * feat, feat)])
    section(front, at["message_out"], feat, feat, smout)
    push(smout, gmout)
    section(front, at["update_self"], edge_w, feat, suin)
    section(front, at["update_neigh"], edge_w, feat, suin, left=feat)
    section(front, at["update_edge"], edge_w, edge_w, suin, left=2 * feat)
    push(suin, guin)
    section(front, at["update_edge"], edge_w, edge_w, gumid, lane=256)
    section(front, at["update_out"], edge_w, edge_w, guout)
    vectors = unpack(back[:1], feat + edge_w, 16, LANES)[0][0].astype(F32)
    for k in range(6):
        size = vectors_out[k].shape[0]
        vectors_out[k][...] = vectors[k : k + 1, :size].reshape(size)
    section(back[:1], 0, feat, feat, smid)
    push(smid, gmid)
    section(back[:1], feat, edge_w, feat, swin, top=2 * feat)
    section(back[1:], 0, 2 * feat, feat, swin)
    push(swin, gwin)
    slab = egrad.shape[0] // 4
    for b in range(4):
        for k in range(b * slab, (b + 1) * slab):
            segrad[k] = egrad[k].astype(F32)
        push(segrad.at[pl.ds(b * slab, slab)], egrad_out.at[pl.ds(b * slab, slab)])
    for copy in sent:
        copy.wait()


def unpack_all(chunks, egrad, grad, node, early, feat, hidden, edge_w, roomy):
    whole, anywhere = pl.BlockSpec(memory_space=pltpu.VMEM), pl.BlockSpec(memory_space=pl.ANY)
    big = [(2 * feat + edge_w, feat), (feat, feat), (feat, feat), (feat, hidden), (hidden, feat), (edge_w, 2 * feat + edge_w), egrad.shape]
    small = [(edge_w, edge_w), (edge_w, edge_w), (feat,), (feat,), (feat,), (feat,), (edge_w,), (edge_w,)]
    shapes = [jax.ShapeDtypeStruct(s, F32) for s in big] + [jax.ShapeDtypeStruct(grad.shape, F32), jax.ShapeDtypeStruct(node.shape, BF16)]
    return pl.pallas_call(
        functools.partial(unpack_body, early, len(chunks) - early, feat, hidden, edge_w),
        in_specs=[whole] * (len(chunks) + 3),
        out_specs=[anywhere] * 9 + [whole] * 8,
        out_shape=shapes + [jax.ShapeDtypeStruct(s, F32) for s in small],
        scratch_shapes=[pltpu.VMEM(s, F32) for s in big]
        + [pltpu.SemaphoreType.DMA((24,))],
        compiler_params=pltpu.CompilerParams(vmem_limit_bytes=(30 if roomy else 46) * 1024 * 1024),
        name="unpack_all",
    )(*chunks, egrad, grad, node)


def local(n, node_feats, edge_feats, node_cotan, edge_cotan, neighbour, edge_mask, fetch_rows, chain_ids, complex_flag, message_in,
          message_mid, message_out, gain_node, offset_node, expand_weight, contract_weight, gain_ffn, offset_ffn, update_in, update_mid,
          update_out, gain_edge, offset_edge):
    x = node_feats[0]
    rows, feat = x.shape
    fan = neighbour.shape[1]
    edge_w = edge_feats.shape[3]
    e = jnp.transpose(edge_feats[0], (1, 2, 0))
    cot = jnp.transpose(edge_cotan[0], (1, 2, 0))
    nbr = jnp.transpose(neighbour)
    mask = jnp.transpose(edge_mask)
    uin = jnp.transpose(update_in)
    lhs, self_t, mid_t, umid_t, uout_t, uedge, sel, tag, gain_t, offset_t, far_x = table_rows(
        n, fetch_rows[0], x, chain_ids, complex_flag, message_in, message_mid, update_mid, update_out, uin, gain_edge, offset_edge
    )
    table_len = lhs.shape[1] - edge_w
    fit = lambda *options: next(c for c in options + (6, 4, 2, 1) if fan % c == 0)
    slabs = fit(10)
    h1, gp1, gp2, s, keep, cnt = message_forward(e, nbr, mask, tag, lhs, self_t, mid_t, slabs)
    node, lhs3, self3, n1, r1, n2, r2, acted, slope = node_forward(
        n, s, cnt, x, message_out, gain_node, offset_node, expand_weight, contract_weight, gain_ffn, offset_ffn,
        sel, uin
    )
    edge_new, part, guout, gumid, gin3, dself3, ggain, goff = edge_pass(
        e, cot, nbr, lhs3, self3, umid_t, uout_t, update_mid, update_out, uedge, gain_t, offset_t, fit(20, 10)
    )
    hidden = expand_weight.shape[1]
    early_depths, late_depths = chunk_plan(n // 2, early_rows(feat, hidden, edge_w)["end"], feat + edge_w + 16, 2 * feat)
    dfirst, d2, sums, *sources = node_backward(
        n, gin3, dself3, sel, node, node_cotan[0], uin, n1, r1, n2, r2, acted, slope, gain_node, offset_node, gain_ffn,
        expand_weight, contract_weight, s, cnt, message_out, ggain, goff, gumid, guout, early_depths
    )
    egrad, ngrad, *sums = message_backward(
        n, e, h1, gp1, gp2, part, keep, nbr, d2, message_mid, message_in, x, far_x, dfirst, sums, sel, sources, late_depths, table_len, slabs
    )
    gwin, gmid, gmout, gexp, gcon, guin, egrad, ngrad, node, gumid, guout, gnode, onode, gffn, offn, gedge, oedge = unpack_all(
        sums, egrad, ngrad, node, len(sources), feat, hidden, edge_w, table_len <= ROOMY
    )
    native = lambda a: jnp.transpose(a, (2, 0, 1))[None]
    return (node[None], native(edge_new), ngrad[None], native(egrad), gwin, gmid, gmout, gnode, onode, gexp, gcon, gffn, offn,
            jnp.transpose(guin), gumid, guout, gedge, oedge)


def solution(mesh):
    grouped, placed, copied = P("tm", "res", None), P("res", None), P()
    wide = P("tm", "res", None, None)
    arguments = (grouped, wide, grouped, wide, placed, placed, P("res", None, None), P("res"), P("res")) + (copied,) * 14
    return jax.shard_map(
        functools.partial(local, mesh.shape["res"]),
        mesh=mesh,
        in_specs=arguments,
        out_specs=(grouped, wide, grouped, wide) + (copied,) * 14,
        check_vma=False,
    )
```
